128 devices in a mesh: batch: 8 (over y, core), replica: 4 (over x), proto: 4 (over z).
Axes of the slice: x: 4, y: 4, z: 4, core: 2. Of those that a mesh axis runs over, the one named last changes fastest.
Arguments:
- view_one: bfloat16 [16384, 512], P(('batch', 'replica')), may hold values from -4 to 4
- view_two: bfloat16 [16384, 512], P(('batch', 'replica')), may hold values from -4 to 4
- prototypes: bfloat16 [16384, 512], P('proto'), may hold values from -8 to 8
- pairing: int32 [32, 512], P(('batch', 'replica')), may hold values from 0 to 511, as said below
Outputs:
- grad_one: float32 [16384, 512], P(('batch', 'replica'))
- grad_two: float32 [16384, 512], P(('batch', 'replica'))
- grad_prototypes: float32 [16384, 512], P('proto')
The draws below stay inside these ranges and needn't reach their ends.
Inputs may be any that keep to these rules, and one draw needn't show every extreme that they name: Each row of pairing names every one of 0 to 511 once.
All inputs are finite; a program needn't handle non-finite values.
Results may differ from the reference program's by a relative error of at most 0.0018.
The reference program's roundings to bfloat16 on the way count: a program that leaves them out, or rounds other values in their place, can miss the bound.
Values sent between devices are 32-bit elements; how exact they have to be, the bound alone decides.
A program may use at most 128 MiB of HBM per device.

```python
import math
import jax
import jax.numpy as jnp
from jax import lax

D = 512
PROTOS = 16384
ROWS = 512
ITERS = 3
SEG = 16384


def unit_direction(values):
    return values / jnp.sqrt(jnp.sum(values * values, -1, keepdims=True))


def shared_layout(key):
    base_key = jax.random.fold_in(key, 4099)
    draw_keys = jax.random.split(base_key, 5)
    speakers = max(PROTOS // 8, 4)
    centres = unit_direction(jax.random.normal(draw_keys[0], (speakers, D), jnp.float32))
    reach_top = jax.random.randint(draw_keys[1], (SEG,), 1, speakers + 1, dtype=jnp.int32)
    voices = jax.random.randint(draw_keys[2], (SEG,), 0, reach_top, dtype=jnp.int32)
    slot_ids = jax.random.permutation(draw_keys[3], PROTOS)[:speakers].astype(jnp.int32)
    blocks = SEG // ROWS
    block_keys = jax.random.split(draw_keys[4], blocks)
    pairing = jax.vmap(lambda k: jax.random.permutation(k, ROWS))(block_keys).astype(jnp.int32)
    return (centres, voices, slot_ids, pairing)


def embed_rows(centres, voices, noise, along, lengths):
    direction = along * centres[voices] + math.sqrt(1.0 - along * along) * unit_direction(noise)
    return (unit_direction(direction) * lengths).astype(jnp.bfloat16)


def draw_pairing(key, part):
    return shared_layout(key)[3]


def draw_view_one(key, part):
    centres, voices, slot_ids, pairing = shared_layout(key)
    noise_key, length_key = jax.random.split(jax.random.fold_in(key, 11))
    noise = jax.random.normal(noise_key, (SEG, D), jnp.float32)
    lengths = jnp.exp(jax.random.uniform(length_key, (SEG, 1), jnp.float32, math.log(0.5), math.log(2.0)))
    along = 0.75
    return embed_rows(centres, voices, noise, along, lengths)


def draw_view_two(key, part):
    centres, voices, slot_ids, pairing = shared_layout(key)
    blocks = SEG // ROWS
    flat = (jnp.arange(blocks, dtype=jnp.int32)[:, None] * ROWS + pairing).reshape(-1).astype(jnp.int32)
    voices_two = jnp.zeros((SEG,), jnp.int32).at[flat].set(voices)
    noise_key, length_key = jax.random.split(jax.random.fold_in(key, 12))
    noise = jax.random.normal(noise_key, (SEG, D), jnp.float32)
    lengths = jnp.exp(jax.random.uniform(length_key, (SEG, 1), jnp.float32, math.log(0.5), math.log(2.0)))
    along = 0.75
    return embed_rows(centres, voices_two, noise, along, lengths)


def draw_prototypes(key, part):
    centres, voices, slot_ids, pairing = shared_layout(key)
    noise_key, length_key = jax.random.split(jax.random.fold_in(key, 31))
    noise = jax.random.normal(noise_key, (PROTOS, D), jnp.float32)
    lengths = jnp.exp(jax.random.uniform(length_key, (PROTOS, 1), jnp.float32, math.log(1.0), math.log(4.0)))
    along = 0.9
    free_dirs = unit_direction(noise)
    placed = unit_direction(along * centres + math.sqrt(1.0 - along * along) * free_dirs[slot_ids])
    direction = free_dirs.at[slot_ids].set(placed)
    return (direction * lengths).astype(jnp.bfloat16)


def setup_inputs(seed: int = 0) -> dict:
    key_of = jax.random.split(jax.random.key(seed), 5)
    return {
        "view_one": draw_view_one(jax.random.fold_in(key_of[4], 71), 0),
        "view_two": draw_view_two(jax.random.fold_in(key_of[4], 71), 0),
        "prototypes": draw_prototypes(jax.random.fold_in(key_of[4], 71), 0),
        "pairing": draw_pairing(jax.random.fold_in(key_of[4], 71), 0),
    }


sink_eps = 0.05
softness_divisor = 0.1

def unit_rows(x):
    xf = x.astype(jnp.float32)
    inv = lax.rsqrt(lax.optimization_barrier(jnp.sum(xf * xf, -1, keepdims=True)) + 1e-06)
    return (xf * inv, inv)

def unit_back(grad, unit, inv):
    return inv * (grad - unit * lax.optimization_barrier(jnp.sum(unit * grad, -1, keepdims=True)))

def balance(similarity_logits):
    codes = jnp.exp(similarity_logits / sink_eps)
    for step in range(ITERS):
        codes = codes / lax.optimization_barrier(jnp.sum(codes, 0, keepdims=True))
        codes = codes / lax.optimization_barrier(jnp.sum(codes, 1, keepdims=True))
    return codes

def predict(similarity_logits):
    exponent_terms = jnp.exp(similarity_logits / softness_divisor)
    return exponent_terms / lax.optimization_barrier(jnp.sum(exponent_terms, 1, keepdims=True))

def reference(view_one, view_two, prototypes, pairing):
    unit_one, inv_one = unit_rows(view_one)
    unit_two, inv_two = unit_rows(view_two)
    unit_proto, inv_proto = unit_rows(prototypes)
    low_one = unit_one.astype(jnp.bfloat16)
    low_two = unit_two.astype(jnp.bfloat16)
    low_proto = unit_proto.astype(jnp.bfloat16)
    dims = (((1,), (1,)), ((), ()))
    logits_first_view = lax.dot_general(low_one, low_proto, dims, preferred_element_type=jnp.float32)
    logits_second_view = lax.dot_general(low_two, low_proto, dims, preferred_element_type=jnp.float32)
    codes_one = balance(logits_first_view)
    codes_two = balance(logits_second_view)
    blocks = pairing.shape[0]
    flat = (jnp.arange(blocks, dtype=jnp.int32)[:, None] * ROWS + pairing).reshape(-1).astype(jnp.int32)
    inverse = jnp.zeros((SEG,), jnp.int32).at[flat].set(jnp.arange(SEG, dtype=jnp.int32))
    target_one = codes_two[flat]
    target_two = codes_one[inverse]
    gradient_scale_factor = 0.5 / softness_divisor
    dscore_one = (gradient_scale_factor * (predict(logits_first_view) - target_one)).astype(jnp.bfloat16)
    dscore_two = (gradient_scale_factor * (predict(logits_second_view) - target_two)).astype(jnp.bfloat16)
    dunit_one = jnp.dot(dscore_one, low_proto, preferred_element_type=jnp.float32)
    dunit_two = jnp.dot(dscore_two, low_proto, preferred_element_type=jnp.float32)
    tdims = (((0,), (0,)), ((), ()))
    dunit_proto = lax.dot_general(dscore_one, low_one, tdims, preferred_element_type=jnp.float32)
    dunit_proto = dunit_proto + lax.dot_general(dscore_two, low_two, tdims, preferred_element_type=jnp.float32)
    grad_one = unit_back(dunit_one, unit_one, inv_one)
    grad_two = unit_back(dunit_two, unit_two, inv_two)
    grad_prototypes = unit_back(dunit_proto, unit_proto, inv_proto)
    return (grad_one, grad_two, grad_prototypes)
```

```python
import functools

import jax
import jax.numpy as jnp
from jax import lax
from jax.experimental import pallas as pl
from jax.experimental.pallas import tpu as pltpu
from jax.sharding import PartitionSpec as P

ITERS = 3
EPS = 1e-06
F32 = jnp.float32
BF16 = jnp.bfloat16
MESH = pl.DeviceIdType.MESH
NN = (((1,), (0,)), ((), ()))
NT = (((1,), (1,)), ((), ()))
TN = (((0,), (0,)), ((), ()))
LOG2E = 1.4426950408889634


def dot(a, b, dims):
    return lax.dot_general(a, b, dims, preferred_element_type=F32)


def here():
    batch = lax.axis_index("batch")
    return lax.div(batch, 2), lax.rem(batch, 2), lax.axis_index("replica"), lax.axis_index("proto")


def greet(peers):
    barrier = pltpu.get_barrier_semaphore()
    for peer in peers:
        pl.semaphore_signal(barrier, inc=1, device_id=peer, device_id_type=MESH)
    pl.semaphore_wait(barrier, len(peers))


def send(src, dst, send_sem, recv_sem, peer):
    copy = pltpu.make_async_remote_copy(
        src_ref=src, dst_ref=dst, send_sem=send_sem, recv_sem=recv_sem,
        device_id=peer, device_id_type=MESH,
    )
    copy.start()
    return copy


def balance_kernel(
    nx, ny, nz,
    one_ref, two_ref, proto_ref, pair_ref,
    dproto_ref, dunit_ref,
    expo, dscore, low_seg, low_seg_t, low_two, low_proto, onehot, row_scale, prob_scale,
    cols, cols_in, cols_y, weight, rows, rows_in, tile_u,
    send_sem, recv_sem,
):
    y, core, x, z = here()
    line = 2 * nx
    spot = core * nx + x

    def line_peer(step):
        other = lax.rem(spot + step, line)
        return other, (y * 2 + lax.div(other, nx), lax.rem(other, nx), z)

    def y_peer(step):
        return (lax.rem(y + step, ny) * 2 + core, x, z)

    def z_peer(step):
        return (y * 2 + core, x, lax.rem(z + step, nz))

    greet(
        [line_peer(s)[1] for s in range(1, line)]
        + [y_peer(s) for s in range(1, ny)]
        + [z_peer(s) for s in range(1, nz)]
    )

    segs = one_ref.shape[0]
    protos, width = low_proto.shape
    both = 2 * segs

    def unit(block):
        xf = block.astype(F32)
        inv = lax.rsqrt(jnp.sum(xf * xf, -1, keepdims=True) + EPS)
        return (xf * inv).astype(BF16)

    def norm_views(i, carry):
        at = pl.ds(pl.multiple_of(i * 128, 128), 128)
        low_seg[at, :] = unit(one_ref[at, :])
        low_two[at, :] = unit(two_ref[at, :])
        return carry

    lax.fori_loop(0, segs // 128, norm_views, 0)
    pair = jnp.broadcast_to(pair_ref[...], (segs, segs))
    number = lax.broadcasted_iota(jnp.int32, (segs, segs), 0)
    onehot[...] = jnp.where(pair == number, 1.0, 0.0).astype(BF16)
    low_seg[segs:both, :] = dot(onehot[...], low_two[...], TN).astype(BF16)
    for i in range(both // 128):
        block = low_seg[i * 128:(i + 1) * 128, :].astype(F32)
        low_seg_t[:, i * 128:(i + 1) * 128] = jnp.transpose(block).astype(BF16)

    def norm_protos(i, carry):
        at = pl.ds(pl.multiple_of(i * 128, 128), 128)
        low_proto[at, :] = unit(proto_ref[at, :])
        return carry

    lax.fori_loop(0, protos // 128, norm_protos, 0)

    wide = protos // 4

    def scores(j, carry):
        for q in range(wide // 256):
            at = pl.ds(pl.multiple_of(j * wide + q * 256, 256), 256)
            s = dot(low_seg[...], low_proto[at, :], NT)
            e = jnp.exp2(s * (10.0 * LOG2E))
            expo[:, at] = e
            k = e * e
            for view in range(2):
                total = jnp.sum(k[view * segs:(view + 1) * segs], axis=0, keepdims=True)
                for h in range(2):
                    cols[0, view * 4 + j, q * 2 + h:q * 2 + h + 1, :] = total[:, h * 128:(h + 1) * 128]
        return carry

    lax.fori_loop(0, 4, scores, 0)

    def col_sums(it):
        def block(k, carry):
            first = pl.multiple_of(lax.div(k, 4) * segs, segs)
            left = lax.rem(k, 4) * wide

            def some(r, acc):
                acc = list(acc)
                for t in range(4):
                    at = pl.ds(pl.multiple_of(first + r * 32 + t * 8, 8), 8)
                    u = row_scale[at, :]
                    for l in range(wide // 128):
                        e = expo[at, pl.ds(pl.multiple_of(left + l * 128, 128), 128)]
                        acc[l] = acc[l] + (e * e) * u
                return tuple(acc)

            zero = jnp.zeros((8, 128), F32)
            acc = lax.fori_loop(0, segs // 32, some, (zero,) * (wide // 128))
            for l in range(wide // 128):
                cols[it, k, l:l + 1, :] = jnp.sum(acc[l], axis=0, keepdims=True)
            return carry

        lax.fori_loop(0, 8, block, 0)

    def all_cols(it):
        copies = []
        for s in range(1, line):
            other, peer = line_peer(s)
            copies.append(send(cols.at[it, other], cols_in.at[it, spot],
                               send_sem.at[it, s - 1], recv_sem.at[it, s - 1], peer))
        cols_in[it, spot] = cols[it, spot]
        for copy in copies:
            copy.wait()
        total = cols_in[it, 0]
        for k in range(1, line):
            total = total + cols_in[it, k]
        cols_y[it, y] = total
        copies = []
        for s in range(1, ny):
            copies.append(send(cols_y.at[it, y], cols_y.at[it, y],
                               send_sem.at[it, 7 + s - 1], recv_sem.at[it, 7 + s - 1], y_peer(s)))
        for copy in copies:
            copy.wait()
        total = cols_y[it, 0]
        for k in range(1, ny):
            total = total + cols_y[it, k]
        weight[it, spot] = 1.0 / total
        copies = []
        for s in range(1, line):
            copies.append(send(weight.at[it, spot], weight.at[it, spot],
                               send_sem.at[it, 10 + s - 1], recv_sem.at[it, 10 + s - 1], line_peer(s)[1]))
        for copy in copies:
            copy.wait()

    def row_sums(it, with_total):
        def block(b, carry):
            at = pl.ds(pl.multiple_of(b * 128, 128), 128)
            view = lax.div(b, 4)
            acc = jnp.zeros((128, 128), F32)
            tot = jnp.zeros((128, 128), F32)
            for l in range(protos // 128):
                e = expo[at, l * 128:(l + 1) * 128]
                v = weight[it, view * 4 + l // 8, l % 8:l % 8 + 1, :]
                acc = acc + (e * e) * v
                if with_total:
                    tot = tot + e
            rows[it, pl.ds(b, 1), :] = jnp.sum(jnp.transpose(acc), axis=0, keepdims=True)
            if with_total:
                rows[it, pl.ds(8 + b, 1), :] = jnp.sum(jnp.transpose(tot), axis=0, keepdims=True)
            return carry

        lax.fori_loop(0, 8, block, 0)

    def spread(out, row):
        def block(b, carry):
            at = pl.ds(pl.multiple_of(b * 128, 128), 128)
            out[at, :] = jnp.transpose(jnp.broadcast_to(tile_u[pl.ds(row + b, 1), :], (128, 128)))
            return carry

        lax.fori_loop(0, 8, block, 0)

    def all_rows(it, with_total, scale):
        size = 16 if with_total else 8
        rows_in[it, z] = rows[it]
        copies = []
        for s in range(1, nz):
            copies.append(send(rows.at[it, 0:size], rows_in.at[it, z, 0:size],
                               send_sem.at[it, 17 + s - 1], recv_sem.at[it, 17 + s - 1], z_peer(s)))
        for copy in copies:
            copy.wait()
        total = rows_in[it, 0, 0:size]
        for k in range(1, nz):
            total = total + rows_in[it, k, 0:size]
        tile_u[0:8, :] = scale / total[0:8]
        spread(row_scale, 0)
        if with_total:
            tile_u[8:16, :] = 5.0 / total[8:16]
            spread(prob_scale, 8)

    for it in range(ITERS):
        if it:
            col_sums(it)
        all_cols(it)
        row_sums(it, it == 0)
        all_rows(it, it == 0, 5.0 if it == ITERS - 1 else 1.0)

    last = ITERS - 1

    def grads(j, carry):
        for h in range(2):
            at = pl.ds(pl.multiple_of(j * 256 + h * 128, 128), 128)
            tile = lax.div(j, 4)
            row = lax.rem(j, 4) * 2 + h
            v_one = weight[last, tile, pl.ds(row, 1), :]
            v_two = weight[last, 4 + tile, pl.ds(row, 1), :]
            for b in range(segs // 64):
                first = slice(b * 64, (b + 1) * 64)
                second = slice(segs + b * 64, segs + (b + 1) * 64)
                e_one = expo[first, at]
                e_two = expo[second, at]
                t_one = (e_two * e_two) * row_scale[second, :] * v_two
                t_two = (e_one * e_one) * row_scale[first, :] * v_one
                dscore[first, at] = (e_one * prob_scale[first, :] - t_one).astype(BF16)
                dscore[second, at] = (e_two * prob_scale[second, :] - t_two).astype(BF16)
        at = pl.ds(pl.multiple_of(j * 256, 256), 256)
        part = dot(low_seg_t[...], dscore[:, at], NN)
        dproto_ref[2 * j] = part[:, 0:128]
        dproto_ref[2 * j + 1] = part[:, 128:256]
        return carry

    lax.fori_loop(0, protos // 256, grads, 0)

    def views(i, carry):
        at = pl.ds(pl.multiple_of(i * 256, 256), 256)
        dunit_ref[at, :] = dot(dscore[at, :], low_proto[...], NN)
        return carry

    lax.fori_loop(0, both // 256, views, 0)
    d = dunit_ref[segs:both, :]
    high = d.astype(BF16)
    rest = d - high.astype(F32)
    mid = rest.astype(BF16)
    low = (rest - mid.astype(F32)).astype(BF16)
    tail = dot(onehot[...], mid, NN) + dot(onehot[...], low, NN)
    dunit_ref[segs:both, :] = dot(onehot[...], high, NN) + tail


def balance(mesh, one, two, protos, pair):
    nx, ny, nz = mesh.shape["replica"], mesh.shape["batch"] // 2, mesh.shape["proto"]
    segs, width = one.shape
    count = protos.shape[0]
    both = 2 * segs
    vmem = pl.BlockSpec(memory_space=pltpu.VMEM)
    return pl.pallas_call(
        functools.partial(balance_kernel, nx, ny, nz),
        out_shape=(
            jax.ShapeDtypeStruct((count // 128, width, 128), F32),
            jax.ShapeDtypeStruct((both, width), F32),
        ),
        in_specs=[vmem] * 4,
        out_specs=(vmem, vmem),
        scratch_shapes=[
            pltpu.VMEM((both, count), F32),
            pltpu.VMEM((both, count), BF16),
            pltpu.VMEM((both, width), BF16),
            pltpu.VMEM((width, both), BF16),
            pltpu.VMEM((segs, width), BF16),
            pltpu.VMEM((count, width), BF16),
            pltpu.VMEM((segs, segs), BF16),
            pltpu.VMEM((both, 128), F32),
            pltpu.VMEM((both, 128), F32),
            pltpu.VMEM((ITERS, 8, 8, 128), F32),
            pltpu.VMEM((ITERS, 8, 8, 128), F32),
            pltpu.VMEM((ITERS, ny, 8, 128), F32),
            pltpu.VMEM((ITERS, 8, 8, 128), F32),
            pltpu.VMEM((ITERS, 16, 128), F32),
            pltpu.VMEM((ITERS, nz, 16, 128), F32),
            pltpu.VMEM((16, 128), F32),
            pltpu.SemaphoreType.DMA((ITERS, 20)),
            pltpu.SemaphoreType.DMA((ITERS, 20)),
        ],
        compiler_params=pltpu.CompilerParams(
            collective_id=0, has_side_effects=True, vmem_limit_bytes=60 << 20
        ),
        name="balance",
    )(one, two, protos, pair)


def unit_rows(x):
    xf = x.astype(F32)
    inv = lax.rsqrt(jnp.sum(xf * xf, -1, keepdims=True) + EPS)
    return xf * inv, inv


def unit_back(grad, x):
    unit, inv = unit_rows(x)
    return inv * (grad - unit * jnp.sum(unit * grad, -1, keepdims=True))


def per_device(mesh, view_one, view_two, prototypes, pairing):
    dproto, dunit = balance(mesh, view_one, view_two, prototypes, pairing)
    dunit = lax.psum(dunit, "proto")
    dproto = lax.psum(dproto, ("batch", "replica"))
    dproto = jnp.swapaxes(dproto, 1, 2).reshape(prototypes.shape)
    segs = view_one.shape[0]
    return (
        unit_back(dunit[:segs], view_one),
        unit_back(dunit[segs:], view_two),
        unit_back(dproto, prototypes),
    )


def solution(mesh):
    rows = P(("batch", "replica"), None)
    protos = P("proto", None)
    return jax.shard_map(
        functools.partial(per_device, mesh),
        mesh=mesh,
        in_specs=(rows, rows, protos, rows),
        out_specs=(rows, rows, protos),
        check_vma=False,
    )
```

```python
import functools

import jax
import jax.numpy as jnp
from jax import lax
from jax.experimental import pallas as pl
from jax.experimental.pallas import tpu as pltpu
from jax.sharding import PartitionSpec as P

ITERS = 3
EPS = 1e-06
F32 = jnp.float32
BF16 = jnp.bfloat16
MESH = pl.DeviceIdType.MESH
NN = (((1,), (0,)), ((), ()))
NT = (((1,), (1,)), ((), ()))
TN = (((0,), (0,)), ((), ()))
LOG2E = 1.4426950408889634


def dot(a, b, dims):
    return lax.dot_general(a, b, dims, preferred_element_type=F32)


def here():
    batch = lax.axis_index("batch")
    return lax.div(batch, 2), lax.rem(batch, 2), lax.axis_index("replica"), lax.axis_index("proto")


class Links:
    def __init__(self, send_sem, recv_sem):
        self.send_sem, self.recv_sem, self.used, self.sent = send_sem, recv_sem, 0, []

    def send(self, src, dst, peer):
        copy = pltpu.make_async_remote_copy(
            src_ref=src, dst_ref=dst,
            send_sem=self.send_sem.at[self.used], recv_sem=self.recv_sem.at[self.used],
            device_id=peer, device_id_type=MESH,
        )
        copy.start()
        self.used += 1
        self.sent.append(copy)
        return copy

    def drain(self):
        for copy in self.sent:
            copy.wait_send()
        self.sent = []


def back(d, raw):
    xf = raw.astype(F32)
    inv = lax.rsqrt(jnp.sum(xf * xf, -1, keepdims=True) + EPS)
    u = xf * inv
    return inv * (d - u * jnp.sum(u * d, -1, keepdims=True))


def balance_kernel(
    nx, ny, nz,
    one_hbm, two_hbm, proto_hbm, pair_ref,
    gview_hbm, gproto_hbm,
    raw, expo, dscore, low_seg, low_seg_t, low_two, low_proto, onehot, row_scale, prob_scale,
    cols, cols_in, cols_y, weight, rows, rows_in, tile_u,
    dproto, from_core, dunit, own_proto, gproto, gview,
    a_relay, a_plain, a_joint, b_relay, b_plain, b_joint, z_relay, z_plain, z_joint,
    send_sem, recv_sem, local_sem,
):
    y, core, x, z = here()
    line = 2 * nx
    spot = core * nx + x
    links = Links(send_sem, recv_sem)
    at_a = core * y + (1 - core) * x
    at_b = core * x + (1 - core) * y
    mine = core * 16 + at_a * 4 + at_b

    def line_peer(step):
        other = lax.rem(spot + step, line)
        return other, (y * 2 + lax.div(other, nx), lax.rem(other, nx), z)

    def y_peer(step):
        return (lax.rem(y + step, ny) * 2 + core, x, z)

    def z_peer(step):
        return (y * 2 + core, x, lax.rem(z + step, nz))

    def a_peer(step):
        return (lax.rem(y + core * step, ny) * 2 + core, lax.rem(x + (1 - core) * step, nx), z)

    def b_peer(step):
        return (lax.rem(y + (1 - core) * step, ny) * 2 + core, lax.rem(x + core * step, nx), z)

    sibling = (y * 2 + 1 - core, x, z)

    segs = one_hbm.shape[0]
    protos, width = low_proto.shape
    both = 2 * segs
    fetch = [
        pltpu.make_async_copy(one_hbm, raw.at[0:segs], local_sem.at[0]),
        pltpu.make_async_copy(two_hbm, raw.at[segs:both], local_sem.at[1]),
        pltpu.make_async_copy(proto_hbm, low_proto, local_sem.at[2]),
        pltpu.make_async_copy(proto_hbm.at[pl.ds(mine * 128, 128)], own_proto, local_sem.at[3]),
    ]
    for copy in fetch:
        copy.start()
    peers = (
        [line_peer(s)[1] for s in range(1, line)]
        + [y_peer(s) for s in range(1, ny)]
        + [z_peer(s) for s in range(1, nz)]
    )
    barrier = pltpu.get_barrier_semaphore()
    for peer in peers:
        pl.semaphore_signal(barrier, inc=1, device_id=peer, device_id_type=MESH)

    def unit(block):
        xf = block.astype(F32)
        inv = lax.rsqrt(jnp.sum(xf * xf, -1, keepdims=True) + EPS)
        return (xf * inv).astype(BF16)

    def norm_views(i, carry):
        at = pl.ds(pl.multiple_of(i * 128, 128), 128)
        low_seg[at, :] = unit(raw[at, :])
        low_two[at, :] = unit(raw[pl.ds(pl.multiple_of(segs + i * 128, 128), 128), :])
        return carry

    fetch[0].wait()
    fetch[1].wait()
    lax.fori_loop(0, segs // 128, norm_views, 0)
    pair = jnp.broadcast_to(pair_ref[...], (segs, segs))
    number = lax.broadcasted_iota(jnp.int32, (segs, segs), 0)
    onehot[...] = jnp.where(pair == number, 1.0, 0.0).astype(BF16)
    low_seg[segs:both, :] = dot(onehot[...], low_two[...], TN).astype(BF16)
    for i in range(both // 128):
        block = low_seg[i * 128:(i + 1) * 128, :].astype(F32)
        low_seg_t[:, i * 128:(i + 1) * 128] = jnp.transpose(block).astype(BF16)

    def norm_protos(i, carry):
        at = pl.ds(pl.multiple_of(i * 128, 128), 128)
        low_proto[at, :] = unit(low_proto[at, :])
        return carry

    fetch[2].wait()
    lax.fori_loop(0, protos // 128, norm_protos, 0)

    wide = protos // 4

    def scores(j, carry):
        for q in range(wide // 256):
            at = pl.ds(pl.multiple_of(j * wide + q * 256, 256), 256)
            s = dot(low_seg[...], low_proto[at, :], NT)
            e = jnp.exp2(s * (10.0 * LOG2E))
            expo[:, at] = e
            k = e * e
            for view in range(2):
                total = jnp.sum(k[view * segs:(view + 1) * segs], axis=0, keepdims=True)
                for h in range(2):
                    cols[0, view * 4 + j, q * 2 + h:q * 2 + h + 1, :] = total[:, h * 128:(h + 1) * 128]
        return carry

    lax.fori_loop(0, 4, scores, 0)

    def col_sums(it):
        def block(k, carry):
            first = pl.multiple_of(lax.div(k, 4) * segs, segs)
            left = lax.rem(k, 4) * wide

            def some(r, acc):
                acc = list(acc)
                for t in range(4):
                    at = pl.ds(pl.multiple_of(first + r * 32 + t * 8, 8), 8)
                    u = row_scale[at, :]
                    for l in range(wide // 128):
                        e = expo[at, pl.ds(pl.multiple_of(left + l * 128, 128), 128)]
                        acc[l] = acc[l] + (e * e) * u
                return tuple(acc)

            zero = jnp.zeros((8, 128), F32)
            acc = lax.fori_loop(0, segs // 32, some, (zero,) * (wide // 128))
            for l in range(wide // 128):
                cols[it, k, l:l + 1, :] = jnp.sum(acc[l], axis=0, keepdims=True)
            return carry

        lax.fori_loop(0, 8, block, 0)

    def all_cols(it):
        copies = []
        for s in range(1, line):
            other, peer = line_peer(s)
            copies.append(links.send(cols.at[it, other], cols_in.at[it, spot], peer))
        cols_in[it, spot] = cols[it, spot]
        for copy in copies:
            copy.wait_recv()
        total = cols_in[it, 0]
        for k in range(1, line):
            total = total + cols_in[it, k]
        cols_y[it, y] = total
        copies = []
        for s in range(1, ny):
            copies.append(links.send(cols_y.at[it, y], cols_y.at[it, y], y_peer(s)))
        for copy in copies:
            copy.wait_recv()
        total = cols_y[it, 0]
        for k in range(1, ny):
            total = total + cols_y[it, k]
        weight[it, spot] = 1.0 / total
        copies = []
        for s in range(1, line):
            copies.append(links.send(weight.at[it, spot], weight.at[it, spot], line_peer(s)[1]))
        for copy in copies:
            copy.wait_recv()

    def row_sums(it, with_total):
        def block(b, carry):
            at = pl.ds(pl.multiple_of(b * 128, 128), 128)
            view = lax.div(b, 4)
            acc = jnp.zeros((128, 128), F32)
            tot = jnp.zeros((128, 128), F32)
            for l in range(protos // 128):
                e = expo[at, l * 128:(l + 1) * 128]
                v = weight[it, view * 4 + l // 8, l % 8:l % 8 + 1, :]
                acc = acc + (e * e) * v
                if with_total:
                    tot = tot + e
            rows[it, pl.ds(b, 1), :] = jnp.sum(jnp.transpose(acc), axis=0, keepdims=True)
            if with_total:
                rows[it, pl.ds(8 + b, 1), :] = jnp.sum(jnp.transpose(tot), axis=0, keepdims=True)
            return carry

        lax.fori_loop(0, 8, block, 0)

    def spread(out, row):
        def block(b, carry):
            at = pl.ds(pl.multiple_of(b * 128, 128), 128)
            out[at, :] = jnp.transpose(jnp.broadcast_to(tile_u[pl.ds(row + b, 1), :], (128, 128)))
            return carry

        lax.fori_loop(0, 8, block, 0)

    def all_rows(it, with_total, scale):
        size = 16 if with_total else 8
        rows_in[it, z] = rows[it]
        copies = []
        for s in range(1, nz):
            copies.append(links.send(rows.at[it, 0:size], rows_in.at[it, z, 0:size], z_peer(s)))
        for copy in copies:
            copy.wait_recv()
        total = rows_in[it, 0, 0:size]
        for k in range(1, nz):
            total = total + rows_in[it, k, 0:size]
        tile_u[0:8, :] = scale / total[0:8]
        spread(row_scale, 0)
        if with_total:
            tile_u[8:16, :] = 5.0 / total[8:16]
            spread(prob_scale, 8)

    pl.semaphore_wait(barrier, len(peers))
    for it in range(ITERS):
        if it:
            col_sums(it)
        all_cols(it)
        row_sums(it, it == 0)
        all_rows(it, it == 0, 5.0 if it == ITERS - 1 else 1.0)

    last = ITERS - 1

    def group(half, a):
        first_chunk = half * 16 + a * 4

        def grads(j, carry):
            chunk = first_chunk + j * 2
            for h in range(2):
                at = pl.ds(pl.multiple_of((chunk + h) * 128, 128), 128)
                tile = lax.div(chunk, 8)
                row = lax.rem(chunk, 8) + h
                v_one = weight[last, tile, pl.ds(row, 1), :]
                v_two = weight[last, 4 + tile, pl.ds(row, 1), :]
                for b in range(segs // 64):
                    first = slice(b * 64, (b + 1) * 64)
                    second = slice(segs + b * 64, segs + (b + 1) * 64)
                    e_one = expo[first, at]
                    e_two = expo[second, at]
                    t_one = (e_two * e_two) * row_scale[second, :] * v_two
                    t_two = (e_one * e_one) * row_scale[first, :] * v_one
                    dscore[first, at] = (e_one * prob_scale[first, :] - t_one).astype(BF16)
                    dscore[second, at] = (e_two * prob_scale[second, :] - t_two).astype(BF16)
            at = pl.ds(pl.multiple_of(chunk * 128, 256), 256)
            part = dot(low_seg_t[...], dscore[:, at], NN)
            dproto[chunk] = part[:, 0:128]
            dproto[chunk + 1] = part[:, 128:256]
            return carry

        lax.fori_loop(0, 2, grads, 0)
        return first_chunk

    order = (2, 1, 3, 0)
    crossing = []
    for t in order:
        a = lax.rem(at_b + t, 4)
        first = group(1 - core, a)
        crossing.append(links.send(dproto.at[pl.ds(first, 4)], from_core.at[pl.ds(a * 4, 4)], sibling))
    relays, plains, joints = [None] * 2, [None] * 2, [None] * 2
    base = {}
    for t, arrival in zip(order, crossing):
        a = lax.rem(at_a + t, 4)
        first = group(core, a)
        base[t] = first
        arrival.wait_recv()
        for q in range(4):
            dproto[first + q] = dproto[first + q] + from_core[a * 4 + q]
        low, high = dproto.at[pl.ds(first, 2)], dproto.at[pl.ds(first + 2, 2)]
        if t == 2:
            relays = [links.send(low, a_relay.at[0], a_peer(1)), links.send(high, a_relay.at[1], a_peer(3))]
        if t == 1:
            plains[0] = links.send(high, a_plain.at[0], a_peer(1))
        if t == 3:
            plains[1] = links.send(low, a_plain.at[1], a_peer(3))

    def views(i):
        at = slice(i * 256, (i + 1) * 256)
        dunit[at, :] = dot(dscore[at, :], low_proto[...], NN)

    views(0)
    views(1)
    relays[0].wait_recv()
    for q in range(2):
        dproto[base[1] + q] = dproto[base[1] + q] + a_relay[0, q]
    joints[0] = links.send(dproto.at[pl.ds(base[1], 2)], a_joint.at[0], a_peer(1))
    relays[1].wait_recv()
    for q in range(2):
        dproto[base[3] + 2 + q] = dproto[base[3] + 2 + q] + a_relay[1, q]
    joints[1] = links.send(dproto.at[pl.ds(base[3] + 2, 2)], a_joint.at[1], a_peer(3))

    views(2)
    views(3)
    d = dunit[segs:both, :]
    top = d.astype(BF16)
    rest = d - top.astype(F32)
    middle = rest.astype(BF16)
    end = (rest - middle.astype(F32)).astype(BF16)
    rest = dot(onehot[...], middle, NN) + dot(onehot[...], end, NN)
    dunit[segs:both, :] = dot(onehot[...], top, NN) + rest

    def part(ref, k, size, lower):
        half = size // 2
        start = k * size + (0 if lower else half)
        return ref.at[pl.ds(pl.multiple_of(start, half), half)]

    seg_part = both // nz
    z_right, z_left, z_far = lax.rem(z + 1, 4), lax.rem(z + 3, 4), lax.rem(z + 2, 4)
    z_relays = [
        links.send(part(dunit, z_far, seg_part, True), z_relay.at[0], z_peer(1)),
        links.send(part(dunit, z_far, seg_part, False), z_relay.at[1], z_peer(3)),
    ]
    z_plains = [
        links.send(part(dunit, z_right, seg_part, False), z_plain.at[0], z_peer(1)),
        links.send(part(dunit, z_left, seg_part, True), z_plain.at[1], z_peer(3)),
    ]

    own = base[0]
    for copy in plains + joints:
        copy.wait_recv()
    for q in range(2):
        dproto[own + q] = dproto[own + q] + (a_joint[0, q] + a_plain[1, q])
        dproto[own + 2 + q] = dproto[own + 2 + q] + (a_plain[0, q] + a_joint[1, q])
    b_right, b_left, b_far = lax.rem(at_b + 1, 4), lax.rem(at_b + 3, 4), lax.rem(at_b + 2, 4)
    half = width // 2
    b_relays = [
        links.send(dproto.at[own + b_far, 0:half], b_relay.at[0], b_peer(1)),
        links.send(dproto.at[own + b_far, half:width], b_relay.at[1], b_peer(3)),
    ]
    b_plains = [
        links.send(dproto.at[own + b_right, half:width], b_plain.at[0], b_peer(1)),
        links.send(dproto.at[own + b_left, 0:half], b_plain.at[1], b_peer(3)),
    ]

    z_half = seg_part // 2
    z_joints = []
    for way, k, skip, peer in ((0, z_right, 0, z_peer(1)), (1, z_left, z_half, z_peer(3))):
        z_relays[way].wait_recv()
        at = pl.ds(pl.multiple_of(k * seg_part + skip, z_half), z_half)
        dunit[at, :] = dunit[at, :] + z_relay[way]
        z_joints.append(links.send(dunit.at[at], z_joint.at[way], peer))

    b_joints = []
    for way, k, skip, peer in ((0, b_right, 0, b_peer(1)), (1, b_left, half, b_peer(3))):
        b_relays[way].wait_recv()
        at = slice(skip, skip + half)
        dproto[own + k, at, :] = dproto[own + k, at, :] + b_relay[way]
        b_joints.append(links.send(dproto.at[own + k, at], b_joint.at[way], peer))
    for copy in b_plains + b_joints:
        copy.wait_recv()
    me = own + at_b
    dproto[me, 0:half, :] = dproto[me, 0:half, :] + (b_joint[0] + b_plain[1])
    dproto[me, half:width, :] = dproto[me, half:width, :] + (b_plain[0] + b_joint[1])
    fetch[3].wait()
    gproto[...] = back(jnp.transpose(dproto[me]), own_proto[...])

    def rows_of(chunk, part=None):
        if part is None:
            return gproto_hbm.at[pl.ds(pl.multiple_of(chunk * 128, 128), 128)]
        return gproto_hbm.at[pl.ds(pl.multiple_of(chunk * 128 + part * 64, 64), 64)]

    def chunk_of(a, b):
        return core * 16 + a * 4 + b

    across = []

    def to_sibling(place, src=None):
        across.append(links.send(place if src is None else src, place, sibling))

    b_whole = [links.send(gproto, rows_of(mine), b_peer(1)), links.send(gproto, rows_of(mine), b_peer(3))]
    a_whole = {0: [links.send(gproto, rows_of(mine), a_peer(1)), links.send(gproto, rows_of(mine), a_peer(3))]}
    to_sibling(rows_of(mine), gproto)
    keep = pltpu.make_async_copy(gproto, rows_of(mine), local_sem.at[4])
    keep.start()

    for copy in z_plains + z_joints:
        copy.wait_recv()
    at = pl.ds(pl.multiple_of(z * seg_part, z_half), z_half)
    dunit[at, :] = dunit[at, :] + (z_joint[0] + z_plain[1])
    at = pl.ds(pl.multiple_of(z * seg_part + z_half, z_half), z_half)
    dunit[at, :] = dunit[at, :] + (z_plain[0] + z_joint[1])
    at = pl.ds(pl.multiple_of(z * seg_part, seg_part), seg_part)
    gview[...] = back(dunit[at, :], raw[at, :])
    place = gview_hbm.at[at]
    z_whole = [links.send(gview, place, z_peer(1)), links.send(gview, place, z_peer(3))]
    keep_view = pltpu.make_async_copy(gview, place, local_sem.at[5])
    keep_view.start()

    b_halves, a_halves = [], {}
    a_right, a_left, a_far = lax.rem(at_a + 1, 4), lax.rem(at_a + 3, 4), lax.rem(at_a + 2, 4)

    def along_a(key, place):
        a_whole[key] = a_whole.get(key, []) + [links.send(place, place, a_peer(1)), links.send(place, place, a_peer(3))]
        to_sibling(place)

    b_whole[0].wait_recv()
    b_halves.append(links.send(rows_of(chunk_of(at_a, b_left), 0), rows_of(chunk_of(at_a, b_left), 0), b_peer(1)))
    along_a(3, rows_of(chunk_of(at_a, b_left)))
    b_whole[1].wait_recv()
    b_halves.append(links.send(rows_of(chunk_of(at_a, b_right), 1), rows_of(chunk_of(at_a, b_right), 1), b_peer(3)))
    along_a(1, rows_of(chunk_of(at_a, b_right)))

    def pass_on(key, b):
        left, right = chunk_of(a_left, b), chunk_of(a_right, b)
        a_whole[key][0].wait_recv()
        a_halves[key] = [links.send(rows_of(left, 0), rows_of(left, 0), a_peer(1))]
        to_sibling(rows_of(left))
        a_whole[key][1].wait_recv()
        a_halves[key].append(links.send(rows_of(right, 1), rows_of(right, 1), a_peer(3)))
        to_sibling(rows_of(right))

    pass_on(0, at_b)
    far = chunk_of(at_a, b_far)
    b_halves[0].wait_recv()
    b_halves[1].wait_recv()
    along_a(2, rows_of(far))

    z_left_place = gview_hbm.at[pl.ds(pl.multiple_of(z_left * seg_part, seg_part), z_half)]
    z_right_place = gview_hbm.at[pl.ds(pl.multiple_of(z_right * seg_part + z_half, z_half), z_half)]
    z_whole[0].wait_recv()
    z_halves = [links.send(z_left_place, z_left_place, z_peer(1))]
    z_whole[1].wait_recv()
    z_halves.append(links.send(z_right_place, z_right_place, z_peer(3)))

    pass_on(3, b_left)
    pass_on(1, b_right)

    def far_halves(key, b):
        chunk = chunk_of(a_far, b)
        for way in range(2):
            a_halves[key][way].wait_recv()
            to_sibling(rows_of(chunk, way))

    far_halves(0, at_b)
    pass_on(2, b_far)
    far_halves(3, b_left)
    far_halves(1, b_right)
    far_halves(2, b_far)
    for copy in z_halves + across:
        copy.wait_recv()
    keep.wait()
    keep_view.wait()
    links.drain()


def balance(mesh, one, two, protos, pair):
    nx, ny, nz = mesh.shape["replica"], mesh.shape["batch"] // 2, mesh.shape["proto"]
    segs, width = one.shape
    count = protos.shape[0]
    both = 2 * segs
    z_half = both // nz // 2
    copies = ITERS * (2 * (2 * nx - 1) + (ny - 1) + (nz - 1)) + 80
    hbm = pl.BlockSpec(memory_space=pl.ANY)
    return pl.pallas_call(
        functools.partial(balance_kernel, nx, ny, nz),
        out_shape=(
            jax.ShapeDtypeStruct((both, width), F32),
            jax.ShapeDtypeStruct((count, width), F32),
        ),
        in_specs=[hbm, hbm, hbm, pl.BlockSpec(memory_space=pltpu.VMEM)],
        out_specs=(hbm, hbm),
        scratch_shapes=[
            pltpu.VMEM((both, width), BF16),
            pltpu.VMEM((both, count), F32),
            pltpu.VMEM((both, count), BF16),
            pltpu.VMEM((both, width), BF16),
            pltpu.VMEM((width, both), BF16),
            pltpu.VMEM((segs, width), BF16),
            pltpu.VMEM((count, width), BF16),
            pltpu.VMEM((segs, segs), BF16),
            pltpu.VMEM((both, 128), F32),
            pltpu.VMEM((both, 128), F32),
            pltpu.VMEM((ITERS, 8, 8, 128), F32),
            pltpu.VMEM((ITERS, 8, 8, 128), F32),
            pltpu.VMEM((ITERS, ny, 8, 128), F32),
            pltpu.VMEM((ITERS, 8, 8, 128), F32),
            pltpu.VMEM((ITERS, 16, 128), F32),
            pltpu.VMEM((ITERS, nz, 16, 128), F32),
            pltpu.VMEM((16, 128), F32),
            pltpu.VMEM((count // 128, width, 128), F32),
            pltpu.VMEM((count // 256, width, 128), F32),
            pltpu.VMEM((both, width), F32),
            pltpu.VMEM((128, width), BF16),
            pltpu.VMEM((128, width), F32),
            pltpu.VMEM((both // nz, width), F32),
        ]
        + [pltpu.VMEM((2, 2, width, 128), F32)] * 3
        + [pltpu.VMEM((2, width // 2, 128), F32)] * 3
        + [pltpu.VMEM((2, z_half, width), F32)] * 3
        + [
            pltpu.SemaphoreType.DMA((copies,)),
            pltpu.SemaphoreType.DMA((copies,)),
            pltpu.SemaphoreType.DMA((6,)),
        ],
        compiler_params=pltpu.CompilerParams(
            collective_id=0, has_side_effects=True, vmem_limit_bytes=62 << 20
        ),
        name="balance",
    )(one, two, protos, pair)


def per_device(mesh, view_one, view_two, prototypes, pairing):
    gview, gproto = balance(mesh, view_one, view_two, prototypes, pairing)
    segs = view_one.shape[0]
    return gview[:segs], gview[segs:], gproto


def solution(mesh):
    rows = P(("batch", "replica"), None)
    protos = P("proto", None)
    return jax.shard_map(
        functools.partial(per_device, mesh),
        mesh=mesh,
        in_specs=(rows, rows, protos, rows),
        out_specs=(rows, rows, protos),
        check_vma=False,
    )
```

```python
import functools

import jax
import jax.numpy as jnp
from jax import lax
from jax.experimental import pallas as pl
from jax.experimental.pallas import tpu as pltpu
from jax.sharding import PartitionSpec as P

ITERS = 3
EPS = 1e-06
F32 = jnp.float32
BF16 = jnp.bfloat16
MESH = pl.DeviceIdType.MESH
NN = (((1,), (0,)), ((), ()))
NT = (((1,), (1,)), ((), ()))
TN = (((0,), (0,)), ((), ()))
LOG2E = 1.4426950408889634


def dot(a, b, dims):
    return lax.dot_general(a, b, dims, preferred_element_type=F32)


def here():
    batch = lax.axis_index("batch")
    return lax.div(batch, 2), lax.rem(batch, 2), lax.axis_index("replica"), lax.axis_index("proto")


class Links:
    def __init__(self, send_sem, recv_sem):
        self.send_sem, self.recv_sem, self.used, self.sent = send_sem, recv_sem, 0, []

    def send(self, src, dst, peer):
        copy = pltpu.make_async_remote_copy(
            src_ref=src, dst_ref=dst,
            send_sem=self.send_sem.at[self.used], recv_sem=self.recv_sem.at[self.used],
            device_id=peer, device_id_type=MESH,
        )
        copy.start()
        self.used += 1
        self.sent.append(copy)
        return copy

    def drain(self):
        for copy in self.sent:
            copy.wait_send()
        self.sent = []


def back(d, raw):
    xf = raw.astype(F32)
    inv = lax.rsqrt(jnp.sum(xf * xf, -1, keepdims=True) + EPS)
    u = xf * inv
    return inv * (d - u * jnp.sum(u * d, -1, keepdims=True))


def balance_kernel(
    nx, ny, nz,
    one_hbm, two_hbm, proto_hbm, pair_ref,
    gview_hbm, gproto_hbm,
    raw, expo, dscore, low_seg, low_seg_t, low_two, low_proto, onehot, row_scale, prob_scale,
    cols, cols_in, cols_y, weight, rows, rows_in, tile_u, row_part, tot_part,
    dproto, from_core, dunit, own_proto, gproto, gview,
    a_relay, a_plain, a_joint, b_relay, b_plain, b_joint, z_relay, z_plain, z_joint,
    send_sem, recv_sem, local_sem,
):
    y, core, x, z = here()
    line = 2 * nx
    spot = core * nx + x
    links = Links(send_sem, recv_sem)
    at_a = core * y + (1 - core) * x
    at_b = core * x + (1 - core) * y
    mine = core * 16 + at_a * 4 + at_b

    def line_peer(step):
        other = lax.rem(spot + step, line)
        return other, (y * 2 + lax.div(other, nx), lax.rem(other, nx), z)

    def y_peer(step):
        return (lax.rem(y + step, ny) * 2 + core, x, z)

    def z_peer(step):
        return (y * 2 + core, x, lax.rem(z + step, nz))

    def a_peer(step):
        return (lax.rem(y + core * step, ny) * 2 + core, lax.rem(x + (1 - core) * step, nx), z)

    def b_peer(step):
        return (lax.rem(y + (1 - core) * step, ny) * 2 + core, lax.rem(x + core * step, nx), z)

    sibling = (y * 2 + 1 - core, x, z)

    segs = one_hbm.shape[0]
    protos, width = low_proto.shape
    both = 2 * segs
    fetch = [
        pltpu.make_async_copy(one_hbm, raw.at[0:segs], local_sem.at[0]),
        pltpu.make_async_copy(two_hbm, raw.at[segs:both], local_sem.at[1]),
        pltpu.make_async_copy(proto_hbm, low_proto, local_sem.at[2]),
        pltpu.make_async_copy(proto_hbm.at[pl.ds(mine * 128, 128)], own_proto, local_sem.at[3]),
    ]
    for copy in fetch:
        copy.start()
    peers = (
        [line_peer(s)[1] for s in range(1, line)]
        + [y_peer(s) for s in range(1, ny)]
        + [z_peer(s) for s in range(1, nz)]
    )
    barrier = pltpu.get_barrier_semaphore()
    for peer in peers:
        pl.semaphore_signal(barrier, inc=1, device_id=peer, device_id_type=MESH)

    def unit(block):
        xf = block.astype(F32)
        inv = lax.rsqrt(jnp.sum(xf * xf, -1, keepdims=True) + EPS)
        return (xf * inv).astype(BF16)

    def norm_views(i, carry):
        at = pl.ds(pl.multiple_of(i * 128, 128), 128)
        low_seg[at, :] = unit(raw[at, :])
        low_two[at, :] = unit(raw[pl.ds(pl.multiple_of(segs + i * 128, 128), 128), :])
        return carry

    fetch[0].wait()
    fetch[1].wait()
    lax.fori_loop(0, segs // 128, norm_views, 0, unroll=2)
    pair = jnp.broadcast_to(pair_ref[...], (segs, segs))
    number = lax.broadcasted_iota(jnp.int32, (segs, segs), 0)
    onehot[...] = jnp.where(pair == number, 1.0, 0.0).astype(BF16)
    low_seg[segs:both, :] = dot(onehot[...], low_two[...], TN).astype(BF16)
    def norm_protos(i, carry):
        at = pl.ds(pl.multiple_of(i * 128, 128), 128)
        low_proto[at, :] = unit(low_proto[at, :])
        return carry

    fetch[2].wait()
    lax.fori_loop(0, protos // 128, norm_protos, 0, unroll=4)

    wide = protos // 4

    def scores(j, carry):
        for q in range(wide // 256):
            at = pl.ds(pl.multiple_of(j * wide + q * 256, 256), 256)
            s = dot(low_seg[...], low_proto[at, :], NT)
            e = jnp.exp2(s * (10.0 * LOG2E))
            expo[:, at] = e
            k = e * e
            for view in range(2):
                total = jnp.sum(k[view * segs:(view + 1) * segs], axis=0, keepdims=True)
                for h in range(2):
                    cols[0, view * 4 + j, q * 2 + h:q * 2 + h + 1, :] = total[:, h * 128:(h + 1) * 128]
        return carry

    lax.fori_loop(0, 4, scores, 0)

    def col_sums(it):
        def block(k, carry):
            first = pl.multiple_of(lax.div(k, 4) * segs, segs)
            left = lax.rem(k, 4) * wide

            def some(r, acc):
                acc = list(acc)
                for t in range(16):
                    at = pl.ds(pl.multiple_of(first + r * 128 + t * 8, 8), 8)
                    u = row_scale[at, :]
                    for l in range(wide // 128):
                        e = expo[at, pl.ds(pl.multiple_of(left + l * 128, 128), 128)]
                        n = (t % 2) * (wide // 128) + l
                        acc[n] = acc[n] + (e * e) * u
                return tuple(acc)

            zero = jnp.zeros((8, 128), F32)
            acc = lax.fori_loop(0, segs // 128, some, (zero,) * (wide // 64))
            acc = [acc[l] + acc[wide // 128 + l] for l in range(wide // 128)]
            for l in range(wide // 128):
                cols[it, k, l:l + 1, :] = jnp.sum(acc[l], axis=0, keepdims=True)
            return carry

        lax.fori_loop(0, 8, block, 0)

    def turn_segs():
        for i in range(both // 128):
            block = low_seg[i * 128:(i + 1) * 128, :].astype(F32)
            low_seg_t[:, i * 128:(i + 1) * 128] = jnp.transpose(block).astype(BF16)

    def all_cols(it):
        copies = []
        for s in range(1, line):
            other, peer = line_peer(s)
            copies.append(links.send(cols.at[it, other], cols_in.at[it, spot], peer))
        cols_in[it, spot] = cols[it, spot]
        if it == 0:
            turn_segs()
        for copy in copies:
            copy.wait_recv()
        total = cols_in[it, 0]
        for k in range(1, line):
            total = total + cols_in[it, k]
        cols_y[it, y] = total
        copies = []
        for s in range(1, ny):
            copies.append(links.send(cols_y.at[it, y], cols_y.at[it, y], y_peer(s)))
        for copy in copies:
            copy.wait_recv()
        total = cols_y[it, 0]
        for k in range(1, ny):
            total = total + cols_y[it, k]
        weight[it, spot] = 1.0 / total
        copies = []
        for s in range(1, line):
            copies.append(links.send(weight.at[it, spot], weight.at[it, spot], line_peer(s)[1]))
        for copy in copies:
            copy.wait_recv()

    def row_sums(it, with_total):
        def block(b, carry):
            at = pl.ds(pl.multiple_of(b * 64, 64), 64)
            view = lax.div(b, segs // 64)
            acc = jnp.zeros((64, 128), F32)
            tot = jnp.zeros((64, 128), F32)
            for l in range(protos // 128):
                e = expo[at, l * 128:(l + 1) * 128]
                v = weight[it, view * 4 + l // 8, l % 8:l % 8 + 1, :]
                acc = acc + (e * e) * v
                if with_total:
                    tot = tot + e
            row_part[at, :] = acc
            if with_total:
                tot_part[at, :] = tot
            return carry

        lax.fori_loop(0, both // 64, block, 0)
        for b in range(both // 128):
            at = slice(b * 128, (b + 1) * 128)
            rows[it, b:b + 1, :] = jnp.sum(jnp.transpose(row_part[at, :]), axis=0, keepdims=True)
            if with_total:
                rows[it, 8 + b:9 + b, :] = jnp.sum(jnp.transpose(tot_part[at, :]), axis=0, keepdims=True)

    def spread(out, row):
        for b in range(both // 128):
            wide_row = jnp.broadcast_to(tile_u[row + b:row + b + 1, :], (128, 128))
            out[b * 128:(b + 1) * 128, :] = jnp.transpose(wide_row)

    def all_rows(it, with_total, scale):
        size = 16 if with_total else 8
        rows_in[it, z] = rows[it]
        copies = []
        for s in range(1, nz):
            copies.append(links.send(rows.at[it, 0:size], rows_in.at[it, z, 0:size], z_peer(s)))
        for copy in copies:
            copy.wait_recv()
        total = rows_in[it, 0, 0:size]
        for k in range(1, nz):
            total = total + rows_in[it, k, 0:size]
        tile_u[0:8, :] = scale / total[0:8]
        spread(row_scale, 0)
        if with_total:
            tile_u[8:16, :] = 5.0 / total[8:16]
            spread(prob_scale, 8)

    pl.semaphore_wait(barrier, len(peers))
    for it in range(ITERS):
        if it:
            col_sums(it)
        all_cols(it)
        row_sums(it, it == 0)
        all_rows(it, it == 0, 5.0 if it == ITERS - 1 else 1.0)

    last = ITERS - 1

    half_b = 256

    def elements(ds, chunk, j):
        for h in range(2):
            at = pl.ds(pl.multiple_of((chunk + j * 2 + h) * 128, 128), 128)
            to = pl.ds(pl.multiple_of(j * half_b + h * 128, 128), 128)
            tile = lax.div(chunk, 8)
            row = lax.rem(chunk, 8) + j * 2 + h
            v_one = weight[last, tile, pl.ds(row, 1), :]
            v_two = weight[last, 4 + tile, pl.ds(row, 1), :]
            for b in range(segs // 64):
                first = slice(b * 64, (b + 1) * 64)
                second = slice(segs + b * 64, segs + (b + 1) * 64)
                e_one = expo[first, at]
                e_two = expo[second, at]
                t_one = (e_two * e_two) * row_scale[second, :] * v_two
                t_two = (e_one * e_one) * row_scale[first, :] * v_one
                ds[first, to] = (e_one * prob_scale[first, :] - t_one).astype(BF16)
                ds[second, to] = (e_two * prob_scale[second, :] - t_two).astype(BF16)

    def step(new, old):
        def both_parts(j, carry):
            if old is not None:
                at = pl.ds(pl.multiple_of(j * half_b, half_b), half_b)
                part = dot(low_seg_t[...], dscore[old][:, at], NN)
                dproto[old][2 * j] = part[:, 0:128]
                dproto[old][2 * j + 1] = part[:, 128:256]
            if new is not None:
                elements(dscore[new], chunks[new], j)
            return carry

        lax.fori_loop(0, 2, both_parts, 0)

    order = (2, 1, 3, 0)
    chunks, spots = [], []
    for t in order:
        for half, place in ((1 - core, at_b), (core, at_a)):
            spots.append(lax.rem(place + t, 4))
            chunks.append(half * 16 + spots[-1] * 4)
    relays, plains, joints = [None] * 2, [None] * 2, [None] * 2
    crossing = [None] * 8
    step(0, None)
    for g in range(8):
        step(g + 1 if g < 7 else None, g)
        if g % 2 == 0:
            crossing[g] = links.send(dproto[g], from_core.at[g // 2], sibling)
            continue
        crossing[g - 1].wait_recv()
        for q in range(4):
            dproto[g][q] = dproto[g][q] + from_core[g // 2, q]
        low, high = dproto[g].at[0:2], dproto[g].at[2:4]
        t = order[g // 2]
        if t == 2:
            relays = [links.send(low, a_relay.at[0], a_peer(1)), links.send(high, a_relay.at[1], a_peer(3))]
        if t == 1:
            plains[0] = links.send(high, a_plain.at[0], a_peer(1))
        if t == 3:
            plains[1] = links.send(low, a_plain.at[1], a_peer(3))
    d_right, d_left, d_own = dproto[3], dproto[5], dproto[7]

    def views(i):
        at = slice(i * 256, (i + 1) * 256)
        total = None
        for g in range(8):
            rows_g = low_proto[pl.ds(pl.multiple_of(chunks[g] * 128, 512), 512), :]
            term = dot(dscore[g][at, :], rows_g, NN)
            total = term if total is None else total + term
        dunit[at, :] = total

    views(0)
    views(1)
    relays[0].wait_recv()
    for q in range(2):
        d_right[q] = d_right[q] + a_relay[0, q]
    joints[0] = links.send(d_right.at[0:2], a_joint.at[0], a_peer(1))
    relays[1].wait_recv()
    for q in range(2):
        d_left[2 + q] = d_left[2 + q] + a_relay[1, q]
    joints[1] = links.send(d_left.at[2:4], a_joint.at[1], a_peer(3))

    views(2)
    views(3)
    d = dunit[segs:both, :]
    top = d.astype(BF16)
    rest = d - top.astype(F32)
    middle = rest.astype(BF16)
    end = (rest - middle.astype(F32)).astype(BF16)
    rest = dot(onehot[...], middle, NN) + dot(onehot[...], end, NN)
    dunit[segs:both, :] = dot(onehot[...], top, NN) + rest

    def part(ref, k, size, lower):
        half = size // 2
        start = k * size + (0 if lower else half)
        return ref.at[pl.ds(pl.multiple_of(start, half), half)]

    seg_part = both // nz
    z_right, z_left, z_far = lax.rem(z + 1, 4), lax.rem(z + 3, 4), lax.rem(z + 2, 4)
    z_relays = [
        links.send(part(dunit, z_far, seg_part, True), z_relay.at[0], z_peer(1)),
        links.send(part(dunit, z_far, seg_part, False), z_relay.at[1], z_peer(3)),
    ]
    z_plains = [
        links.send(part(dunit, z_right, seg_part, False), z_plain.at[0], z_peer(1)),
        links.send(part(dunit, z_left, seg_part, True), z_plain.at[1], z_peer(3)),
    ]

    for copy in plains + joints:
        copy.wait_recv()
    for q in range(2):
        d_own[q] = d_own[q] + (a_joint[0, q] + a_plain[1, q])
        d_own[2 + q] = d_own[2 + q] + (a_plain[0, q] + a_joint[1, q])
    b_right, b_left, b_far = lax.rem(at_b + 1, 4), lax.rem(at_b + 3, 4), lax.rem(at_b + 2, 4)
    half = width // 2
    b_relays = [
        links.send(d_own.at[b_far, 0:half], b_relay.at[0], b_peer(1)),
        links.send(d_own.at[b_far, half:width], b_relay.at[1], b_peer(3)),
    ]
    b_plains = [
        links.send(d_own.at[b_right, half:width], b_plain.at[0], b_peer(1)),
        links.send(d_own.at[b_left, 0:half], b_plain.at[1], b_peer(3)),
    ]

    z_half = seg_part // 2
    z_joints = []
    for way, k, skip, peer in ((0, z_right, 0, z_peer(1)), (1, z_left, z_half, z_peer(3))):
        z_relays[way].wait_recv()
        at = pl.ds(pl.multiple_of(k * seg_part + skip, z_half), z_half)
        dunit[at, :] = dunit[at, :] + z_relay[way]
        z_joints.append(links.send(dunit.at[at], z_joint.at[way], peer))

    b_joints = []
    for way, k, skip, peer in ((0, b_right, 0, b_peer(1)), (1, b_left, half, b_peer(3))):
        b_relays[way].wait_recv()
        at = slice(skip, skip + half)
        d_own[k, at, :] = d_own[k, at, :] + b_relay[way]
        b_joints.append(links.send(d_own.at[k, at], b_joint.at[way], peer))
    for copy in b_plains + b_joints:
        copy.wait_recv()
    me = at_b
    d_own[me, 0:half, :] = d_own[me, 0:half, :] + (b_joint[0] + b_plain[1])
    d_own[me, half:width, :] = d_own[me, half:width, :] + (b_plain[0] + b_joint[1])
    fetch[3].wait()
    gproto[...] = back(jnp.transpose(d_own[me]), own_proto[...])

    def rows_of(chunk, part=None):
        if part is None:
            return gproto_hbm.at[pl.ds(pl.multiple_of(chunk * 128, 128), 128)]
        return gproto_hbm.at[pl.ds(pl.multiple_of(chunk * 128 + part * 64, 64), 64)]

    def chunk_of(a, b):
        return core * 16 + a * 4 + b

    across = []

    def to_sibling(place, src=None):
        across.append(links.send(place if src is None else src, place, sibling))

    b_whole = [links.send(gproto, rows_of(mine), b_peer(1)), links.send(gproto, rows_of(mine), b_peer(3))]
    a_whole = {0: [links.send(gproto, rows_of(mine), a_peer(1)), links.send(gproto, rows_of(mine), a_peer(3))]}
    to_sibling(rows_of(mine), gproto)
    keep = pltpu.make_async_copy(gproto, rows_of(mine), local_sem.at[4])
    keep.start()

    for copy in z_plains + z_joints:
        copy.wait_recv()
    at = pl.ds(pl.multiple_of(z * seg_part, z_half), z_half)
    dunit[at, :] = dunit[at, :] + (z_joint[0] + z_plain[1])
    at = pl.ds(pl.multiple_of(z * seg_part + z_half, z_half), z_half)
    dunit[at, :] = dunit[at, :] + (z_plain[0] + z_joint[1])
    at = pl.ds(pl.multiple_of(z * seg_part, seg_part), seg_part)
    gview[...] = back(dunit[at, :], raw[at, :])
    place = gview_hbm.at[at]
    z_whole = [links.send(gview, place, z_peer(1)), links.send(gview, place, z_peer(3))]
    keep_view = pltpu.make_async_copy(gview, place, local_sem.at[5])
    keep_view.start()

    b_halves, a_halves = [], {}
    a_right, a_left, a_far = lax.rem(at_a + 1, 4), lax.rem(at_a + 3, 4), lax.rem(at_a + 2, 4)

    def along_a(key, place):
        a_whole[key] = a_whole.get(key, []) + [links.send(place, place, a_peer(1)), links.send(place, place, a_peer(3))]
        to_sibling(place)

    b_whole[0].wait_recv()
    b_halves.append(links.send(rows_of(chunk_of(at_a, b_left), 0), rows_of(chunk_of(at_a, b_left), 0), b_peer(1)))
    along_a(3, rows_of(chunk_of(at_a, b_left)))
    b_whole[1].wait_recv()
    b_halves.append(links.send(rows_of(chunk_of(at_a, b_right), 1), rows_of(chunk_of(at_a, b_right), 1), b_peer(3)))
    along_a(1, rows_of(chunk_of(at_a, b_right)))

    def pass_on(key, b):
        left, right = chunk_of(a_left, b), chunk_of(a_right, b)
        a_whole[key][0].wait_recv()
        a_halves[key] = [links.send(rows_of(left, 0), rows_of(left, 0), a_peer(1))]
        to_sibling(rows_of(left))
        a_whole[key][1].wait_recv()
        a_halves[key].append(links.send(rows_of(right, 1), rows_of(right, 1), a_peer(3)))
        to_sibling(rows_of(right))

    pass_on(0, at_b)
    far = chunk_of(at_a, b_far)
    b_halves[0].wait_recv()
    b_halves[1].wait_recv()
    along_a(2, rows_of(far))

    z_left_place = gview_hbm.at[pl.ds(pl.multiple_of(z_left * seg_part, seg_part), z_half)]
    z_right_place = gview_hbm.at[pl.ds(pl.multiple_of(z_right * seg_part + z_half, z_half), z_half)]
    z_whole[0].wait_recv()
    z_halves = [links.send(z_left_place, z_left_place, z_peer(1))]
    z_whole[1].wait_recv()
    z_halves.append(links.send(z_right_place, z_right_place, z_peer(3)))

    pass_on(3, b_left)
    pass_on(1, b_right)

    def far_halves(key, b):
        chunk = chunk_of(a_far, b)
        for way in range(2):
            a_halves[key][way].wait_recv()
            to_sibling(rows_of(chunk, way))

    far_halves(0, at_b)
    pass_on(2, b_far)
    far_halves(3, b_left)
    far_halves(1, b_right)
    far_halves(2, b_far)
    for copy in z_halves + across:
        copy.wait_recv()
    keep.wait()
    keep_view.wait()
    links.drain()


def balance(mesh, one, two, protos, pair):
    nx, ny, nz = mesh.shape["replica"], mesh.shape["batch"] // 2, mesh.shape["proto"]
    segs, width = one.shape
    count = protos.shape[0]
    both = 2 * segs
    z_half = both // nz // 2
    copies = ITERS * (2 * (2 * nx - 1) + (ny - 1) + (nz - 1)) + 80
    hbm = pl.BlockSpec(memory_space=pl.ANY)
    return pl.pallas_call(
        functools.partial(balance_kernel, nx, ny, nz),
        out_shape=(
            jax.ShapeDtypeStruct((both, width), F32),
            jax.ShapeDtypeStruct((count, width), F32),
        ),
        in_specs=[hbm, hbm, hbm, pl.BlockSpec(memory_space=pltpu.VMEM)],
        out_specs=(hbm, hbm),
        scratch_shapes=[
            pltpu.VMEM((both, width), BF16),
            pltpu.VMEM((both, count), F32),
            [pltpu.VMEM((both, count // 8), BF16)] * 8,
            pltpu.VMEM((both, width), BF16),
            pltpu.VMEM((width, both), BF16),
            pltpu.VMEM((segs, width), BF16),
            pltpu.VMEM((count, width), BF16),
            pltpu.VMEM((segs, segs), BF16),
            pltpu.VMEM((both, 128), F32),
            pltpu.VMEM((both, 128), F32),
            pltpu.VMEM((ITERS, 8, 8, 128), F32),
            pltpu.VMEM((ITERS, 8, 8, 128), F32),
            pltpu.VMEM((ITERS, ny, 8, 128), F32),
            pltpu.VMEM((ITERS, 8, 8, 128), F32),
            pltpu.VMEM((ITERS, 16, 128), F32),
            pltpu.VMEM((ITERS, nz, 16, 128), F32),
            pltpu.VMEM((16, 128), F32),
            pltpu.VMEM((both, 128), F32),
            pltpu.VMEM((both, 128), F32),
            [pltpu.VMEM((4, width, 128), F32)] * 8,
            pltpu.VMEM((4, 4, width, 128), F32),
            pltpu.VMEM((both, width), F32),
            pltpu.VMEM((128, width), BF16),
            pltpu.VMEM((128, width), F32),
            pltpu.VMEM((both // nz, width), F32),
        ]
        + [pltpu.VMEM((2, 2, width, 128), F32)] * 3
        + [pltpu.VMEM((2, width // 2, 128), F32)] * 3
        + [pltpu.VMEM((2, z_half, width), F32)] * 3
        + [
            pltpu.SemaphoreType.DMA((copies,)),
            pltpu.SemaphoreType.DMA((copies,)),
            pltpu.SemaphoreType.DMA((6,)),
        ],
        compiler_params=pltpu.CompilerParams(
            collective_id=0, has_side_effects=True, vmem_limit_bytes=62 << 20
        ),
        name="balance",
    )(one, two, protos, pair)


def hand_over_kernel(gview, gproto, one_out, two_out, proto_out, sems):
    segs = one_out.shape[0]
    parts = sems.shape[0] - 2
    rows = proto_out.shape[0] // parts
    copies = [
        pltpu.make_async_copy(gproto.at[i * rows:(i + 1) * rows], proto_out.at[i * rows:(i + 1) * rows], sems.at[i])
        for i in range(parts)
    ]
    copies.append(pltpu.make_async_copy(gview.at[0:segs], one_out, sems.at[parts]))
    copies.append(pltpu.make_async_copy(gview.at[segs:2 * segs], two_out, sems.at[parts + 1]))
    for copy in copies:
        copy.start()
    for copy in copies:
        copy.wait()


def hand_over(gview, gproto):
    half = jax.ShapeDtypeStruct((gview.shape[0] // 2, gview.shape[1]), F32)
    hbm = pl.BlockSpec(memory_space=pl.ANY)
    return pl.pallas_call(
        hand_over_kernel,
        out_shape=(half, half, jax.ShapeDtypeStruct(gproto.shape, F32)),
        in_specs=[hbm] * 2,
        out_specs=(hbm,) * 3,
        scratch_shapes=[pltpu.SemaphoreType.DMA((10,))],
        name="hand_over",
    )(gview, gproto)


def per_device(mesh, view_one, view_two, prototypes, pairing):
    gview, gproto = balance(mesh, view_one, view_two, prototypes, pairing)
    return hand_over(gview, gproto)


def solution(mesh):
    rows = P(("batch", "replica"), None)
    protos = P("proto", None)
    return jax.shard_map(
        functools.partial(per_device, mesh),
        mesh=mesh,
        in_specs=(rows, rows, protos, rows),
        out_specs=(rows, rows, protos),
        check_vma=False,
    )
```

```python
import functools

import jax
import jax.numpy as jnp
from jax import lax
from jax.experimental import pallas as pl
from jax.experimental.pallas import tpu as pltpu
from jax.sharding import PartitionSpec as P

ITERS = 3
EPS = 1e-06
F32 = jnp.float32
BF16 = jnp.bfloat16
MESH = pl.DeviceIdType.MESH
NN = (((1,), (0,)), ((), ()))
NT = (((1,), (1,)), ((), ()))
TN = (((0,), (0,)), ((), ()))
LOG2E = 1.4426950408889634


def dot(a, b, dims):
    return lax.dot_general(a, b, dims, preferred_element_type=F32)


def here():
    batch = lax.axis_index("batch")
    return lax.div(batch, 2), lax.rem(batch, 2), lax.axis_index("replica"), lax.axis_index("proto")


class Links:
    def __init__(self, send_sem, recv_sem):
        self.send_sem, self.recv_sem, self.used, self.sent = send_sem, recv_sem, 0, []

    def send(self, src, dst, peer):
        copy = pltpu.make_async_remote_copy(
            src_ref=src, dst_ref=dst,
            send_sem=self.send_sem.at[self.used], recv_sem=self.recv_sem.at[self.used],
            device_id=peer, device_id_type=MESH,
        )
        copy.start()
        self.used += 1
        self.sent.append(copy)
        return copy

    def drain(self):
        for copy in self.sent:
            copy.wait_send()
        self.sent = []


def back(d, raw):
    xf = raw.astype(F32)
    inv = lax.rsqrt(jnp.sum(xf * xf, -1, keepdims=True) + EPS)
    u = xf * inv
    return inv * (d - u * jnp.sum(u * d, -1, keepdims=True))


def balance_kernel(
    nx, ny, nz,
    one_hbm, two_hbm, proto_hbm, pair_ref,
    gview_hbm, gproto_hbm,
    raw, expo, dscore, low_seg, low_seg_t, low_two, low_proto, onehot, row_scale, prob_scale,
    cols, cols_in, cols_y, weight, rows, rows_in, tile_u, row_part, tot_part,
    dproto, from_core, dunit, own_proto, gproto, gview,
    a_relay, a_plain, a_joint, b_relay, b_plain, b_joint, z_relay, z_plain, z_joint,
    send_sem, recv_sem, local_sem,
):
    y, core, x, z = here()
    line = 2 * nx
    spot = core * nx + x
    links = Links(send_sem, recv_sem)
    at_a = core * y + (1 - core) * x
    at_b = core * x + (1 - core) * y
    mine = core * 16 + at_a * 4 + at_b

    def line_peer(step):
        other = lax.rem(spot + step, line)
        return other, (y * 2 + lax.div(other, nx), lax.rem(other, nx), z)

    def y_peer(step):
        return (lax.rem(y + step, ny) * 2 + core, x, z)

    def z_peer(step):
        return (y * 2 + core, x, lax.rem(z + step, nz))

    def a_peer(step):
        return (lax.rem(y + core * step, ny) * 2 + core, lax.rem(x + (1 - core) * step, nx), z)

    def b_peer(step):
        return (lax.rem(y + (1 - core) * step, ny) * 2 + core, lax.rem(x + core * step, nx), z)

    sibling = (y * 2 + 1 - core, x, z)

    segs = one_hbm.shape[0]
    protos, width = low_proto.shape
    both = 2 * segs
    fetch = [
        pltpu.make_async_copy(one_hbm, raw.at[0:segs], local_sem.at[0]),
        pltpu.make_async_copy(two_hbm, raw.at[segs:both], local_sem.at[1]),
        pltpu.make_async_copy(proto_hbm, low_proto, local_sem.at[2]),
        pltpu.make_async_copy(proto_hbm.at[pl.ds(mine * 128, 128)], own_proto, local_sem.at[3]),
    ]
    for copy in fetch:
        copy.start()
    peers = (
        [line_peer(s)[1] for s in range(1, line)]
        + [y_peer(s) for s in range(1, ny)]
        + [z_peer(s) for s in range(1, nz)]
    )
    barrier = pltpu.get_barrier_semaphore()
    for peer in peers:
        pl.semaphore_signal(barrier, inc=1, device_id=peer, device_id_type=MESH)

    def unit(block):
        xf = block.astype(F32)
        inv = lax.rsqrt(jnp.sum(xf * xf, -1, keepdims=True) + EPS)
        return (xf * inv).astype(BF16)

    def norm_views(i, carry):
        at = pl.ds(pl.multiple_of(i * 128, 128), 128)
        low_seg[at, :] = unit(raw[at, :])
        low_two[at, :] = unit(raw[pl.ds(pl.multiple_of(segs + i * 128, 128), 128), :])
        return carry

    fetch[0].wait()
    fetch[1].wait()
    lax.fori_loop(0, segs // 128, norm_views, 0, unroll=2)
    pair = jnp.broadcast_to(pair_ref[...], (segs, segs))
    number = lax.broadcasted_iota(jnp.int32, (segs, segs), 0)
    onehot[...] = jnp.where(pair == number, 1.0, 0.0).astype(BF16)
    low_seg[segs:both, :] = dot(onehot[...], low_two[...], TN).astype(BF16)
    def norm_protos(i, carry):
        at = pl.ds(pl.multiple_of(i * 128, 128), 128)
        low_proto[at, :] = unit(low_proto[at, :])
        return carry

    fetch[2].wait()
    lax.fori_loop(0, protos // 128, norm_protos, 0, unroll=4)

    wide = protos // 4

    def scores(j, carry):
        for q in range(wide // 256):
            at = pl.ds(pl.multiple_of(j * wide + q * 256, 256), 256)
            s = dot(low_seg[...], low_proto[at, :], NT)
            e = jnp.exp2(s * (10.0 * LOG2E))
            expo[:, at] = e
            k = e * e
            for view in range(2):
                total = jnp.sum(k[view * segs:(view + 1) * segs], axis=0, keepdims=True)
                for h in range(2):
                    cols[0, view * 4 + j, q * 2 + h:q * 2 + h + 1, :] = total[:, h * 128:(h + 1) * 128]
        return carry

    lax.fori_loop(0, 4, scores, 0)

    def col_sums(it):
        def block(k, carry):
            first = pl.multiple_of(lax.div(k, 4) * segs, segs)
            left = lax.rem(k, 4) * wide

            def some(r, acc):
                acc = list(acc)
                at = pl.ds(pl.multiple_of(first + r * 128, 128), 128)
                scale = row_scale.at[at]
                tiles = expo.at[at, pl.ds(pl.multiple_of(left, 128), wide)]
                for t in range(16):
                    u = scale[t * 8:(t + 1) * 8, :]
                    for l in range(wide // 128):
                        e = tiles[t * 8:(t + 1) * 8, l * 128:(l + 1) * 128]
                        n = (t % 2) * (wide // 128) + l
                        acc[n] = acc[n] + (e * e) * u
                return tuple(acc)

            zero = jnp.zeros((8, 128), F32)
            acc = lax.fori_loop(0, segs // 128, some, (zero,) * (wide // 64))
            acc = [acc[l] + acc[wide // 128 + l] for l in range(wide // 128)]
            for l in range(wide // 128):
                cols[it, k, l:l + 1, :] = jnp.sum(acc[l], axis=0, keepdims=True)
            return carry

        lax.fori_loop(0, 8, block, 0)

    def turn_segs():
        for i in range(both // 128):
            block = low_seg[i * 128:(i + 1) * 128, :].astype(F32)
            low_seg_t[:, i * 128:(i + 1) * 128] = jnp.transpose(block).astype(BF16)

    def all_cols(it):
        copies = []
        for s in range(1, line):
            other, peer = line_peer(s)
            copies.append(links.send(cols.at[it, other], cols_in.at[it, spot], peer))
        cols_in[it, spot] = cols[it, spot]
        if it == 0:
            turn_segs()
        for copy in copies:
            copy.wait_recv()
        total = cols_in[it, 0]
        for k in range(1, line):
            total = total + cols_in[it, k]
        cols_y[it, y] = total
        copies = []
        for s in range(1, ny):
            copies.append(links.send(cols_y.at[it, y], cols_y.at[it, y], y_peer(s)))
        for copy in copies:
            copy.wait_recv()
        total = cols_y[it, 0]
        for k in range(1, ny):
            total = total + cols_y[it, k]
        weight[it, spot] = 1.0 / total
        copies = []
        for s in range(1, line):
            copies.append(links.send(weight.at[it, spot], weight.at[it, spot], line_peer(s)[1]))
        for copy in copies:
            copy.wait_recv()

    def row_sums(it, with_total):
        def block(b, carry):
            at = pl.ds(pl.multiple_of(b * 64, 64), 64)
            view = lax.div(b, segs // 64)
            acc = jnp.zeros((64, 128), F32)
            tot = jnp.zeros((64, 128), F32)
            tiles = expo.at[at]
            scale = weight.at[it, pl.ds(view * 4, 4)]
            for l in range(protos // 128):
                e = tiles[:, l * 128:(l + 1) * 128]
                v = scale[l // 8, l % 8:l % 8 + 1, :]
                acc = acc + (e * e) * v
                if with_total:
                    tot = tot + e
            row_part[at, :] = acc
            if with_total:
                tot_part[at, :] = tot
            return carry

        lax.fori_loop(0, both // 64, block, 0)
        for b in range(both // 128):
            at = slice(b * 128, (b + 1) * 128)
            rows[it, b:b + 1, :] = jnp.sum(jnp.transpose(row_part[at, :]), axis=0, keepdims=True)
            if with_total:
                rows[it, 8 + b:9 + b, :] = jnp.sum(jnp.transpose(tot_part[at, :]), axis=0, keepdims=True)

    def spread(out, row):
        for b in range(both // 128):
            wide_row = jnp.broadcast_to(tile_u[row + b:row + b + 1, :], (128, 128))
            out[b * 128:(b + 1) * 128, :] = jnp.transpose(wide_row)

    def all_rows(it, with_total, scale):
        size = 16 if with_total else 8
        rows_in[it, z] = rows[it]
        copies = []
        for s in range(1, nz):
            copies.append(links.send(rows.at[it, 0:size], rows_in.at[it, z, 0:size], z_peer(s)))
        for copy in copies:
            copy.wait_recv()
        total = rows_in[it, 0, 0:size]
        for k in range(1, nz):
            total = total + rows_in[it, k, 0:size]
        tile_u[0:8, :] = scale / total[0:8]
        spread(row_scale, 0)
        if with_total:
            tile_u[8:16, :] = 5.0 / total[8:16]
            spread(prob_scale, 8)

    pl.semaphore_wait(barrier, len(peers))
    for it in range(ITERS):
        if it:
            col_sums(it)
        all_cols(it)
        row_sums(it, it == 0)
        all_rows(it, it == 0, 5.0 if it == ITERS - 1 else 1.0)

    last = ITERS - 1

    half_b = 256

    def elements(ds, chunk, j):
        tiles = expo.at[:, pl.ds(pl.multiple_of(chunk * 128 + j * half_b, half_b), half_b)]
        to = ds.at[:, pl.ds(pl.multiple_of(j * half_b, half_b), half_b)]
        tile = lax.div(chunk, 8)
        row = lax.rem(chunk, 8) + j * 2
        v_one = [weight[last, tile, pl.ds(row + h, 1), :] for h in range(2)]
        v_two = [weight[last, 4 + tile, pl.ds(row + h, 1), :] for h in range(2)]
        for b in range(segs // 32):
            first = slice(b * 32, (b + 1) * 32)
            second = slice(segs + b * 32, segs + (b + 1) * 32)
            u_one, u_two = row_scale[first, :], row_scale[second, :]
            p_one, p_two = prob_scale[first, :], prob_scale[second, :]
            for h in range(2):
                at = slice(h * 128, (h + 1) * 128)
                e_one = tiles[first, at]
                e_two = tiles[second, at]
                t_one = (e_two * e_two) * u_two * v_two[h]
                t_two = (e_one * e_one) * u_one * v_one[h]
                to[first, at] = (e_one * p_one - t_one).astype(BF16)
                to[second, at] = (e_two * p_two - t_two).astype(BF16)

    def step(new, old):
        def both_parts(j, carry):
            if old is not None:
                at = pl.ds(pl.multiple_of(j * half_b, half_b), half_b)
                part = dot(low_seg_t[...], dscore[old][:, at], NN)
                dproto[old][2 * j] = part[:, 0:128]
                dproto[old][2 * j + 1] = part[:, 128:256]
            if new is not None:
                elements(dscore[new], chunks[new], j)
            return carry

        lax.fori_loop(0, 2, both_parts, 0)

    order = (2, 1, 3, 0)
    chunks, spots = [], []
    for t in order:
        for half, place in ((1 - core, at_b), (core, at_a)):
            spots.append(lax.rem(place + t, 4))
            chunks.append(half * 16 + spots[-1] * 4)
    relays, plains, joints = [None] * 2, [None] * 2, [None] * 2
    crossing = [None] * 8
    step(0, None)
    for g in range(8):
        step(g + 1 if g < 7 else None, g)
        if g % 2 == 0:
            crossing[g] = links.send(dproto[g], from_core.at[g // 2], sibling)
            continue
        crossing[g - 1].wait_recv()
        for q in range(4):
            dproto[g][q] = dproto[g][q] + from_core[g // 2, q]
        low, high = dproto[g].at[0:2], dproto[g].at[2:4]
        t = order[g // 2]
        if t == 2:
            relays = [links.send(low, a_relay.at[0], a_peer(1)), links.send(high, a_relay.at[1], a_peer(3))]
        if t == 1:
            plains[0] = links.send(high, a_plain.at[0], a_peer(1))
        if t == 3:
            plains[1] = links.send(low, a_plain.at[1], a_peer(3))
    d_right, d_left, d_own = dproto[3], dproto[5], dproto[7]

    def views(i):
        at = slice(i * 256, (i + 1) * 256)
        total = None
        for g in range(8):
            rows_g = low_proto[pl.ds(pl.multiple_of(chunks[g] * 128, 512), 512), :]
            term = dot(dscore[g][at, :], rows_g, NN)
            total = term if total is None else total + term
        dunit[at, :] = total

    views(0)
    views(1)
    relays[0].wait_recv()
    for q in range(2):
        d_right[q] = d_right[q] + a_relay[0, q]
    joints[0] = links.send(d_right.at[0:2], a_joint.at[0], a_peer(1))
    relays[1].wait_recv()
    for q in range(2):
        d_left[2 + q] = d_left[2 + q] + a_relay[1, q]
    joints[1] = links.send(d_left.at[2:4], a_joint.at[1], a_peer(3))

    views(2)
    views(3)
    d = dunit[segs:both, :]
    top = d.astype(BF16)
    rest = d - top.astype(F32)
    middle = rest.astype(BF16)
    end = (rest - middle.astype(F32)).astype(BF16)
    rest = dot(onehot[...], middle, NN) + dot(onehot[...], end, NN)
    dunit[segs:both, :] = dot(onehot[...], top, NN) + rest

    def part(ref, k, size, lower):
        half = size // 2
        start = k * size + (0 if lower else half)
        return ref.at[pl.ds(pl.multiple_of(start, half), half)]

    seg_part = both // nz
    z_right, z_left, z_far = lax.rem(z + 1, 4), lax.rem(z + 3, 4), lax.rem(z + 2, 4)
    z_relays = [
        links.send(part(dunit, z_far, seg_part, True), z_relay.at[0], z_peer(1)),
        links.send(part(dunit, z_far, seg_part, False), z_relay.at[1], z_peer(3)),
    ]
    z_plains = [
        links.send(part(dunit, z_right, seg_part, False), z_plain.at[0], z_peer(1)),
        links.send(part(dunit, z_left, seg_part, True), z_plain.at[1], z_peer(3)),
    ]

    for copy in plains + joints:
        copy.wait_recv()
    for q in range(2):
        d_own[q] = d_own[q] + (a_joint[0, q] + a_plain[1, q])
        d_own[2 + q] = d_own[2 + q] + (a_plain[0, q] + a_joint[1, q])
    b_right, b_left, b_far = lax.rem(at_b + 1, 4), lax.rem(at_b + 3, 4), lax.rem(at_b + 2, 4)
    half = width // 2
    b_relays = [
        links.send(d_own.at[b_far, 0:half], b_relay.at[0], b_peer(1)),
        links.send(d_own.at[b_far, half:width], b_relay.at[1], b_peer(3)),
    ]
    b_plains = [
        links.send(d_own.at[b_right, half:width], b_plain.at[0], b_peer(1)),
        links.send(d_own.at[b_left, 0:half], b_plain.at[1], b_peer(3)),
    ]

    z_half = seg_part // 2
    z_joints = []
    for way, k, skip, peer in ((0, z_right, 0, z_peer(1)), (1, z_left, z_half, z_peer(3))):
        z_relays[way].wait_recv()
        at = pl.ds(pl.multiple_of(k * seg_part + skip, z_half), z_half)
        dunit[at, :] = dunit[at, :] + z_relay[way]
        z_joints.append(links.send(dunit.at[at], z_joint.at[way], peer))

    b_joints = []
    for way, k, skip, peer in ((0, b_right, 0, b_peer(1)), (1, b_left, half, b_peer(3))):
        b_relays[way].wait_recv()
        at = slice(skip, skip + half)
        d_own[k, at, :] = d_own[k, at, :] + b_relay[way]
        b_joints.append(links.send(d_own.at[k, at], b_joint.at[way], peer))
    for copy in b_plains + b_joints:
        copy.wait_recv()
    me = at_b
    d_own[me, 0:half, :] = d_own[me, 0:half, :] + (b_joint[0] + b_plain[1])
    d_own[me, half:width, :] = d_own[me, half:width, :] + (b_plain[0] + b_joint[1])
    fetch[3].wait()
    gproto[...] = back(jnp.transpose(d_own[me]), own_proto[...])

    def rows_of(chunk, part=None):
        if part is None:
            return gproto_hbm.at[pl.ds(pl.multiple_of(chunk * 128, 128), 128)]
        return gproto_hbm.at[pl.ds(pl.multiple_of(chunk * 128 + part * 64, 64), 64)]

    def chunk_of(a, b):
        return core * 16 + a * 4 + b

    across = []

    def to_sibling(place, src=None):
        across.append(links.send(place if src is None else src, place, sibling))

    b_whole = [links.send(gproto, rows_of(mine), b_peer(1)), links.send(gproto, rows_of(mine), b_peer(3))]
    a_whole = {0: [links.send(gproto, rows_of(mine), a_peer(1)), links.send(gproto, rows_of(mine), a_peer(3))]}
    to_sibling(rows_of(mine), gproto)
    keep = pltpu.make_async_copy(gproto, rows_of(mine), local_sem.at[4])
    keep.start()

    for copy in z_plains + z_joints:
        copy.wait_recv()
    at = pl.ds(pl.multiple_of(z * seg_part, z_half), z_half)
    dunit[at, :] = dunit[at, :] + (z_joint[0] + z_plain[1])
    at = pl.ds(pl.multiple_of(z * seg_part + z_half, z_half), z_half)
    dunit[at, :] = dunit[at, :] + (z_plain[0] + z_joint[1])
    at = pl.ds(pl.multiple_of(z * seg_part, seg_part), seg_part)
    gview[...] = back(dunit[at, :], raw[at, :])
    place = gview_hbm.at[at]
    z_whole = [links.send(gview, place, z_peer(1)), links.send(gview, place, z_peer(3))]
    keep_view = pltpu.make_async_copy(gview, place, local_sem.at[5])
    keep_view.start()

    b_halves, a_halves = [], {}
    a_right, a_left, a_far = lax.rem(at_a + 1, 4), lax.rem(at_a + 3, 4), lax.rem(at_a + 2, 4)

    def along_a(key, place):
        a_whole[key] = a_whole.get(key, []) + [links.send(place, place, a_peer(1)), links.send(place, place, a_peer(3))]
        to_sibling(place)

    b_whole[0].wait_recv()
    b_halves.append(links.send(rows_of(chunk_of(at_a, b_left), 0), rows_of(chunk_of(at_a, b_left), 0), b_peer(1)))
    along_a(3, rows_of(chunk_of(at_a, b_left)))
    b_whole[1].wait_recv()
    b_halves.append(links.send(rows_of(chunk_of(at_a, b_right), 1), rows_of(chunk_of(at_a, b_right), 1), b_peer(3)))
    along_a(1, rows_of(chunk_of(at_a, b_right)))

    def pass_on(key, b):
        left, right = chunk_of(a_left, b), chunk_of(a_right, b)
        a_whole[key][0].wait_recv()
        a_halves[key] = [links.send(rows_of(left, 0), rows_of(left, 0), a_peer(1))]
        to_sibling(rows_of(left))
        a_whole[key][1].wait_recv()
        a_halves[key].append(links.send(rows_of(right, 1), rows_of(right, 1), a_peer(3)))
        to_sibling(rows_of(right))

    pass_on(0, at_b)
    far = chunk_of(at_a, b_far)
    b_halves[0].wait_recv()
    b_halves[1].wait_recv()
    along_a(2, rows_of(far))

    z_left_place = gview_hbm.at[pl.ds(pl.multiple_of(z_left * seg_part, seg_part), z_half)]
    z_right_place = gview_hbm.at[pl.ds(pl.multiple_of(z_right * seg_part + z_half, z_half), z_half)]
    z_whole[0].wait_recv()
    z_halves = [links.send(z_left_place, z_left_place, z_peer(1))]
    z_whole[1].wait_recv()
    z_halves.append(links.send(z_right_place, z_right_place, z_peer(3)))

    pass_on(3, b_left)
    pass_on(1, b_right)

    def far_halves(key, b):
        chunk = chunk_of(a_far, b)
        for way in range(2):
            a_halves[key][way].wait_recv()
            to_sibling(rows_of(chunk, way))

    far_halves(0, at_b)
    pass_on(2, b_far)
    far_halves(3, b_left)
    far_halves(1, b_right)
    far_halves(2, b_far)
    for copy in z_halves + across:
        copy.wait_recv()
    keep.wait()
    keep_view.wait()
    links.drain()


def balance(mesh, one, two, protos, pair):
    nx, ny, nz = mesh.shape["replica"], mesh.shape["batch"] // 2, mesh.shape["proto"]
    segs, width = one.shape
    count = protos.shape[0]
    both = 2 * segs
    z_half = both // nz // 2
    copies = ITERS * (2 * (2 * nx - 1) + (ny - 1) + (nz - 1)) + 80
    hbm = pl.BlockSpec(memory_space=pl.ANY)
    return pl.pallas_call(
        functools.partial(balance_kernel, nx, ny, nz),
        out_shape=(
            jax.ShapeDtypeStruct((both, width), F32),
            jax.ShapeDtypeStruct((count, width), F32),
        ),
        in_specs=[hbm, hbm, hbm, pl.BlockSpec(memory_space=pltpu.VMEM)],
        out_specs=(hbm, hbm),
        scratch_shapes=[
            pltpu.VMEM((both, width), BF16),
            pltpu.VMEM((both, count), F32),
            [pltpu.VMEM((both, count // 8), BF16)] * 8,
            pltpu.VMEM((both, width), BF16),
            pltpu.VMEM((width, both), BF16),
            pltpu.VMEM((segs, width), BF16),
            pltpu.VMEM((count, width), BF16),
            pltpu.VMEM((segs, segs), BF16),
            pltpu.VMEM((both, 128), F32),
            pltpu.VMEM((both, 128), F32),
            pltpu.VMEM((ITERS, 8, 8, 128), F32),
            pltpu.VMEM((ITERS, 8, 8, 128), F32),
            pltpu.VMEM((ITERS, ny, 8, 128), F32),
            pltpu.VMEM((ITERS, 8, 8, 128), F32),
            pltpu.VMEM((ITERS, 16, 128), F32),
            pltpu.VMEM((ITERS, nz, 16, 128), F32),
            pltpu.VMEM((16, 128), F32),
            pltpu.VMEM((both, 128), F32),
            pltpu.VMEM((both, 128), F32),
            [pltpu.VMEM((4, width, 128), F32)] * 8,
            pltpu.VMEM((4, 4, width, 128), F32),
            pltpu.VMEM((both, width), F32),
            pltpu.VMEM((128, width), BF16),
            pltpu.VMEM((128, width), F32),
            pltpu.VMEM((both // nz, width), F32),
        ]
        + [pltpu.VMEM((2, 2, width, 128), F32)] * 3
        + [pltpu.VMEM((2, width // 2, 128), F32)] * 3
        + [pltpu.VMEM((2, z_half, width), F32)] * 3
        + [
            pltpu.SemaphoreType.DMA((copies,)),
            pltpu.SemaphoreType.DMA((copies,)),
            pltpu.SemaphoreType.DMA((6,)),
        ],
        compiler_params=pltpu.CompilerParams(
            collective_id=0, has_side_effects=True, vmem_limit_bytes=62 << 20
        ),
        name="balance",
    )(one, two, protos, pair)


def hand_over_kernel(gview, gproto, one_out, two_out, proto_out, stage, sems):
    size = stage.shape[1]
    pairs = [(gview.at[0:size], one_out), (gview.at[size:2 * size], two_out)]
    for i in range(proto_out.shape[0] // size):
        at = slice(i * size, (i + 1) * size)
        pairs.append((gproto.at[at], proto_out.at[at]))
    come = [pltpu.make_async_copy(src, stage.at[i], sems.at[0, i]) for i, (src, _) in enumerate(pairs)]
    go = [pltpu.make_async_copy(stage.at[i], dst, sems.at[1, i]) for i, (_, dst) in enumerate(pairs)]
    for copy in come:
        copy.start()
    for arrived, copy in zip(come, go):
        arrived.wait()
        copy.start()
    for copy in go:
        copy.wait()


def hand_over(gview, gproto):
    segs, width = gview.shape[0] // 2, gview.shape[1]
    half = jax.ShapeDtypeStruct((segs, width), F32)
    parts = 2 + gproto.shape[0] // segs
    hbm = pl.BlockSpec(memory_space=pltpu.HBM)
    return pl.pallas_call(
        hand_over_kernel,
        out_shape=(half, half, jax.ShapeDtypeStruct(gproto.shape, F32)),
        in_specs=[hbm] * 2,
        out_specs=(hbm,) * 3,
        scratch_shapes=[pltpu.VMEM((parts, segs, width), F32), pltpu.SemaphoreType.DMA((2, parts))],
        compiler_params=pltpu.CompilerParams(vmem_limit_bytes=62 << 20),
        name="hand_over",
    )(gview, gproto)


def per_device(mesh, view_one, view_two, prototypes, pairing):
    gview, gproto = balance(mesh, view_one, view_two, prototypes, pairing)
    return hand_over(gview, gproto)


def solution(mesh):
    rows = P(("batch", "replica"), None)
    protos = P("proto", None)
    return jax.shard_map(
        functools.partial(per_device, mesh),
        mesh=mesh,
        in_specs=(rows, rows, protos, rows),
        out_specs=(rows, rows, protos),
        check_vma=False,
    )
```

```python
import functools

import jax
import jax.numpy as jnp
from jax import lax
from jax.experimental import pallas as pl
from jax.experimental.pallas import tpu as pltpu
from jax.sharding import PartitionSpec as P

ITERS = 3
EPS = 1e-06
F32 = jnp.float32
BF16 = jnp.bfloat16
MESH = pl.DeviceIdType.MESH
NN = (((1,), (0,)), ((), ()))
NT = (((1,), (1,)), ((), ()))
TN = (((0,), (0,)), ((), ()))
LOG2E = 1.4426950408889634


def dot(a, b, dims):
    return lax.dot_general(a, b, dims, preferred_element_type=F32)


def here():
    batch = lax.axis_index("batch")
    return lax.div(batch, 2), lax.rem(batch, 2), lax.axis_index("replica"), lax.axis_index("proto")


class Links:
    def __init__(self, send_sem, recv_sem):
        self.send_sem, self.recv_sem, self.used, self.sent = send_sem, recv_sem, 0, []

    def send(self, src, dst, peer):
        copy = pltpu.make_async_remote_copy(
            src_ref=src, dst_ref=dst,
            send_sem=self.send_sem.at[self.used], recv_sem=self.recv_sem.at[self.used],
            device_id=peer, device_id_type=MESH,
        )
        copy.start()
        self.used += 1
        self.sent.append(copy)
        return copy

    def drain(self):
        for copy in self.sent:
            copy.wait_send()
        self.sent = []


def back(d, raw):
    xf = raw.astype(F32)
    inv = lax.rsqrt(jnp.sum(xf * xf, -1, keepdims=True) + EPS)
    u = xf * inv
    return inv * (d - u * jnp.sum(u * d, -1, keepdims=True))


def balance_kernel(
    nx, ny, nz,
    one_hbm, two_hbm, proto_hbm, pair_ref,
    gview_hbm, gproto_hbm,
    raw, expo, dscore, low_seg, low_seg_t, low_two, low_proto, onehot, row_scale, prob_scale,
    cols, cols_in, plane_in, weight, rows, rows_in, tile_u, row_part, tot_part,
    dproto, from_core, dunit, own_proto, gproto, gview,
    a_relay, a_plain, a_joint, b_relay, b_plain, b_joint, z_relay, z_plain, z_joint,
    send_sem, recv_sem, local_sem,
):
    y, core, x, z = here()
    spot = y * nx + x
    links = Links(send_sem, recv_sem)
    at_a = core * y + (1 - core) * x
    at_b = core * x + (1 - core) * y
    mine = core * 16 + at_a * 4 + at_b

    def plane_peer(dx, dy):
        return (lax.rem(y + dy, ny) * 2 + core, lax.rem(x + dx, nx), z)

    def z_peer(step):
        return (y * 2 + core, x, lax.rem(z + step, nz))

    def a_peer(step):
        return (lax.rem(y + core * step, ny) * 2 + core, lax.rem(x + (1 - core) * step, nx), z)

    def b_peer(step):
        return (lax.rem(y + (1 - core) * step, ny) * 2 + core, lax.rem(x + core * step, nx), z)

    sibling = (y * 2 + 1 - core, x, z)

    segs = one_hbm.shape[0]
    protos, width = low_proto.shape
    both = 2 * segs
    pieces = 8
    piece = protos // pieces
    fetch = [
        pltpu.make_async_copy(one_hbm, raw.at[0:segs], local_sem.at[0]),
        pltpu.make_async_copy(two_hbm, raw.at[segs:both], local_sem.at[1]),
        pltpu.make_async_copy(proto_hbm.at[pl.ds(mine * 128, 128)], own_proto, local_sem.at[2]),
    ]
    fetch_protos = [
        pltpu.make_async_copy(
            proto_hbm.at[i * piece:(i + 1) * piece], low_proto.at[i * piece:(i + 1) * piece], local_sem.at[3 + i]
        )
        for i in range(pieces)
    ]
    for copy in fetch + fetch_protos:
        copy.start()
    def hops(step):
        return min(step[0], nx - step[0]) + min(step[1], ny - step[1])

    steps = sorted([(dx, dy) for dx in range(nx) for dy in range(ny)][1:], key=hops, reverse=True)
    peers = [plane_peer(*p) for p in steps] + [z_peer(s) for s in range(1, nz)] + [sibling]
    barrier = pltpu.get_barrier_semaphore()
    for peer in peers:
        pl.semaphore_signal(barrier, inc=1, device_id=peer, device_id_type=MESH)

    def unit(block):
        xf = block.astype(F32)
        inv = lax.rsqrt(jnp.sum(xf * xf, -1, keepdims=True) + EPS)
        return (xf * inv).astype(BF16)

    def norm_views(i, carry):
        at = pl.ds(pl.multiple_of(i * 128, 128), 128)
        low_seg[at, :] = unit(raw[at, :])
        low_two[at, :] = unit(raw[pl.ds(pl.multiple_of(segs + i * 128, 128), 128), :])
        return carry

    fetch[0].wait()
    fetch[1].wait()
    lax.fori_loop(0, segs // 128, norm_views, 0, unroll=2)
    pair = jnp.broadcast_to(pair_ref[...], (segs, segs))
    number = lax.broadcasted_iota(jnp.int32, (segs, segs), 0)
    onehot[...] = jnp.where(pair == number, 1.0, 0.0).astype(BF16)
    low_seg[segs:both, :] = dot(onehot[...], low_two[...], TN).astype(BF16)
    def norm_protos(i, carry):
        at = pl.ds(pl.multiple_of(i * 128, 128), 128)
        low_proto[at, :] = unit(low_proto[at, :])
        return carry

    for i, copy in enumerate(fetch_protos):
        copy.wait()
        lax.fori_loop(i * piece // 128, (i + 1) * piece // 128, norm_protos, 0, unroll=4)

    wide = protos // 4

    def scores(j, carry):
        for q in range(wide // 256):
            at = pl.ds(pl.multiple_of(j * wide + q * 256, 256), 256)
            s = dot(low_seg[...], low_proto[at, :], NT)
            e = jnp.exp2(s * (10.0 * LOG2E))
            expo[:, at] = e
            k = e * e
            for view in range(2):
                total = jnp.sum(k[view * segs:(view + 1) * segs], axis=0, keepdims=True)
                for h in range(2):
                    cols[0, view * 4 + j, q * 2 + h:q * 2 + h + 1, :] = total[:, h * 128:(h + 1) * 128]
        return carry

    lax.fori_loop(0, 4, scores, 0)

    def col_sums(it, view):
        def block(j, carry):
            k = view * 4 + j
            first = pl.multiple_of(lax.div(k, 4) * segs, segs)
            left = lax.rem(k, 4) * wide

            def some(r, acc):
                acc = list(acc)
                at = pl.ds(pl.multiple_of(first + r * 128, 128), 128)
                scale = row_scale.at[at]
                tiles = expo.at[at, pl.ds(pl.multiple_of(left, 128), wide)]
                for t in range(16):
                    u = scale[t * 8:(t + 1) * 8, :]
                    for l in range(wide // 128):
                        e = tiles[t * 8:(t + 1) * 8, l * 128:(l + 1) * 128]
                        n = (t % 2) * (wide // 128) + l
                        acc[n] = acc[n] + (e * e) * u
                return tuple(acc)

            zero = jnp.zeros((8, 128), F32)
            acc = lax.fori_loop(0, segs // 128, some, (zero,) * (wide // 64))
            acc = [acc[l] + acc[wide // 128 + l] for l in range(wide // 128)]
            for l in range(wide // 128):
                cols[it, k, l:l + 1, :] = jnp.sum(acc[l], axis=0, keepdims=True)
            return carry

        lax.fori_loop(0, 4, block, 0)

    def turn_segs():
        for i in range(both // 128):
            block = low_seg[i * 128:(i + 1) * 128, :].astype(F32)
            low_seg_t[:, i * 128:(i + 1) * 128] = jnp.transpose(block).astype(BF16)

    def tiles_of(k):
        return pl.ds(pl.multiple_of(k * 4, 4), 4)

    def swap_cols(it):
        return links.send(cols.at[it, tiles_of(1 - core)], cols_in.at[it], sibling)

    def all_cols(it, swap):
        swap.wait_recv()
        plane_in[it, spot] = cols[it, tiles_of(core)] + cols_in[it]
        copies = [
            links.send(plane_in.at[it, spot], plane_in.at[it, spot], plane_peer(*p)) for p in steps
        ]
        if it == 0:
            turn_segs()
        for copy in copies:
            copy.wait_recv()
        total = plane_in[it, 0]
        for k in range(1, nx * ny):
            total = total + plane_in[it, k]
        weight[it, tiles_of(core)] = 1.0 / total
        return links.send(weight.at[it, tiles_of(core)], weight.at[it, tiles_of(core)], sibling)

    def row_sums(it, with_total, view):
        def block(b, carry):
            at = pl.ds(pl.multiple_of(view * segs + b * 64, 64), 64)
            acc = jnp.zeros((64, 128), F32)
            tot = jnp.zeros((64, 128), F32)
            tiles = expo.at[at]
            scale = weight.at[it, pl.ds(view * 4, 4)]
            for l in range(protos // 128):
                e = tiles[:, l * 128:(l + 1) * 128]
                v = scale[l // 8, l % 8:l % 8 + 1, :]
                acc = acc + (e * e) * v
                if with_total:
                    tot = tot + e
            row_part[at, :] = acc
            if with_total:
                tot_part[at, :] = tot
            return carry

        lax.fori_loop(0, segs // 64, block, 0)

    def turn_sums(it, with_total):
        for b in range(both // 128):
            at = slice(b * 128, (b + 1) * 128)
            rows[it, b:b + 1, :] = jnp.sum(jnp.transpose(row_part[at, :]), axis=0, keepdims=True)
            if with_total:
                rows[it, 8 + b:9 + b, :] = jnp.sum(jnp.transpose(tot_part[at, :]), axis=0, keepdims=True)

    def spread(out, row):
        for b in range(both // 128):
            wide_row = jnp.broadcast_to(tile_u[row + b:row + b + 1, :], (128, 128))
            out[b * 128:(b + 1) * 128, :] = jnp.transpose(wide_row)

    def all_rows(it, with_total, scale):
        size = 16 if with_total else 8
        rows_in[it, z] = rows[it]
        copies = []
        for s in range(1, nz):
            copies.append(links.send(rows.at[it, 0:size], rows_in.at[it, z, 0:size], z_peer(s)))
        for copy in copies:
            copy.wait_recv()
        total = rows_in[it, 0, 0:size]
        for k in range(1, nz):
            total = total + rows_in[it, k, 0:size]
        tile_u[0:8, :] = scale / total[0:8]
        spread(row_scale, 0)
        if with_total:
            tile_u[8:16, :] = 5.0 / total[8:16]
            spread(prob_scale, 8)

    pl.semaphore_wait(barrier, len(peers))
    for it in range(ITERS):
        if it:
            col_sums(it, 1 - core)
            swap = swap_cols(it)
            col_sums(it, core)
        else:
            swap = swap_cols(it)
        back_copy = all_cols(it, swap)
        row_sums(it, it == 0, core)
        back_copy.wait_recv()
        row_sums(it, it == 0, 1 - core)
        turn_sums(it, it == 0)
        all_rows(it, it == 0, 5.0 if it == ITERS - 1 else 1.0)

    last = ITERS - 1

    half_b = 256

    def elements(ds, chunk, j):
        tiles = expo.at[:, pl.ds(pl.multiple_of(chunk * 128 + j * half_b, half_b), half_b)]
        to = ds.at[:, pl.ds(pl.multiple_of(j * half_b, half_b), half_b)]
        tile = lax.div(chunk, 8)
        row = lax.rem(chunk, 8) + j * 2
        v_one = [weight[last, tile, pl.ds(row + h, 1), :] for h in range(2)]
        v_two = [weight[last, 4 + tile, pl.ds(row + h, 1), :] for h in range(2)]
        for b in range(segs // 32):
            first = slice(b * 32, (b + 1) * 32)
            second = slice(segs + b * 32, segs + (b + 1) * 32)
            u_one, u_two = row_scale[first, :], row_scale[second, :]
            p_one, p_two = prob_scale[first, :], prob_scale[second, :]
            for h in range(2):
                at = slice(h * 128, (h + 1) * 128)
                e_one = tiles[first, at]
                e_two = tiles[second, at]
                t_one = (e_two * e_two) * u_two * v_two[h]
                t_two = (e_one * e_one) * u_one * v_one[h]
                to[first, at] = (e_one * p_one - t_one).astype(BF16)
                to[second, at] = (e_two * p_two - t_two).astype(BF16)

    def step(new, old):
        def both_parts(j, carry):
            if old is not None:
                at = pl.ds(pl.multiple_of(j * half_b, half_b), half_b)
                part = dot(low_seg_t[...], dscore[old][:, at], NN)
                dproto[old][2 * j] = part[:, 0:128]
                dproto[old][2 * j + 1] = part[:, 128:256]
            if new is not None:
                elements(dscore[new], chunks[new], j)
            return carry

        lax.fori_loop(0, 2, both_parts, 0)

    order = (2, 1, 3, 0)
    chunks, spots = [], []
    for t in order:
        for half, place in ((1 - core, at_b), (core, at_a)):
            spots.append(lax.rem(place + t, 4))
            chunks.append(half * 16 + spots[-1] * 4)
    relays, plains, joints = [None] * 2, [None] * 2, [None] * 2
    crossing = [None] * 8
    step(0, None)
    for g in range(8):
        step(g + 1 if g < 7 else None, g)
        if g % 2 == 0:
            crossing[g] = links.send(dproto[g], from_core.at[g // 2], sibling)
            continue
        crossing[g - 1].wait_recv()
        for q in range(4):
            dproto[g][q] = dproto[g][q] + from_core[g // 2, q]
        low, high = dproto[g].at[0:2], dproto[g].at[2:4]
        t = order[g // 2]
        if t == 2:
            relays = [links.send(low, a_relay.at[0], a_peer(1)), links.send(high, a_relay.at[1], a_peer(3))]
        if t == 1:
            plains[0] = links.send(high, a_plain.at[0], a_peer(1))
        if t == 3:
            plains[1] = links.send(low, a_plain.at[1], a_peer(3))
    d_right, d_left, d_own = dproto[3], dproto[5], dproto[7]

    def views(i):
        at = slice(i * 256, (i + 1) * 256)
        total = None
        for g in range(8):
            rows_g = low_proto[pl.ds(pl.multiple_of(chunks[g] * 128, 512), 512), :]
            term = dot(dscore[g][at, :], rows_g, NN)
            total = term if total is None else total + term
        dunit[at, :] = total

    views(0)
    views(1)
    relays[0].wait_recv()
    for q in range(2):
        d_right[q] = d_right[q] + a_relay[0, q]
    joints[0] = links.send(d_right.at[0:2], a_joint.at[0], a_peer(1))
    relays[1].wait_recv()
    for q in range(2):
        d_left[2 + q] = d_left[2 + q] + a_relay[1, q]
    joints[1] = links.send(d_left.at[2:4], a_joint.at[1], a_peer(3))

    views(2)
    views(3)
    d = dunit[segs:both, :]
    top = d.astype(BF16)
    rest = d - top.astype(F32)
    middle = rest.astype(BF16)
    end = (rest - middle.astype(F32)).astype(BF16)
    rest = dot(onehot[...], middle, NN) + dot(onehot[...], end, NN)
    dunit[segs:both, :] = dot(onehot[...], top, NN) + rest

    def part(ref, k, size, lower):
        half = size // 2
        start = k * size + (0 if lower else half)
        return ref.at[pl.ds(pl.multiple_of(start, half), half)]

    seg_part = both // nz
    z_right, z_left, z_far = lax.rem(z + 1, 4), lax.rem(z + 3, 4), lax.rem(z + 2, 4)
    z_relays = [
        links.send(part(dunit, z_far, seg_part, True), z_relay.at[0], z_peer(1)),
        links.send(part(dunit, z_far, seg_part, False), z_relay.at[1], z_peer(3)),
    ]
    z_plains = [
        links.send(part(dunit, z_right, seg_part, False), z_plain.at[0], z_peer(1)),
        links.send(part(dunit, z_left, seg_part, True), z_plain.at[1], z_peer(3)),
    ]

    for copy in plains + joints:
        copy.wait_recv()
    for q in range(2):
        d_own[q] = d_own[q] + (a_joint[0, q] + a_plain[1, q])
        d_own[2 + q] = d_own[2 + q] + (a_plain[0, q] + a_joint[1, q])
    b_right, b_left, b_far = lax.rem(at_b + 1, 4), lax.rem(at_b + 3, 4), lax.rem(at_b + 2, 4)
    width_half = width // 2
    b_relays = [
        links.send(d_own.at[b_far, 0:width_half], b_relay.at[0], b_peer(1)),
        links.send(d_own.at[b_far, width_half:width], b_relay.at[1], b_peer(3)),
    ]
    b_plains = [
        links.send(d_own.at[b_right, width_half:width], b_plain.at[0], b_peer(1)),
        links.send(d_own.at[b_left, 0:width_half], b_plain.at[1], b_peer(3)),
    ]

    z_half = seg_part // 2
    z_joints = []
    for way, k, skip, peer in ((0, z_right, 0, z_peer(1)), (1, z_left, z_half, z_peer(3))):
        z_relays[way].wait_recv()
        at = pl.ds(pl.multiple_of(k * seg_part + skip, z_half), z_half)
        dunit[at, :] = dunit[at, :] + z_relay[way]
        z_joints.append(links.send(dunit.at[at], z_joint.at[way], peer))

    b_joints = []
    for way, k, skip, peer in ((0, b_right, 0, b_peer(1)), (1, b_left, width_half, b_peer(3))):
        b_relays[way].wait_recv()
        at = slice(skip, skip + width_half)
        d_own[k, at, :] = d_own[k, at, :] + b_relay[way]
        b_joints.append(links.send(d_own.at[k, at], b_joint.at[way], peer))
    for copy in b_plains + b_joints:
        copy.wait_recv()
    me = at_b
    d_own[me, 0:width_half, :] = d_own[me, 0:width_half, :] + (b_joint[0] + b_plain[1])
    d_own[me, width_half:width, :] = d_own[me, width_half:width, :] + (b_plain[0] + b_joint[1])
    fetch[2].wait()
    gproto[...] = back(jnp.transpose(d_own[me]), own_proto[...])

    def rows_of(chunk, part=None):
        if part is None:
            return gproto_hbm.at[pl.ds(pl.multiple_of(chunk * 128, 128), 128)]
        return gproto_hbm.at[pl.ds(pl.multiple_of(chunk * 128 + part * 64, 64), 64)]

    def chunk_of(a, b):
        return core * 16 + a * 4 + b

    across = []

    def to_sibling(place, src=None):
        across.append(links.send(place if src is None else src, place, sibling))

    b_whole = [links.send(gproto, rows_of(mine), b_peer(1)), links.send(gproto, rows_of(mine), b_peer(3))]
    a_whole = {0: [links.send(gproto, rows_of(mine), a_peer(1)), links.send(gproto, rows_of(mine), a_peer(3))]}
    to_sibling(rows_of(mine), gproto)
    keep = pltpu.make_async_copy(gproto, rows_of(mine), local_sem.at[11])
    keep.start()

    for copy in z_plains + z_joints:
        copy.wait_recv()
    at = pl.ds(pl.multiple_of(z * seg_part, z_half), z_half)
    dunit[at, :] = dunit[at, :] + (z_joint[0] + z_plain[1])
    at = pl.ds(pl.multiple_of(z * seg_part + z_half, z_half), z_half)
    dunit[at, :] = dunit[at, :] + (z_plain[0] + z_joint[1])
    at = pl.ds(pl.multiple_of(z * seg_part, seg_part), seg_part)
    gview[...] = back(dunit[at, :], raw[at, :])
    place = gview_hbm.at[at]
    z_whole = [links.send(gview, place, z_peer(1)), links.send(gview, place, z_peer(3))]
    keep_view = pltpu.make_async_copy(gview, place, local_sem.at[12])
    keep_view.start()

    b_halves, a_halves = [], {}
    a_right, a_left, a_far = lax.rem(at_a + 1, 4), lax.rem(at_a + 3, 4), lax.rem(at_a + 2, 4)

    def along_a(key, place):
        a_whole[key] = a_whole.get(key, []) + [links.send(place, place, a_peer(1)), links.send(place, place, a_peer(3))]
        to_sibling(place)

    b_whole[0].wait_recv()
    b_halves.append(links.send(rows_of(chunk_of(at_a, b_left), 0), rows_of(chunk_of(at_a, b_left), 0), b_peer(1)))
    along_a(3, rows_of(chunk_of(at_a, b_left)))
    b_whole[1].wait_recv()
    b_halves.append(links.send(rows_of(chunk_of(at_a, b_right), 1), rows_of(chunk_of(at_a, b_right), 1), b_peer(3)))
    along_a(1, rows_of(chunk_of(at_a, b_right)))

    def pass_on(key, b):
        left, right = chunk_of(a_left, b), chunk_of(a_right, b)
        a_whole[key][0].wait_recv()
        a_halves[key] = [links.send(rows_of(left, 0), rows_of(left, 0), a_peer(1))]
        to_sibling(rows_of(left))
        a_whole[key][1].wait_recv()
        a_halves[key].append(links.send(rows_of(right, 1), rows_of(right, 1), a_peer(3)))
        to_sibling(rows_of(right))

    pass_on(0, at_b)
    far = chunk_of(at_a, b_far)
    b_halves[0].wait_recv()
    b_halves[1].wait_recv()
    along_a(2, rows_of(far))

    z_left_place = gview_hbm.at[pl.ds(pl.multiple_of(z_left * seg_part, seg_part), z_half)]
    z_right_place = gview_hbm.at[pl.ds(pl.multiple_of(z_right * seg_part + z_half, z_half), z_half)]
    z_whole[0].wait_recv()
    z_halves = [links.send(z_left_place, z_left_place, z_peer(1))]
    z_whole[1].wait_recv()
    z_halves.append(links.send(z_right_place, z_right_place, z_peer(3)))

    pass_on(3, b_left)
    pass_on(1, b_right)

    def far_halves(key, b):
        chunk = chunk_of(a_far, b)
        for way in range(2):
            a_halves[key][way].wait_recv()
            to_sibling(rows_of(chunk, way))

    far_halves(0, at_b)
    pass_on(2, b_far)
    far_halves(3, b_left)
    far_halves(1, b_right)
    far_halves(2, b_far)
    for copy in z_halves + across:
        copy.wait_recv()
    keep.wait()
    keep_view.wait()
    links.drain()


def balance(mesh, one, two, protos, pair):
    nx, ny, nz = mesh.shape["replica"], mesh.shape["batch"] // 2, mesh.shape["proto"]
    segs, width = one.shape
    count = protos.shape[0]
    both = 2 * segs
    z_half = both // nz // 2
    copies = ITERS * (nx * ny + nz + 1) + 80
    hbm = pl.BlockSpec(memory_space=pl.ANY)
    return pl.pallas_call(
        functools.partial(balance_kernel, nx, ny, nz),
        out_shape=(
            jax.ShapeDtypeStruct((both, width), F32),
            jax.ShapeDtypeStruct((count, width), F32),
        ),
        in_specs=[hbm, hbm, hbm, pl.BlockSpec(memory_space=pltpu.VMEM)],
        out_specs=(hbm, hbm),
        scratch_shapes=[
            pltpu.VMEM((both, width), BF16),
            pltpu.VMEM((both, count), F32),
            [pltpu.VMEM((both, count // 8), BF16)] * 8,
            pltpu.VMEM((both, width), BF16),
            pltpu.VMEM((width, both), BF16),
            pltpu.VMEM((segs, width), BF16),
            pltpu.VMEM((count, width), BF16),
            pltpu.VMEM((segs, segs), BF16),
            pltpu.VMEM((both, 128), F32),
            pltpu.VMEM((both, 128), F32),
            pltpu.VMEM((ITERS, 8, 8, 128), F32),
            pltpu.VMEM((ITERS, 4, 8, 128), F32),
            pltpu.VMEM((ITERS, nx * ny, 4, 8, 128), F32),
            pltpu.VMEM((ITERS, 8, 8, 128), F32),
            pltpu.VMEM((ITERS, 16, 128), F32),
            pltpu.VMEM((ITERS, nz, 16, 128), F32),
            pltpu.VMEM((16, 128), F32),
            pltpu.VMEM((both, 128), F32),
            pltpu.VMEM((both, 128), F32),
            [pltpu.VMEM((4, width, 128), F32)] * 8,
            pltpu.VMEM((4, 4, width, 128), F32),
            pltpu.VMEM((both, width), F32),
            pltpu.VMEM((128, width), BF16),
            pltpu.VMEM((128, width), F32),
            pltpu.VMEM((both // nz, width), F32),
        ]
        + [pltpu.VMEM((2, 2, width, 128), F32)] * 3
        + [pltpu.VMEM((2, width // 2, 128), F32)] * 3
        + [pltpu.VMEM((2, z_half, width), F32)] * 3
        + [
            pltpu.SemaphoreType.DMA((copies,)),
            pltpu.SemaphoreType.DMA((copies,)),
            pltpu.SemaphoreType.DMA((13,)),
        ],
        compiler_params=pltpu.CompilerParams(
            collective_id=0, has_side_effects=True, vmem_limit_bytes=62 << 20
        ),
        name="balance",
    )(one, two, protos, pair)


def hand_over_kernel(gview, gproto, one_out, two_out, proto_out, stage, sems):
    size = stage.shape[1]
    pairs = []
    for i in range(one_out.shape[0] // size):
        at = slice(i * size, (i + 1) * size)
        pairs.append((gview.at[at], one_out.at[at]))
        late = slice(one_out.shape[0] + i * size, one_out.shape[0] + (i + 1) * size)
        pairs.append((gview.at[late], two_out.at[at]))
    for i in range(proto_out.shape[0] // size):
        at = slice(i * size, (i + 1) * size)
        pairs.append((gproto.at[at], proto_out.at[at]))
    come = [pltpu.make_async_copy(src, stage.at[i], sems.at[0, i]) for i, (src, _) in enumerate(pairs)]
    go = [pltpu.make_async_copy(stage.at[i], dst, sems.at[1, i]) for i, (_, dst) in enumerate(pairs)]
    ahead = 4
    for copy in come[:ahead]:
        copy.start()
    for i, copy in enumerate(go):
        come[i].wait()
        copy.start()
        if i + ahead < len(come):
            come[i + ahead].start()
    for copy in go:
        copy.wait()


def hand_over(gview, gproto):
    segs, width = gview.shape[0] // 2, gview.shape[1]
    half = jax.ShapeDtypeStruct((segs, width), F32)
    size = segs // 2
    parts = (2 * segs + gproto.shape[0]) // size
    hbm = pl.BlockSpec(memory_space=pltpu.HBM)
    return pl.pallas_call(
        hand_over_kernel,
        out_shape=(half, half, jax.ShapeDtypeStruct(gproto.shape, F32)),
        in_specs=[hbm] * 2,
        out_specs=(hbm,) * 3,
        scratch_shapes=[pltpu.VMEM((parts, size, width), F32), pltpu.SemaphoreType.DMA((2, parts))],
        compiler_params=pltpu.CompilerParams(vmem_limit_bytes=62 << 20),
        name="hand_over",
    )(gview, gproto)


def per_device(mesh, view_one, view_two, prototypes, pairing):
    gview, gproto = balance(mesh, view_one, view_two, prototypes, pairing)
    return hand_over(gview, gproto)


def solution(mesh):
    rows = P(("batch", "replica"), None)
    protos = P("proto", None)
    return jax.shard_map(
        functools.partial(per_device, mesh),
        mesh=mesh,
        in_specs=(rows, rows, protos, rows),
        out_specs=(rows, rows, protos),
        check_vma=False,
    )
```

```python
import functools

import jax
import jax.numpy as jnp
from jax import lax
from jax.experimental import pallas as pl
from jax.experimental.pallas import tpu as pltpu
from jax.sharding import PartitionSpec as P

ITERS = 3
EPS = 1e-06
F32 = jnp.float32
BF16 = jnp.bfloat16
MESH = pl.DeviceIdType.MESH
NN = (((1,), (0,)), ((), ()))
NT = (((1,), (1,)), ((), ()))
TN = (((0,), (0,)), ((), ()))
LOG2E = 1.4426950408889634


def dot(a, b, dims):
    return lax.dot_general(a, b, dims, preferred_element_type=F32)


def here():
    batch = lax.axis_index("batch")
    return lax.div(batch, 2), lax.rem(batch, 2), lax.axis_index("replica"), lax.axis_index("proto")


class Links:
    def __init__(self, send_sem, recv_sem):
        self.send_sem, self.recv_sem, self.used, self.sent = send_sem, recv_sem, 0, []

    def send(self, src, dst, peer):
        copy = pltpu.make_async_remote_copy(
            src_ref=src, dst_ref=dst,
            send_sem=self.send_sem.at[self.used], recv_sem=self.recv_sem.at[self.used],
            device_id=peer, device_id_type=MESH,
        )
        copy.start()
        self.used += 1
        self.sent.append(copy)
        return copy

    def drain(self):
        for copy in self.sent:
            copy.wait_send()
        self.sent = []


def back(d, raw):
    xf = raw.astype(F32)
    inv = lax.rsqrt(jnp.sum(xf * xf, -1, keepdims=True) + EPS)
    u = xf * inv
    return inv * (d - u * jnp.sum(u * d, -1, keepdims=True))


def balance_kernel(
    nx, ny, nz,
    one_hbm, two_hbm, proto_hbm, pair_ref,
    gview_hbm, gproto_hbm, pair_out,
    raw, expo, dscore, low_seg, low_seg_t, low_proto, row_scale, prob_scale,
    cols, cols_in, plane_in, weight, rows, rows_in, tile_u,
    dproto, from_core, own_proto, gproto,
    a_relay, a_plain, a_joint, b_relay, b_plain, b_joint, z_relay, z_plain, z_joint,
    send_sem, recv_sem, local_sem,
):
    y, core, x, z = here()
    spot = y * nx + x
    links = Links(send_sem, recv_sem)
    at_a = core * y + (1 - core) * x
    at_b = core * x + (1 - core) * y
    mine = core * 16 + at_a * 4 + at_b

    def plane_peer(dx, dy):
        return (lax.rem(y + dy, ny) * 2 + core, lax.rem(x + dx, nx), z)

    def z_peer(step):
        return (y * 2 + core, x, lax.rem(z + step, nz))

    def a_peer(step):
        return (lax.rem(y + core * step, ny) * 2 + core, lax.rem(x + (1 - core) * step, nx), z)

    def b_peer(step):
        return (lax.rem(y + (1 - core) * step, ny) * 2 + core, lax.rem(x + core * step, nx), z)

    sibling = (y * 2 + 1 - core, x, z)

    segs = one_hbm.shape[0]
    protos, width = low_proto.shape
    both = 2 * segs
    pieces = 8
    piece = protos // pieces
    fetch = [
        pltpu.make_async_copy(one_hbm, raw.at[0:segs], local_sem.at[0]),
        pltpu.make_async_copy(two_hbm, low_seg.at[0:segs], local_sem.at[1]),
        pltpu.make_async_copy(proto_hbm.at[pl.ds(mine * 128, 128)], own_proto, local_sem.at[2]),
    ]
    fetch_protos = [
        pltpu.make_async_copy(
            proto_hbm.at[i * piece:(i + 1) * piece], low_proto.at[i * piece:(i + 1) * piece], local_sem.at[3 + i]
        )
        for i in range(pieces)
    ]
    for copy in fetch + fetch_protos:
        copy.start()
    def hops(step):
        return min(step[0], nx - step[0]) + min(step[1], ny - step[1])

    steps = sorted([(dx, dy) for dx in range(nx) for dy in range(ny)][1:], key=hops, reverse=True)
    peers = [plane_peer(*p) for p in steps] + [z_peer(s) for s in range(1, nz)] + [sibling]
    barrier = pltpu.get_barrier_semaphore()
    for peer in peers:
        pl.semaphore_signal(barrier, inc=1, device_id=peer, device_id_type=MESH)

    def unit(block):
        xf = block.astype(F32)
        inv = lax.rsqrt(jnp.sum(xf * xf, -1, keepdims=True) + EPS)
        return (xf * inv).astype(BF16)

    def norm_views(i, carry):
        at = pl.ds(pl.multiple_of(i * 128, 128), 128)
        low_seg[at, :] = unit(raw[at, :])
        return carry

    fetch[0].wait()
    fetch[1].wait()
    pair_out[...] = pair_ref[...]
    pair = jnp.broadcast_to(pair_ref[...], (segs, segs))
    number = lax.broadcasted_iota(jnp.int32, (segs, segs), 0)
    onehot = dscore[0].at[0:segs]
    onehot[...] = jnp.where(pair == number, 1.0, 0.0).astype(BF16)
    raw[segs:both, :] = dot(onehot[...], low_seg[0:segs, :], TN).astype(BF16)
    lax.fori_loop(0, both // 128, norm_views, 0, unroll=2)

    def norm_protos(i, carry):
        at = pl.ds(pl.multiple_of(i * 128, 128), 128)
        low_proto[at, :] = unit(low_proto[at, :])
        return carry

    for i, copy in enumerate(fetch_protos):
        copy.wait()
        lax.fori_loop(i * piece // 128, (i + 1) * piece // 128, norm_protos, 0, unroll=4)

    wide = protos // 4

    def scores(j, carry):
        for q in range(wide // 256):
            at = pl.ds(pl.multiple_of(j * wide + q * 256, 256), 256)
            s = dot(low_seg[...], low_proto[at, :], NT)
            e = jnp.exp2(s * (10.0 * LOG2E))
            expo[:, at] = e
            k = e * e
            for view in range(2):
                total = jnp.sum(k[view * segs:(view + 1) * segs], axis=0, keepdims=True)
                for h in range(2):
                    cols[0, view * 4 + j, q * 2 + h:q * 2 + h + 1, :] = total[:, h * 128:(h + 1) * 128]
        return carry

    lax.fori_loop(0, 4, scores, 0)

    def col_sums(it, view):
        def block(j, carry):
            k = view * 4 + j
            first = pl.multiple_of(lax.div(k, 4) * segs, segs)
            left = lax.rem(k, 4) * wide

            def some(r, acc):
                acc = list(acc)
                at = pl.ds(pl.multiple_of(first + r * 128, 128), 128)
                scale = row_scale.at[at]
                tiles = expo.at[at, pl.ds(pl.multiple_of(left, 128), wide)]
                for t in range(16):
                    u = scale[t * 8:(t + 1) * 8, :]
                    for l in range(wide // 128):
                        e = tiles[t * 8:(t + 1) * 8, l * 128:(l + 1) * 128]
                        n = (t % 2) * (wide // 128) + l
                        acc[n] = acc[n] + (e * e) * u
                return tuple(acc)

            zero = jnp.zeros((8, 128), F32)
            acc = lax.fori_loop(0, segs // 128, some, (zero,) * (wide // 64))
            acc = [acc[l] + acc[wide // 128 + l] for l in range(wide // 128)]
            for l in range(wide // 128):
                cols[it, k, l:l + 1, :] = jnp.sum(acc[l], axis=0, keepdims=True)
            return carry

        lax.fori_loop(0, 4, block, 0)

    def turn_segs():
        for i in range(both // 128):
            block = low_seg[i * 128:(i + 1) * 128, :].astype(F32)
            low_seg_t[:, i * 128:(i + 1) * 128] = jnp.transpose(block).astype(BF16)

    def tiles_of(k):
        return pl.ds(pl.multiple_of(k * 4, 4), 4)

    def swap_cols(it):
        return links.send(cols.at[it, tiles_of(1 - core)], cols_in.at[it], sibling)

    def all_cols(it, swap):
        swap.wait_recv()
        plane_in[it, spot] = cols[it, tiles_of(core)] + cols_in[it]
        copies = [
            links.send(plane_in.at[it, spot], plane_in.at[it, spot], plane_peer(*p)) for p in steps
        ]
        if it == 0:
            turn_segs()
        for copy in copies:
            copy.wait_recv()
        total = plane_in[it, 0]
        for k in range(1, nx * ny):
            total = total + plane_in[it, k]
        weight[it, tiles_of(core)] = 1.0 / total
        return links.send(weight.at[it, tiles_of(core)], weight.at[it, tiles_of(core)], sibling)

    spare = dproto[7]

    def row_sums(it, with_total, view):
        def block(b, carry):
            at = pl.ds(pl.multiple_of(view * segs + b * 64, 64), 64)
            acc = jnp.zeros((64, 128), F32)
            tot = jnp.zeros((64, 128), F32)
            tiles = expo.at[at]
            scale = weight.at[it, pl.ds(view * 4, 4)]
            for l in range(protos // 128):
                e = tiles[:, l * 128:(l + 1) * 128]
                v = scale[l // 8, l % 8:l % 8 + 1, :]
                acc = acc + (e * e) * v
                if with_total:
                    tot = tot + e
            spare[view, pl.ds(pl.multiple_of(b * 64, 64), 64), :] = acc
            if with_total:
                spare[2 + view, pl.ds(pl.multiple_of(b * 64, 64), 64), :] = tot
            return carry

        lax.fori_loop(0, segs // 64, block, 0)

    def turn_sums(it, with_total):
        for b in range(both // 128):
            view, at = b // 4, slice(b % 4 * 128, (b % 4 + 1) * 128)
            rows[it, b:b + 1, :] = jnp.sum(jnp.transpose(spare[view, at, :]), axis=0, keepdims=True)
            if with_total:
                tot = jnp.sum(jnp.transpose(spare[2 + view, at, :]), axis=0, keepdims=True)
                rows[it, 8 + b:9 + b, :] = tot

    def spread(out, row):
        for b in range(both // 128):
            wide_row = jnp.broadcast_to(tile_u[row + b:row + b + 1, :], (128, 128))
            out[b * 128:(b + 1) * 128, :] = jnp.transpose(wide_row)

    def all_rows(it, with_total, scale):
        size = 16 if with_total else 8
        rows_in[it, z] = rows[it]
        copies = []
        for s in range(1, nz):
            copies.append(links.send(rows.at[it, 0:size], rows_in.at[it, z, 0:size], z_peer(s)))
        for copy in copies:
            copy.wait_recv()
        total = rows_in[it, 0, 0:size]
        for k in range(1, nz):
            total = total + rows_in[it, k, 0:size]
        tile_u[0:8, :] = scale / total[0:8]
        spread(row_scale, 0)
        if with_total:
            tile_u[8:16, :] = 5.0 / total[8:16]
            spread(prob_scale, 8)

    pl.semaphore_wait(barrier, len(peers))
    for it in range(ITERS):
        if it:
            col_sums(it, 1 - core)
            swap = swap_cols(it)
            col_sums(it, core)
        else:
            swap = swap_cols(it)
        back_copy = all_cols(it, swap)
        row_sums(it, it == 0, core)
        back_copy.wait_recv()
        row_sums(it, it == 0, 1 - core)
        turn_sums(it, it == 0)
        all_rows(it, it == 0, 5.0 if it == ITERS - 1 else 1.0)

    last = ITERS - 1

    half_b = 256

    def elements(ds, chunk, j):
        tiles = expo.at[:, pl.ds(pl.multiple_of(chunk * 128 + j * half_b, half_b), half_b)]
        to = ds.at[:, pl.ds(pl.multiple_of(j * half_b, half_b), half_b)]
        tile = lax.div(chunk, 8)
        row = lax.rem(chunk, 8) + j * 2
        v_one = [weight[last, tile, pl.ds(row + h, 1), :] for h in range(2)]
        v_two = [weight[last, 4 + tile, pl.ds(row + h, 1), :] for h in range(2)]
        for b in range(segs // 32):
            first = slice(b * 32, (b + 1) * 32)
            second = slice(segs + b * 32, segs + (b + 1) * 32)
            u_one, u_two = row_scale[first, :], row_scale[second, :]
            p_one, p_two = prob_scale[first, :], prob_scale[second, :]
            for h in range(2):
                at = slice(h * 128, (h + 1) * 128)
                e_one = tiles[first, at]
                e_two = tiles[second, at]
                t_one = (e_two * e_two) * u_two * v_two[h]
                t_two = (e_one * e_one) * u_one * v_one[h]
                to[first, at] = (e_one * p_one - t_one).astype(BF16)
                to[second, at] = (e_two * p_two - t_two).astype(BF16)

    def step(new, old):
        def both_parts(j, carry):
            if old is not None:
                at = pl.ds(pl.multiple_of(j * half_b, half_b), half_b)
                part = dot(low_seg_t[...], dscore[old][:, at], NN)
                dproto[old][2 * j] = part[:, 0:128]
                dproto[old][2 * j + 1] = part[:, 128:256]
            if new is not None:
                elements(dscore[new], chunks[new], j)
            return carry

        lax.fori_loop(0, 2, both_parts, 0)

    order = (2, 1, 3, 0)
    chunks, spots = [], []
    for t in order:
        for half, place in ((1 - core, at_b), (core, at_a)):
            spots.append(lax.rem(place + t, 4))
            chunks.append(half * 16 + spots[-1] * 4)
    relays, plains, joints = [None] * 2, [None] * 2, [None] * 2
    crossing = [None] * 8
    step(0, None)
    for g in range(8):
        step(g + 1 if g < 7 else None, g)
        if g % 2 == 0:
            crossing[g] = links.send(dproto[g], from_core.at[g // 2], sibling)
            continue
        crossing[g - 1].wait_recv()
        for q in range(4):
            dproto[g][q] = dproto[g][q] + from_core[g // 2, q]
        low, high = dproto[g].at[0:2], dproto[g].at[2:4]
        t = order[g // 2]
        if t == 2:
            relays = [links.send(low, a_relay.at[0], a_peer(1)), links.send(high, a_relay.at[1], a_peer(3))]
        if t == 1:
            plains[0] = links.send(high, a_plain.at[0], a_peer(1))
        if t == 3:
            plains[1] = links.send(low, a_plain.at[1], a_peer(3))
    d_right, d_left, d_own = dproto[3], dproto[5], dproto[7]

    dunit = expo.at[:, 0:width]
    seg_part = both // nz
    z_half = seg_part // 2
    z_right, z_left, z_far = lax.rem(z + 1, 4), lax.rem(z + 3, 4), lax.rem(z + 2, 4)

    def views(k):
        at = pl.ds(pl.multiple_of(k * seg_part, seg_part), seg_part)
        total = None
        for g in range(8):
            rows_g = low_proto[pl.ds(pl.multiple_of(chunks[g] * 128, 512), 512), :]
            term = dot(dscore[g][at, :], rows_g, NN)
            total = term if total is None else total + term
        dunit[at, :] = total

    def part(ref, k, lower):
        start = k * seg_part + (0 if lower else z_half)
        return ref.at[pl.ds(pl.multiple_of(start, z_half), z_half)]

    views(z_far)
    z_relays = [
        links.send(part(dunit, z_far, True), z_relay.at[0], z_peer(1)),
        links.send(part(dunit, z_far, False), z_relay.at[1], z_peer(3)),
    ]
    views(z_right)
    z_plains = [links.send(part(dunit, z_right, False), z_plain.at[0], z_peer(1))]
    relays[0].wait_recv()
    for q in range(2):
        d_right[q] = d_right[q] + a_relay[0, q]
    joints[0] = links.send(d_right.at[0:2], a_joint.at[0], a_peer(1))
    relays[1].wait_recv()
    for q in range(2):
        d_left[2 + q] = d_left[2 + q] + a_relay[1, q]
    joints[1] = links.send(d_left.at[2:4], a_joint.at[1], a_peer(3))

    views(z_left)
    z_plains.append(links.send(part(dunit, z_left, True), z_plain.at[1], z_peer(3)))
    views(z)

    for copy in plains + joints:
        copy.wait_recv()
    for q in range(2):
        d_own[q] = d_own[q] + (a_joint[0, q] + a_plain[1, q])
        d_own[2 + q] = d_own[2 + q] + (a_plain[0, q] + a_joint[1, q])
    b_right, b_left, b_far = lax.rem(at_b + 1, 4), lax.rem(at_b + 3, 4), lax.rem(at_b + 2, 4)
    width_half = width // 2
    b_relays = [
        links.send(d_own.at[b_far, 0:width_half], b_relay.at[0], b_peer(1)),
        links.send(d_own.at[b_far, width_half:width], b_relay.at[1], b_peer(3)),
    ]
    b_plains = [
        links.send(d_own.at[b_right, width_half:width], b_plain.at[0], b_peer(1)),
        links.send(d_own.at[b_left, 0:width_half], b_plain.at[1], b_peer(3)),
    ]

    z_joints = []
    for way, k, skip, peer in ((0, z_right, 0, z_peer(1)), (1, z_left, z_half, z_peer(3))):
        z_relays[way].wait_recv()
        at = pl.ds(pl.multiple_of(k * seg_part + skip, z_half), z_half)
        dunit[at, :] = dunit[at, :] + z_relay[way]
        z_joints.append(links.send(dunit.at[at], z_joint.at[way], peer))

    b_joints = []
    for way, k, skip, peer in ((0, b_right, 0, b_peer(1)), (1, b_left, width_half, b_peer(3))):
        b_relays[way].wait_recv()
        at = slice(skip, skip + width_half)
        d_own[k, at, :] = d_own[k, at, :] + b_relay[way]
        b_joints.append(links.send(d_own.at[k, at], b_joint.at[way], peer))
    for copy in b_plains + b_joints:
        copy.wait_recv()
    me = at_b
    d_own[me, 0:width_half, :] = d_own[me, 0:width_half, :] + (b_joint[0] + b_plain[1])
    d_own[me, width_half:width, :] = d_own[me, width_half:width, :] + (b_plain[0] + b_joint[1])
    fetch[2].wait()
    gproto[...] = back(jnp.transpose(d_own[me]), own_proto[...])

    def rows_of(chunk, part=None):
        if part is None:
            return gproto_hbm.at[pl.ds(pl.multiple_of(chunk * 128, 128), 128)]
        return gproto_hbm.at[pl.ds(pl.multiple_of(chunk * 128 + part * 64, 64), 64)]

    def chunk_of(a, b):
        return core * 16 + a * 4 + b

    across = []

    def to_sibling(place, src=None):
        across.append(links.send(place if src is None else src, place, sibling))

    b_whole = [links.send(gproto, rows_of(mine), b_peer(1)), links.send(gproto, rows_of(mine), b_peer(3))]
    a_whole = {0: [links.send(gproto, rows_of(mine), a_peer(1)), links.send(gproto, rows_of(mine), a_peer(3))]}
    to_sibling(rows_of(mine), gproto)
    keep = pltpu.make_async_copy(gproto, rows_of(mine), local_sem.at[11])
    keep.start()

    for copy in z_plains + z_joints:
        copy.wait_recv()
    at = pl.ds(pl.multiple_of(z * seg_part, z_half), z_half)
    dunit[at, :] = dunit[at, :] + (z_joint[0] + z_plain[1])
    at = pl.ds(pl.multiple_of(z * seg_part + z_half, z_half), z_half)
    dunit[at, :] = dunit[at, :] + (z_plain[0] + z_joint[1])
    at = pl.ds(pl.multiple_of(z * seg_part, seg_part), seg_part)
    dunit[at, :] = back(dunit[at, :], raw[at, :])
    gview, place = dunit.at[at], gview_hbm.at[at]
    z_whole = [links.send(gview, place, z_peer(1)), links.send(gview, place, z_peer(3))]
    keep_view = pltpu.make_async_copy(gview, place, local_sem.at[12])
    keep_view.start()

    b_halves, a_halves = [], {}
    a_right, a_left, a_far = lax.rem(at_a + 1, 4), lax.rem(at_a + 3, 4), lax.rem(at_a + 2, 4)

    def along_a(key, place):
        a_whole[key] = a_whole.get(key, []) + [links.send(place, place, a_peer(1)), links.send(place, place, a_peer(3))]
        to_sibling(place)

    b_whole[0].wait_recv()
    b_halves.append(links.send(rows_of(chunk_of(at_a, b_left), 0), rows_of(chunk_of(at_a, b_left), 0), b_peer(1)))
    along_a(3, rows_of(chunk_of(at_a, b_left)))
    b_whole[1].wait_recv()
    b_halves.append(links.send(rows_of(chunk_of(at_a, b_right), 1), rows_of(chunk_of(at_a, b_right), 1), b_peer(3)))
    along_a(1, rows_of(chunk_of(at_a, b_right)))

    def pass_on(key, b):
        left, right = chunk_of(a_left, b), chunk_of(a_right, b)
        a_whole[key][0].wait_recv()
        a_halves[key] = [links.send(rows_of(left, 0), rows_of(left, 0), a_peer(1))]
        to_sibling(rows_of(left))
        a_whole[key][1].wait_recv()
        a_halves[key].append(links.send(rows_of(right, 1), rows_of(right, 1), a_peer(3)))
        to_sibling(rows_of(right))

    pass_on(0, at_b)
    far = chunk_of(at_a, b_far)
    b_halves[0].wait_recv()
    b_halves[1].wait_recv()
    along_a(2, rows_of(far))

    z_left_place = gview_hbm.at[pl.ds(pl.multiple_of(z_left * seg_part, seg_part), z_half)]
    z_right_place = gview_hbm.at[pl.ds(pl.multiple_of(z_right * seg_part + z_half, z_half), z_half)]
    z_whole[0].wait_recv()
    z_halves = [links.send(z_left_place, z_left_place, z_peer(1))]
    z_whole[1].wait_recv()
    z_halves.append(links.send(z_right_place, z_right_place, z_peer(3)))

    pass_on(3, b_left)
    pass_on(1, b_right)

    def far_halves(key, b):
        chunk = chunk_of(a_far, b)
        for way in range(2):
            a_halves[key][way].wait_recv()
            to_sibling(rows_of(chunk, way))

    far_halves(0, at_b)
    pass_on(2, b_far)
    far_halves(3, b_left)
    far_halves(1, b_right)
    far_halves(2, b_far)
    for copy in z_halves + across:
        copy.wait_recv()
    keep.wait()
    keep_view.wait()
    links.drain()


def balance(mesh, one, two, protos, pair):
    nx, ny, nz = mesh.shape["replica"], mesh.shape["batch"] // 2, mesh.shape["proto"]
    segs, width = one.shape
    count = protos.shape[0]
    both = 2 * segs
    z_half = both // nz // 2
    copies = ITERS * (nx * ny + nz + 1) + 80
    vmem, hbm = pl.BlockSpec(memory_space=pltpu.VMEM), pl.BlockSpec(memory_space=pl.ANY)
    return pl.pallas_call(
        functools.partial(balance_kernel, nx, ny, nz),
        out_shape=(
            pltpu.VMEM((both, width), F32),
            pltpu.VMEM((count, width), F32),
            pltpu.VMEM(pair.shape, jnp.int32),
        ),
        in_specs=[hbm, hbm, hbm, vmem],
        out_specs=(hbm, hbm, vmem),
        scratch_shapes=[
            pltpu.VMEM((both, width), BF16),
            pltpu.VMEM((both, count), F32),
            [pltpu.VMEM((both, count // 8), BF16)] * 8,
            pltpu.VMEM((both, width), BF16),
            pltpu.VMEM((width, both), BF16),
            pltpu.VMEM((count, width), BF16),
            pltpu.VMEM((both, 128), F32),
            pltpu.VMEM((both, 128), F32),
            pltpu.VMEM((ITERS, 8, 8, 128), F32),
            pltpu.VMEM((ITERS, 4, 8, 128), F32),
            pltpu.VMEM((ITERS, nx * ny, 4, 8, 128), F32),
            pltpu.VMEM((ITERS, 8, 8, 128), F32),
            pltpu.VMEM((ITERS, 16, 128), F32),
            pltpu.VMEM((ITERS, nz, 16, 128), F32),
            pltpu.VMEM((16, 128), F32),
            [pltpu.VMEM((4, width, 128), F32)] * 8,
            pltpu.VMEM((4, 4, width, 128), F32),
            pltpu.VMEM((128, width), BF16),
            pltpu.VMEM((128, width), F32),
        ]
        + [pltpu.VMEM((2, 2, width, 128), F32)] * 3
        + [pltpu.VMEM((2, width // 2, 128), F32)] * 3
        + [pltpu.VMEM((2, z_half, width), F32)] * 3
        + [
            pltpu.SemaphoreType.DMA((copies,)),
            pltpu.SemaphoreType.DMA((copies,)),
            pltpu.SemaphoreType.DMA((13,)),
        ],
        compiler_params=pltpu.CompilerParams(
            collective_id=0, has_side_effects=True, vmem_limit_bytes=53 << 20
        ),
        name="balance",
    )(one, two, protos, pair)


def hand_over_kernel(gview, gproto, pair_ref, one_out, two_out, proto_out, two, sems):
    segs = one_out.shape[0]
    parts = 8
    size = proto_out.shape[0] // parts
    copies = [pltpu.make_async_copy(gview.at[0:segs], one_out, sems.at[parts])]
    for i in range(parts):
        at = slice(i * size, (i + 1) * size)
        copies.append(pltpu.make_async_copy(gproto.at[at], proto_out.at[at], sems.at[i]))
    for copy in copies:
        copy.start()
    pair = jnp.broadcast_to(pair_ref[...], (segs, segs))
    number = lax.broadcasted_iota(jnp.int32, (segs, segs), 0)
    onehot = jnp.where(pair == number, 1.0, 0.0).astype(BF16)
    d = gview[segs:2 * segs, :]
    top = d.astype(BF16)
    rest = d - top.astype(F32)
    middle = rest.astype(BF16)
    end = (rest - middle.astype(F32)).astype(BF16)
    two[...] = dot(onehot, top, NN) + (dot(onehot, middle, NN) + dot(onehot, end, NN))
    copies.append(pltpu.make_async_copy(two, two_out, sems.at[parts + 1]))
    copies[-1].start()
    for copy in copies:
        copy.wait()


def hand_over(gview, gproto, pairing):
    segs, width = gview.shape[0] // 2, gview.shape[1]
    half = jax.ShapeDtypeStruct((segs, width), F32)
    vmem, hbm = pl.BlockSpec(memory_space=pltpu.VMEM), pl.BlockSpec(memory_space=pl.ANY)
    return pl.pallas_call(
        hand_over_kernel,
        out_shape=(half, half, jax.ShapeDtypeStruct(gproto.shape, F32)),
        in_specs=[vmem, hbm, vmem],
        out_specs=(hbm,) * 3,
        scratch_shapes=[
            pltpu.VMEM((segs, width), F32),
            pltpu.SemaphoreType.DMA((10,)),
        ],
        compiler_params=pltpu.CompilerParams(vmem_limit_bytes=10 << 20),
        name="hand_over",
    )(gview, gproto, pairing)


def per_device(mesh, view_one, view_two, prototypes, pairing):
    return hand_over(*balance(mesh, view_one, view_two, prototypes, pairing))


def solution(mesh):
    rows = P(("batch", "replica"), None)
    protos = P("proto", None)
    return jax.shard_map(
        functools.partial(per_device, mesh),
        mesh=mesh,
        in_specs=(rows, rows, protos, rows),
        out_specs=(rows, rows, protos),
        check_vma=False,
    )
```

```python
import functools

import jax
import jax.numpy as jnp
from jax import lax
from jax.experimental import pallas as pl
from jax.experimental.pallas import tpu as pltpu
from jax.sharding import PartitionSpec as P

ITERS = 3
EPS = 1e-06
F32 = jnp.float32
BF16 = jnp.bfloat16
MESH = pl.DeviceIdType.MESH
NN = (((1,), (0,)), ((), ()))
NT = (((1,), (1,)), ((), ()))
TN = (((0,), (0,)), ((), ()))
LOG2E = 1.4426950408889634


def dot(a, b, dims):
    return lax.dot_general(a, b, dims, preferred_element_type=F32)


def here():
    batch = lax.axis_index("batch")
    return lax.div(batch, 2), lax.rem(batch, 2), lax.axis_index("replica"), lax.axis_index("proto")


class Links:
    def __init__(self, send_sem, recv_sem):
        self.send_sem, self.recv_sem, self.used, self.sent = send_sem, recv_sem, 0, []

    def send(self, src, dst, peer):
        copy = pltpu.make_async_remote_copy(
            src_ref=src, dst_ref=dst,
            send_sem=self.send_sem.at[self.used], recv_sem=self.recv_sem.at[self.used],
            device_id=peer, device_id_type=MESH,
        )
        copy.start()
        self.used += 1
        self.sent.append(copy)
        return copy

    def drain(self):
        for copy in self.sent:
            copy.wait_send()
        self.sent = []


def back(d, raw):
    xf = raw.astype(F32)
    inv = lax.rsqrt(jnp.sum(xf * xf, -1, keepdims=True) + EPS)
    u = xf * inv
    return inv * (d - u * jnp.sum(u * d, -1, keepdims=True))


def balance_kernel(
    nx, ny, nz,
    one_hbm, two_hbm, proto_hbm, pair_ref,
    gview_hbm, gproto_hbm, pair_out,
    raw, expo, dscore, low_seg, low_seg_t, low_proto, row_scale, prob_scale,
    cols, cols_in, plane_in, weight, rows, rows_in, tile_u,
    dproto, from_core, own_proto, gproto,
    a_relay, a_plain, a_joint, b_relay, b_plain, b_joint, z_relay, z_plain, z_joint,
    send_sem, recv_sem, local_sem,
):
    y, core, x, z = here()
    spot = y * nx + x
    links = Links(send_sem, recv_sem)
    at_a = core * y + (1 - core) * x
    at_b = core * x + (1 - core) * y
    mine = core * 16 + at_a * 4 + at_b

    def plane_peer(dx, dy):
        return (lax.rem(y + dy, ny) * 2 + core, lax.rem(x + dx, nx), z)

    def z_peer(step):
        return (y * 2 + core, x, lax.rem(z + step, nz))

    def a_peer(step):
        return (lax.rem(y + core * step, ny) * 2 + core, lax.rem(x + (1 - core) * step, nx), z)

    def b_peer(step):
        return (lax.rem(y + (1 - core) * step, ny) * 2 + core, lax.rem(x + core * step, nx), z)

    sibling = (y * 2 + 1 - core, x, z)

    segs = one_hbm.shape[0]
    protos, width = low_proto.shape
    both = 2 * segs
    pieces = 8
    piece = protos // pieces
    fetch = [
        pltpu.make_async_copy(one_hbm, raw.at[0:segs], local_sem.at[0]),
        pltpu.make_async_copy(two_hbm, low_seg.at[0:segs], local_sem.at[1]),
        pltpu.make_async_copy(proto_hbm.at[pl.ds(mine * 128, 128)], own_proto, local_sem.at[2]),
    ]
    fetch_protos = [
        pltpu.make_async_copy(
            proto_hbm.at[i * piece:(i + 1) * piece], low_proto.at[i * piece:(i + 1) * piece], local_sem.at[3 + i]
        )
        for i in range(pieces)
    ]
    for copy in fetch + fetch_protos:
        copy.start()
    def hops(step):
        return min(step[0], nx - step[0]) + min(step[1], ny - step[1])

    steps = sorted([(dx, dy) for dx in range(nx) for dy in range(ny)][1:], key=hops, reverse=True)
    peers = [plane_peer(*p) for p in steps] + [z_peer(s) for s in range(1, nz)] + [sibling]
    barrier = pltpu.get_barrier_semaphore()
    for peer in peers:
        pl.semaphore_signal(barrier, inc=1, device_id=peer, device_id_type=MESH)

    def unit(block):
        xf = block.astype(F32)
        inv = lax.rsqrt(jnp.sum(xf * xf, -1, keepdims=True) + EPS)
        return (xf * inv).astype(BF16)

    def norm_views(i, carry):
        at = pl.ds(pl.multiple_of(i * 128, 128), 128)
        low_seg[at, :] = unit(raw[at, :])
        return carry

    fetch[0].wait()
    fetch[1].wait()
    pair_out[...] = pair_ref[...]
    pair = jnp.broadcast_to(pair_ref[...], (segs, segs))
    number = lax.broadcasted_iota(jnp.int32, (segs, segs), 0)
    onehot = dscore[0].at[0:segs]
    onehot[...] = jnp.where(pair == number, 1.0, 0.0).astype(BF16)
    raw[segs:both, :] = dot(onehot[...], low_seg[0:segs, :], TN).astype(BF16)
    lax.fori_loop(0, both // 128, norm_views, 0, unroll=2)

    def norm_protos(i, carry):
        at = pl.ds(pl.multiple_of(i * 128, 128), 128)
        low_proto[at, :] = unit(low_proto[at, :])
        return carry

    for i, copy in enumerate(fetch_protos):
        copy.wait()
        lax.fori_loop(i * piece // 128, (i + 1) * piece // 128, norm_protos, 0, unroll=4)

    wide = protos // 4

    def scores(j, carry):
        for q in range(wide // 256):
            at = pl.ds(pl.multiple_of(j * wide + q * 256, 256), 256)
            s = dot(low_seg[...], low_proto[at, :], NT)
            e = jnp.exp2(s * (10.0 * LOG2E))
            expo[:, at] = e
            k = e * e
            for view in range(2):
                total = jnp.sum(k[view * segs:(view + 1) * segs], axis=0, keepdims=True)
                for h in range(2):
                    cols[0, view * 4 + j, q * 2 + h:q * 2 + h + 1, :] = total[:, h * 128:(h + 1) * 128]
        return carry

    lax.fori_loop(0, 4, scores, 0)

    def col_sums(it, view):
        def block(j, carry):
            k = view * 4 + j
            first = pl.multiple_of(lax.div(k, 4) * segs, segs)
            left = lax.rem(k, 4) * wide

            def some(r, acc):
                acc = list(acc)
                at = pl.ds(pl.multiple_of(first + r * 128, 128), 128)
                scale = row_scale.at[at]
                tiles = expo.at[at, pl.ds(pl.multiple_of(left, 128), wide)]
                for t in range(16):
                    u = scale[t * 8:(t + 1) * 8, :]
                    for l in range(wide // 128):
                        e = tiles[t * 8:(t + 1) * 8, l * 128:(l + 1) * 128]
                        n = (t % 2) * (wide // 128) + l
                        acc[n] = acc[n] + (e * e) * u
                return tuple(acc)

            zero = jnp.zeros((8, 128), F32)
            acc = lax.fori_loop(0, segs // 128, some, (zero,) * (wide // 64))
            acc = [acc[l] + acc[wide // 128 + l] for l in range(wide // 128)]
            for l in range(wide // 128):
                cols[it, k, l:l + 1, :] = jnp.sum(acc[l], axis=0, keepdims=True)
            return carry

        lax.fori_loop(0, 4, block, 0)

    def turn_segs():
        for i in range(both // 128):
            block = low_seg[i * 128:(i + 1) * 128, :].astype(F32)
            low_seg_t[:, i * 128:(i + 1) * 128] = jnp.transpose(block).astype(BF16)

    def tiles_of(k):
        return pl.ds(pl.multiple_of(k * 4, 4), 4)

    def swap_cols(it):
        return links.send(cols.at[it, tiles_of(1 - core)], cols_in.at[it], sibling)

    def all_cols(it, swap):
        swap.wait_recv()
        plane_in[it, spot] = cols[it, tiles_of(core)] + cols_in[it]
        copies = [
            links.send(plane_in.at[it, spot], plane_in.at[it, spot], plane_peer(*p)) for p in steps
        ]
        if it == 0:
            turn_segs()
        for copy in copies:
            copy.wait_recv()
        total = plane_in[it, 0]
        for k in range(1, nx * ny):
            total = total + plane_in[it, k]
        weight[it, tiles_of(core)] = 1.0 / total
        return links.send(weight.at[it, tiles_of(core)], weight.at[it, tiles_of(core)], sibling)

    spare = dproto[7]

    def row_sums(it, with_total, view):
        def block(b, carry):
            at = pl.ds(pl.multiple_of(view * segs + b * 64, 64), 64)
            acc = jnp.zeros((64, 128), F32)
            tot = jnp.zeros((64, 128), F32)
            tiles = expo.at[at]
            scale = weight.at[it, pl.ds(view * 4, 4)]
            for l in range(protos // 128):
                e = tiles[:, l * 128:(l + 1) * 128]
                v = scale[l // 8, l % 8:l % 8 + 1, :]
                acc = acc + (e * e) * v
                if with_total:
                    tot = tot + e
            spare[view, pl.ds(pl.multiple_of(b * 64, 64), 64), :] = acc
            if with_total:
                spare[2 + view, pl.ds(pl.multiple_of(b * 64, 64), 64), :] = tot
            return carry

        lax.fori_loop(0, segs // 64, block, 0)

    def turn_sums(it, with_total):
        for b in range(both // 128):
            view, at = b // 4, slice(b % 4 * 128, (b % 4 + 1) * 128)
            rows[it, b:b + 1, :] = jnp.sum(jnp.transpose(spare[view, at, :]), axis=0, keepdims=True)
            if with_total:
                tot = jnp.sum(jnp.transpose(spare[2 + view, at, :]), axis=0, keepdims=True)
                rows[it, 8 + b:9 + b, :] = tot

    def spread(out, row):
        for b in range(both // 128):
            wide_row = jnp.broadcast_to(tile_u[row + b:row + b + 1, :], (128, 128))
            out[b * 128:(b + 1) * 128, :] = jnp.transpose(wide_row)

    def all_rows(it, with_total, scale):
        size = 16 if with_total else 8
        rows_in[it, z] = rows[it]
        copies = []
        for s in range(1, nz):
            copies.append(links.send(rows.at[it, 0:size], rows_in.at[it, z, 0:size], z_peer(s)))
        for copy in copies:
            copy.wait_recv()
        total = rows_in[it, 0, 0:size]
        for k in range(1, nz):
            total = total + rows_in[it, k, 0:size]
        tile_u[0:8, :] = scale / total[0:8]
        spread(row_scale, 0)
        if with_total:
            tile_u[8:16, :] = 5.0 / total[8:16]
            spread(prob_scale, 8)

    pl.semaphore_wait(barrier, len(peers))
    for it in range(ITERS):
        if it:
            col_sums(it, 1 - core)
            swap = swap_cols(it)
            col_sums(it, core)
        else:
            swap = swap_cols(it)
        back_copy = all_cols(it, swap)
        row_sums(it, it == 0, core)
        back_copy.wait_recv()
        row_sums(it, it == 0, 1 - core)
        turn_sums(it, it == 0)
        all_rows(it, it == 0, 5.0 if it == ITERS - 1 else 1.0)

    last = ITERS - 1

    half_b = 256

    def elements(ds, chunk, j):
        tiles = expo.at[:, pl.ds(pl.multiple_of(chunk * 128 + j * half_b, half_b), half_b)]
        to = ds.at[:, pl.ds(pl.multiple_of(j * half_b, half_b), half_b)]
        tile = lax.div(chunk, 8)
        row = lax.rem(chunk, 8) + j * 2
        v_one = [weight[last, tile, pl.ds(row + h, 1), :] for h in range(2)]
        v_two = [weight[last, 4 + tile, pl.ds(row + h, 1), :] for h in range(2)]
        for b in range(segs // 32):
            first = slice(b * 32, (b + 1) * 32)
            second = slice(segs + b * 32, segs + (b + 1) * 32)
            u_one, u_two = row_scale[first, :], row_scale[second, :]
            p_one, p_two = prob_scale[first, :], prob_scale[second, :]
            for h in range(2):
                at = slice(h * 128, (h + 1) * 128)
                e_one = tiles[first, at]
                e_two = tiles[second, at]
                t_one = (e_two * e_two) * u_two * v_two[h]
                t_two = (e_one * e_one) * u_one * v_one[h]
                to[first, at] = (e_one * p_one - t_one).astype(BF16)
                to[second, at] = (e_two * p_two - t_two).astype(BF16)

    def step(new, old):
        def both_parts(j, carry):
            if old is not None:
                at = pl.ds(pl.multiple_of(j * half_b, half_b), half_b)
                part = dot(low_seg_t[...], dscore[old][:, at], NN)
                middle = at_a if old % 2 == 0 else at_b
                dproto[old][lax.rem(2 * j + 6 - middle, 4)] = part[:, 0:128]
                dproto[old][lax.rem(2 * j + 7 - middle, 4)] = part[:, 128:256]
            if new is not None:
                elements(dscore[new], chunks[new], j)
            return carry

        lax.fori_loop(0, 2, both_parts, 0)

    order = (2, 1, 3, 0)
    chunks, spots = [], []
    for t in order:
        for half, place in ((1 - core, at_b), (core, at_a)):
            spots.append(lax.rem(place + t, 4))
            chunks.append(half * 16 + spots[-1] * 4)
    relays, plains = [None] * 2, [None] * 2
    crossing = [None] * 8
    step(0, None)
    for g in range(8):
        step(g + 1 if g < 7 else None, g)
        if g % 2 == 0:
            crossing[g] = links.send(dproto[g], from_core.at[g // 2], sibling)
            continue
        crossing[g - 1].wait_recv()
        for q in range(4):
            dproto[g][q] = dproto[g][q] + from_core[g // 2, q]
        low, high = dproto[g].at[0:2], dproto[g].at[2:4]
        t = order[g // 2]
        if t == 2:
            relays = [links.send(low, a_relay.at[0], a_peer(1)), links.send(high, a_relay.at[1], a_peer(3))]
        if t == 1:
            plains[0] = links.send(high, a_plain.at[0], a_peer(1))
        if t == 3:
            plains[1] = links.send(low, a_plain.at[1], a_peer(3))
    d_right, d_left, d_own = dproto[3], dproto[5], dproto[7]

    dunit = expo.at[:, 0:width]
    seg_part = both // nz
    z_half = seg_part // 2
    z_right, z_left, z_far = lax.rem(z + 1, 4), lax.rem(z + 3, 4), lax.rem(z + 2, 4)

    def views(k):
        at = pl.ds(pl.multiple_of(k * seg_part, seg_part), seg_part)
        total = None
        for g in range(8):
            rows_g = low_proto[pl.ds(pl.multiple_of(chunks[g] * 128, 512), 512), :]
            term = dot(dscore[g][at, :], rows_g, NN)
            total = term if total is None else total + term
        dunit[at, :] = total

    def part(ref, k, lower):
        start = k * seg_part + (0 if lower else z_half)
        return ref.at[pl.ds(pl.multiple_of(start, z_half), z_half)]

    views(z_far)
    z_relays = [
        links.send(part(dunit, z_far, True), z_relay.at[0], z_peer(1)),
        links.send(part(dunit, z_far, False), z_relay.at[1], z_peer(3)),
    ]
    views(z_right)
    z_plains = [links.send(part(dunit, z_right, False), z_plain.at[0], z_peer(1))]
    relays[0].wait_recv()
    low_joints, high_joints = [None] * 2, [None] * 2
    for q in (0, 1):
        d_right[q] = d_right[q] + a_relay[0, q]
        low_joints[q] = links.send(d_right.at[q], a_joint.at[0, q], a_peer(1))
    relays[1].wait_recv()
    for q in (1, 0):
        d_left[2 + q] = d_left[2 + q] + a_relay[1, q]
        high_joints[q] = links.send(d_left.at[2 + q], a_joint.at[1, q], a_peer(3))

    views(z_left)
    z_plains.append(links.send(part(dunit, z_left, True), z_plain.at[1], z_peer(3)))
    views(z)

    far, left, right = 0, 1, 3
    width_half = width // 2
    for copy in plains:
        copy.wait_recv()
    low_joints[0].wait_recv()
    d_own[far] = d_own[far] + (a_joint[0, 0] + a_plain[1, 0])
    b_relays = [
        links.send(d_own.at[far, 0:width_half], b_relay.at[0], b_peer(1)),
        links.send(d_own.at[far, width_half:width], b_relay.at[1], b_peer(3)),
    ]
    high_joints[1].wait_recv()
    d_own[right] = d_own[right] + (a_plain[0, 1] + a_joint[1, 1])
    b_plains = [links.send(d_own.at[right, width_half:width], b_plain.at[0], b_peer(1))]
    low_joints[1].wait_recv()
    d_own[left] = d_own[left] + (a_joint[0, 1] + a_plain[1, 1])
    b_plains.append(links.send(d_own.at[left, 0:width_half], b_plain.at[1], b_peer(3)))
    high_joints[0].wait_recv()
    d_own[2] = d_own[2] + (a_plain[0, 0] + a_joint[1, 0])

    z_joints = []
    for way, k, skip, peer in ((0, z_right, 0, z_peer(1)), (1, z_left, z_half, z_peer(3))):
        z_relays[way].wait_recv()
        at = pl.ds(pl.multiple_of(k * seg_part + skip, z_half), z_half)
        dunit[at, :] = dunit[at, :] + z_relay[way]
        z_joints.append(links.send(dunit.at[at], z_joint.at[way], peer))

    b_joints = []
    for way, k, skip, peer in ((0, right, 0, b_peer(1)), (1, left, width_half, b_peer(3))):
        b_relays[way].wait_recv()
        at = slice(skip, skip + width_half)
        d_own[k, at, :] = d_own[k, at, :] + b_relay[way]
        b_joints.append(links.send(d_own.at[k, at], b_joint.at[way], peer))
    for copy in b_plains + b_joints:
        copy.wait_recv()
    me = 2
    d_own[me, 0:width_half, :] = d_own[me, 0:width_half, :] + (b_joint[0] + b_plain[1])
    d_own[me, width_half:width, :] = d_own[me, width_half:width, :] + (b_plain[0] + b_joint[1])
    fetch[2].wait()
    gproto[...] = back(jnp.transpose(d_own[me]), own_proto[...])

    def rows_of(chunk, part=None):
        if part is None:
            return gproto_hbm.at[pl.ds(pl.multiple_of(chunk * 128, 128), 128)]
        return gproto_hbm.at[pl.ds(pl.multiple_of(chunk * 128 + part * 64, 64), 64)]

    def chunk_of(a, b):
        return core * 16 + a * 4 + b

    across = []

    def to_sibling(place, src=None):
        across.append(links.send(place if src is None else src, place, sibling))

    b_right, b_left, b_far = lax.rem(at_b + 1, 4), lax.rem(at_b + 3, 4), lax.rem(at_b + 2, 4)
    a_right, a_left, a_far = lax.rem(at_a + 1, 4), lax.rem(at_a + 3, 4), lax.rem(at_a + 2, 4)
    b_in, a_in, a_halves = {}, {}, {}

    def along_a(key, b, part, src=None):
        place = rows_of(chunk_of(at_a, b), part)
        src = place if src is None else src
        a_in[key, 0, part] = links.send(src, place, a_peer(1))
        a_in[key, 1, part] = links.send(src, place, a_peer(3))

    mine_half = [gproto.at[0:64], gproto.at[64:128]]
    b_in[0, 0] = links.send(mine_half[0], rows_of(mine, 0), b_peer(1))
    b_in[1, 1] = links.send(mine_half[1], rows_of(mine, 1), b_peer(3))
    along_a(0, at_b, 0, mine_half[0])
    b_in[0, 1] = links.send(mine_half[1], rows_of(mine, 1), b_peer(1))
    b_in[1, 0] = links.send(mine_half[0], rows_of(mine, 0), b_peer(3))
    along_a(0, at_b, 1, mine_half[1])
    to_sibling(rows_of(mine), gproto)
    keep = pltpu.make_async_copy(gproto, rows_of(mine), local_sem.at[11])
    keep.start()

    for copy in z_plains + z_joints:
        copy.wait_recv()
    at = pl.ds(pl.multiple_of(z * seg_part, z_half), z_half)
    dunit[at, :] = dunit[at, :] + (z_joint[0] + z_plain[1])
    at = pl.ds(pl.multiple_of(z * seg_part + z_half, z_half), z_half)
    dunit[at, :] = dunit[at, :] + (z_plain[0] + z_joint[1])
    at = pl.ds(pl.multiple_of(z * seg_part, seg_part), seg_part)
    dunit[at, :] = back(dunit[at, :], raw[at, :])
    gview, place = dunit.at[at], gview_hbm.at[at]
    z_whole = [links.send(gview, place, z_peer(1)), links.send(gview, place, z_peer(3))]
    keep_view = pltpu.make_async_copy(gview, place, local_sem.at[12])
    keep_view.start()

    b_in[0, 0].wait_recv()
    from_left, from_right = chunk_of(at_a, b_left), chunk_of(at_a, b_right)
    b_halves = [links.send(rows_of(from_left, 0), rows_of(from_left, 0), b_peer(1))]
    along_a(3, b_left, 0)
    b_in[1, 1].wait_recv()
    b_halves.append(links.send(rows_of(from_right, 1), rows_of(from_right, 1), b_peer(3)))
    along_a(1, b_right, 1)
    b_in[0, 1].wait_recv()
    along_a(3, b_left, 1)
    b_in[1, 0].wait_recv()
    along_a(1, b_right, 0)
    to_sibling(rows_of(from_left))
    to_sibling(rows_of(from_right))

    def pass_on(key, b):
        left, right = chunk_of(a_left, b), chunk_of(a_right, b)
        a_in[key, 0, 0].wait_recv()
        a_halves[key] = [links.send(rows_of(left, 0), rows_of(left, 0), a_peer(1))]
        a_in[key, 1, 1].wait_recv()
        a_halves[key].append(links.send(rows_of(right, 1), rows_of(right, 1), a_peer(3)))

    def settle(key, b):
        a_in[key, 0, 1].wait_recv()
        to_sibling(rows_of(chunk_of(a_left, b)))
        a_in[key, 1, 0].wait_recv()
        to_sibling(rows_of(chunk_of(a_right, b)))

    pass_on(0, at_b)
    b_halves[0].wait_recv()
    along_a(2, b_far, 0)
    b_halves[1].wait_recv()
    along_a(2, b_far, 1)
    to_sibling(rows_of(chunk_of(at_a, b_far)))
    settle(0, at_b)

    z_left_place = gview_hbm.at[pl.ds(pl.multiple_of(z_left * seg_part, seg_part), z_half)]
    z_right_place = gview_hbm.at[pl.ds(pl.multiple_of(z_right * seg_part + z_half, z_half), z_half)]
    z_whole[0].wait_recv()
    z_halves = [links.send(z_left_place, z_left_place, z_peer(1))]
    z_whole[1].wait_recv()
    z_halves.append(links.send(z_right_place, z_right_place, z_peer(3)))

    pass_on(3, b_left)
    pass_on(1, b_right)
    settle(3, b_left)
    settle(1, b_right)

    def far_halves(key, b):
        chunk = chunk_of(a_far, b)
        for way in range(2):
            a_halves[key][way].wait_recv()
            to_sibling(rows_of(chunk, way))

    far_halves(0, at_b)
    pass_on(2, b_far)
    far_halves(3, b_left)
    far_halves(1, b_right)
    settle(2, b_far)
    far_halves(2, b_far)
    for copy in z_halves + across:
        copy.wait_recv()
    keep.wait()
    keep_view.wait()
    links.drain()


def balance(mesh, one, two, protos, pair):
    nx, ny, nz = mesh.shape["replica"], mesh.shape["batch"] // 2, mesh.shape["proto"]
    segs, width = one.shape
    count = protos.shape[0]
    both = 2 * segs
    z_half = both // nz // 2
    copies = ITERS * (nx * ny + nz + 1) + 100
    vmem, hbm = pl.BlockSpec(memory_space=pltpu.VMEM), pl.BlockSpec(memory_space=pl.ANY)
    return pl.pallas_call(
        functools.partial(balance_kernel, nx, ny, nz),
        out_shape=(
            pltpu.VMEM((both, width), F32),
            pltpu.VMEM((count, width), F32),
            pltpu.VMEM(pair.shape, jnp.int32),
        ),
        in_specs=[hbm, hbm, hbm, vmem],
        out_specs=(hbm, hbm, vmem),
        scratch_shapes=[
            pltpu.VMEM((both, width), BF16),
            pltpu.VMEM((both, count), F32),
            [pltpu.VMEM((both, count // 8), BF16)] * 8,
            pltpu.VMEM((both, width), BF16),
            pltpu.VMEM((width, both), BF16),
            pltpu.VMEM((count, width), BF16),
            pltpu.VMEM((both, 128), F32),
            pltpu.VMEM((both, 128), F32),
            pltpu.VMEM((ITERS, 8, 8, 128), F32),
            pltpu.VMEM((ITERS, 4, 8, 128), F32),
            pltpu.VMEM((ITERS, nx * ny, 4, 8, 128), F32),
            pltpu.VMEM((ITERS, 8, 8, 128), F32),
            pltpu.VMEM((ITERS, 16, 128), F32),
            pltpu.VMEM((ITERS, nz, 16, 128), F32),
            pltpu.VMEM((16, 128), F32),
            [pltpu.VMEM((4, width, 128), F32)] * 8,
            pltpu.VMEM((4, 4, width, 128), F32),
            pltpu.VMEM((128, width), BF16),
            pltpu.VMEM((128, width), F32),
        ]
        + [pltpu.VMEM((2, 2, width, 128), F32)] * 3
        + [pltpu.VMEM((2, width // 2, 128), F32)] * 3
        + [pltpu.VMEM((2, z_half, width), F32)] * 3
        + [
            pltpu.SemaphoreType.DMA((copies,)),
            pltpu.SemaphoreType.DMA((copies,)),
            pltpu.SemaphoreType.DMA((13,)),
        ],
        compiler_params=pltpu.CompilerParams(
            collective_id=0, has_side_effects=True, vmem_limit_bytes=53 << 20
        ),
        name="balance",
    )(one, two, protos, pair)


def hand_over_kernel(gview, gproto, pair_ref, one_out, two_out, proto_out, two, sems):
    segs = one_out.shape[0]
    parts = 8
    size = proto_out.shape[0] // parts
    copies = [pltpu.make_async_copy(gview.at[0:segs], one_out, sems.at[parts])]
    for i in range(parts):
        at = slice(i * size, (i + 1) * size)
        copies.append(pltpu.make_async_copy(gproto.at[at], proto_out.at[at], sems.at[i]))
    for copy in copies:
        copy.start()
    pair = jnp.broadcast_to(pair_ref[...], (segs, segs))
    number = lax.broadcasted_iota(jnp.int32, (segs, segs), 0)
    onehot = jnp.where(pair == number, 1.0, 0.0).astype(BF16)
    d = gview[segs:2 * segs, :]
    top = d.astype(BF16)
    rest = d - top.astype(F32)
    middle = rest.astype(BF16)
    end = (rest - middle.astype(F32)).astype(BF16)
    two[...] = dot(onehot, top, NN) + (dot(onehot, middle, NN) + dot(onehot, end, NN))
    copies.append(pltpu.make_async_copy(two, two_out, sems.at[parts + 1]))
    copies[-1].start()
    for copy in copies:
        copy.wait()


def hand_over(gview, gproto, pairing):
    segs, width = gview.shape[0] // 2, gview.shape[1]
    half = jax.ShapeDtypeStruct((segs, width), F32)
    vmem, hbm = pl.BlockSpec(memory_space=pltpu.VMEM), pl.BlockSpec(memory_space=pl.ANY)
    return pl.pallas_call(
        hand_over_kernel,
        out_shape=(half, half, jax.ShapeDtypeStruct(gproto.shape, F32)),
        in_specs=[vmem, hbm, vmem],
        out_specs=(hbm,) * 3,
        scratch_shapes=[
            pltpu.VMEM((segs, width), F32),
            pltpu.SemaphoreType.DMA((10,)),
        ],
        compiler_params=pltpu.CompilerParams(vmem_limit_bytes=10 << 20),
        name="hand_over",
    )(gview, gproto, pairing)


def per_device(mesh, view_one, view_two, prototypes, pairing):
    return hand_over(*balance(mesh, view_one, view_two, prototypes, pairing))


def solution(mesh):
    rows = P(("batch", "replica"), None)
    protos = P("proto", None)
    return jax.shard_map(
        functools.partial(per_device, mesh),
        mesh=mesh,
        in_specs=(rows, rows, protos, rows),
        out_specs=(rows, rows, protos),
        check_vma=False,
    )
```

```python
import functools

import jax
import jax.numpy as jnp
from jax import lax
from jax.experimental import pallas as pl
from jax.experimental.pallas import tpu as pltpu
from jax.sharding import PartitionSpec as P

ITERS = 3
EPS = 1e-06
F32 = jnp.float32
BF16 = jnp.bfloat16
MESH = pl.DeviceIdType.MESH
NN = (((1,), (0,)), ((), ()))
NT = (((1,), (1,)), ((), ()))
TN = (((0,), (0,)), ((), ()))
LOG2E = 1.4426950408889634


def dot(a, b, dims):
    return lax.dot_general(a, b, dims, preferred_element_type=F32)


def here():
    batch = lax.axis_index("batch")
    return lax.div(batch, 2), lax.rem(batch, 2), lax.axis_index("replica"), lax.axis_index("proto")


class Links:
    def __init__(self, send_sem, recv_sem):
        self.send_sem, self.recv_sem, self.used, self.sent = send_sem, recv_sem, 0, []

    def send(self, src, dst, peer):
        copy = pltpu.make_async_remote_copy(
            src_ref=src, dst_ref=dst,
            send_sem=self.send_sem.at[self.used], recv_sem=self.recv_sem.at[self.used],
            device_id=peer, device_id_type=MESH,
        )
        copy.start()
        self.used += 1
        self.sent.append(copy)
        return copy

    def drain(self):
        for copy in self.sent:
            copy.wait_send()
        self.sent = []


def back(d, raw):
    xf = raw.astype(F32)
    inv = lax.rsqrt(jnp.sum(xf * xf, -1, keepdims=True) + EPS)
    u = xf * inv
    return inv * (d - u * jnp.sum(u * d, -1, keepdims=True))


def balance_kernel(
    nx, ny, nz,
    one_hbm, two_hbm, proto_hbm, pair_ref,
    gview_hbm, gproto_hbm, pair_out,
    raw, expo, dscore, low_seg, low_seg_t, low_proto, row_scale, prob_scale,
    cols, cols_in, plane_in, weight, rows, rows_in, tile_u,
    dproto, from_core, own_proto, gproto,
    a_relay, a_plain, a_joint, b_relay, b_plain, b_joint, z_relay, z_plain, z_joint,
    send_sem, recv_sem, local_sem,
):
    y, core, x, z = here()
    spot = y * nx + x
    links = Links(send_sem, recv_sem)
    at_a = core * y + (1 - core) * x
    at_b = core * x + (1 - core) * y
    mine = core * 16 + at_a * 4 + at_b

    def plane_peer(dx, dy):
        return (lax.rem(y + dy, ny) * 2 + core, lax.rem(x + dx, nx), z)

    def z_peer(step):
        return (y * 2 + core, x, lax.rem(z + step, nz))

    def a_peer(step):
        return (lax.rem(y + core * step, ny) * 2 + core, lax.rem(x + (1 - core) * step, nx), z)

    def b_peer(step):
        return (lax.rem(y + (1 - core) * step, ny) * 2 + core, lax.rem(x + core * step, nx), z)

    sibling = (y * 2 + 1 - core, x, z)

    segs = one_hbm.shape[0]
    protos, width = low_proto.shape
    both = 2 * segs
    pieces = 8
    piece = protos // pieces
    fetch = [
        pltpu.make_async_copy(one_hbm, raw.at[0:segs], local_sem.at[0]),
        pltpu.make_async_copy(two_hbm, low_seg.at[0:segs], local_sem.at[1]),
        pltpu.make_async_copy(proto_hbm.at[pl.ds(mine * 128, 128)], own_proto, local_sem.at[2]),
    ]
    fetch_protos = [
        pltpu.make_async_copy(
            proto_hbm.at[i * piece:(i + 1) * piece], low_proto.at[i * piece:(i + 1) * piece], local_sem.at[3 + i]
        )
        for i in range(pieces)
    ]
    for copy in fetch + fetch_protos:
        copy.start()
    def hops(step):
        return min(step[0], nx - step[0]) + min(step[1], ny - step[1])

    steps = sorted([(dx, dy) for dx in range(nx) for dy in range(ny)][1:], key=hops, reverse=True)
    peers = [plane_peer(*p) for p in steps] + [z_peer(s) for s in range(1, nz)] + [sibling]
    barrier = pltpu.get_barrier_semaphore()
    for peer in peers:
        pl.semaphore_signal(barrier, inc=1, device_id=peer, device_id_type=MESH)

    def unit(block):
        xf = block.astype(F32)
        inv = lax.rsqrt(jnp.sum(xf * xf, -1, keepdims=True) + EPS)
        return (xf * inv).astype(BF16)

    def norm_views(i, carry):
        at = pl.ds(pl.multiple_of(i * 128, 128), 128)
        low_seg[at, :] = unit(raw[at, :])
        return carry

    fetch[0].wait()
    fetch[1].wait()
    pair_out[...] = pair_ref[...]
    pair = jnp.broadcast_to(pair_ref[...], (segs, segs))
    number = lax.broadcasted_iota(jnp.int32, (segs, segs), 0)
    onehot = dscore[0].at[0:segs]
    onehot[...] = jnp.where(pair == number, 1.0, 0.0).astype(BF16)
    raw[segs:both, :] = dot(onehot[...], low_seg[0:segs, :], TN).astype(BF16)
    lax.fori_loop(0, both // 128, norm_views, 0, unroll=2)

    def norm_protos(i, carry):
        at = pl.ds(pl.multiple_of(i * 128, 128), 128)
        low_proto[at, :] = unit(low_proto[at, :])
        return carry

    for i, copy in enumerate(fetch_protos):
        copy.wait()
        lax.fori_loop(i * piece // 128, (i + 1) * piece // 128, norm_protos, 0, unroll=4)

    wide = protos // 4

    def scores(view):
        ours = pl.ds(pl.multiple_of(view * segs, segs), segs)

        def block(j, carry):
            for q in range(wide // 256):
                at = pl.ds(pl.multiple_of(j * wide + q * 256, 256), 256)
                s = dot(low_seg[ours, :], low_proto[at, :], NT)
                e = jnp.exp2(s * (10.0 * LOG2E))
                expo[ours, at] = e
                total = jnp.sum(e * e, axis=0, keepdims=True)
                for h in range(2):
                    cols[0, view * 4 + j, q * 2 + h:q * 2 + h + 1, :] = total[:, h * 128:(h + 1) * 128]
            return carry

        lax.fori_loop(0, 4, block, 0)

    scores(1 - core)

    def col_sums(it, view):
        def block(j, carry):
            k = view * 4 + j
            first = pl.multiple_of(lax.div(k, 4) * segs, segs)
            left = lax.rem(k, 4) * wide

            def some(r, acc):
                acc = list(acc)
                at = pl.ds(pl.multiple_of(first + r * 128, 128), 128)
                scale = row_scale.at[at]
                tiles = expo.at[at, pl.ds(pl.multiple_of(left, 128), wide)]
                for t in range(16):
                    u = scale[t * 8:(t + 1) * 8, :]
                    for l in range(wide // 128):
                        e = tiles[t * 8:(t + 1) * 8, l * 128:(l + 1) * 128]
                        n = (t % 2) * (wide // 128) + l
                        acc[n] = acc[n] + (e * e) * u
                return tuple(acc)

            zero = jnp.zeros((8, 128), F32)
            acc = lax.fori_loop(0, segs // 128, some, (zero,) * (wide // 64))
            acc = [acc[l] + acc[wide // 128 + l] for l in range(wide // 128)]
            for l in range(wide // 128):
                cols[it, k, l:l + 1, :] = jnp.sum(acc[l], axis=0, keepdims=True)
            return carry

        lax.fori_loop(0, 4, block, 0)

    def turn_segs():
        for i in range(both // 128):
            block = low_seg[i * 128:(i + 1) * 128, :].astype(F32)
            low_seg_t[:, i * 128:(i + 1) * 128] = jnp.transpose(block).astype(BF16)

    def tiles_of(k):
        return pl.ds(pl.multiple_of(k * 4, 4), 4)

    def swap_cols(it):
        return links.send(cols.at[it, tiles_of(1 - core)], cols_in.at[it], sibling)

    def all_cols(it, swap):
        swap.wait_recv()
        plane_in[it, spot] = cols[it, tiles_of(core)] + cols_in[it]
        copies = [
            links.send(plane_in.at[it, spot], plane_in.at[it, spot], plane_peer(*p)) for p in steps
        ]
        if it == 0:
            turn_segs()
        for copy in copies:
            copy.wait_recv()
        total = plane_in[it, 0]
        for k in range(1, nx * ny):
            total = total + plane_in[it, k]
        weight[it, tiles_of(core)] = 1.0 / total
        return links.send(weight.at[it, tiles_of(core)], weight.at[it, tiles_of(core)], sibling)

    spare = dproto[7]

    def row_sums(it, with_total, view):
        def block(b, carry):
            at = pl.ds(pl.multiple_of(view * segs + b * 64, 64), 64)
            acc = jnp.zeros((64, 128), F32)
            tot = jnp.zeros((64, 128), F32)
            tiles = expo.at[at]
            scale = weight.at[it, pl.ds(view * 4, 4)]
            for l in range(protos // 128):
                e = tiles[:, l * 128:(l + 1) * 128]
                v = scale[l // 8, l % 8:l % 8 + 1, :]
                acc = acc + (e * e) * v
                if with_total:
                    tot = tot + e
            spare[view, pl.ds(pl.multiple_of(b * 64, 64), 64), :] = acc
            if with_total:
                spare[2 + view, pl.ds(pl.multiple_of(b * 64, 64), 64), :] = tot
            return carry

        lax.fori_loop(0, segs // 64, block, 0)

    def turn_sums(it, with_total):
        for b in range(both // 128):
            view, at = b // 4, slice(b % 4 * 128, (b % 4 + 1) * 128)
            rows[it, b:b + 1, :] = jnp.sum(jnp.transpose(spare[view, at, :]), axis=0, keepdims=True)
            if with_total:
                tot = jnp.sum(jnp.transpose(spare[2 + view, at, :]), axis=0, keepdims=True)
                rows[it, 8 + b:9 + b, :] = tot

    def spread(out, row):
        for b in range(both // 128):
            wide_row = jnp.broadcast_to(tile_u[row + b:row + b + 1, :], (128, 128))
            out[b * 128:(b + 1) * 128, :] = jnp.transpose(wide_row)

    def all_rows(it, with_total, scale):
        size = 16 if with_total else 8
        rows_in[it, z] = rows[it]
        copies = []
        for s in (2, 1, 3):
            copies.append(links.send(rows.at[it, 0:size], rows_in.at[it, z, 0:size], z_peer(s)))
        for copy in copies:
            copy.wait_recv()
        total = rows_in[it, 0, 0:size]
        for k in range(1, nz):
            total = total + rows_in[it, k, 0:size]
        tile_u[0:8, :] = scale / total[0:8]
        spread(row_scale, 0)
        if with_total:
            tile_u[8:16, :] = 5.0 / total[8:16]
            spread(prob_scale, 8)

    pl.semaphore_wait(barrier, len(peers))
    for it in range(ITERS):
        if it:
            col_sums(it, 1 - core)
            swap = swap_cols(it)
            col_sums(it, core)
        else:
            swap = swap_cols(it)
            scores(core)
        back_copy = all_cols(it, swap)
        row_sums(it, it == 0, core)
        back_copy.wait_recv()
        row_sums(it, it == 0, 1 - core)
        turn_sums(it, it == 0)
        all_rows(it, it == 0, 5.0 if it == ITERS - 1 else 1.0)

    last = ITERS - 1

    half_b = 256

    def elements(ds, chunk, j):
        tiles = expo.at[:, pl.ds(pl.multiple_of(chunk * 128 + j * half_b, half_b), half_b)]
        to = ds.at[:, pl.ds(pl.multiple_of(j * half_b, half_b), half_b)]
        tile = lax.div(chunk, 8)
        row = lax.rem(chunk, 8) + j * 2
        v_one = [weight[last, tile, pl.ds(row + h, 1), :] for h in range(2)]
        v_two = [weight[last, 4 + tile, pl.ds(row + h, 1), :] for h in range(2)]
        for b in range(segs // 32):
            first = slice(b * 32, (b + 1) * 32)
            second = slice(segs + b * 32, segs + (b + 1) * 32)
            u_one, u_two = row_scale[first, :], row_scale[second, :]
            p_one, p_two = prob_scale[first, :], prob_scale[second, :]
            for h in range(2):
                at = slice(h * 128, (h + 1) * 128)
                e_one = tiles[first, at]
                e_two = tiles[second, at]
                t_one = (e_two * e_two) * u_two * v_two[h]
                t_two = (e_one * e_one) * u_one * v_one[h]
                to[first, at] = (e_one * p_one - t_one).astype(BF16)
                to[second, at] = (e_two * p_two - t_two).astype(BF16)

    def step(new, old):
        def both_parts(j, carry):
            if old is not None:
                at = pl.ds(pl.multiple_of(j * half_b, half_b), half_b)
                part = dot(low_seg_t[...], dscore[old][:, at], NN)
                middle = at_a if old % 2 == 0 else at_b
                dproto[old][lax.rem(2 * j + 6 - middle, 4)] = part[:, 0:128]
                dproto[old][lax.rem(2 * j + 7 - middle, 4)] = part[:, 128:256]
            if new is not None:
                elements(dscore[new], chunks[new], j)
            return carry

        lax.fori_loop(0, 2, both_parts, 0)

    order = (2, 1, 3, 0)
    chunks, spots = [], []
    for t in order:
        for half, place in ((1 - core, at_b), (core, at_a)):
            spots.append(lax.rem(place + t, 4))
            chunks.append(half * 16 + spots[-1] * 4)
    relays, plains = [None] * 2, [None] * 2
    crossing = [None] * 8
    step(0, None)
    for g in range(8):
        step(g + 1 if g < 7 else None, g)
        if g % 2 == 0:
            crossing[g] = links.send(dproto[g], from_core.at[g // 2], sibling)
            continue
        crossing[g - 1].wait_recv()
        for q in range(4):
            dproto[g][q] = dproto[g][q] + from_core[g // 2, q]
        low, high = dproto[g].at[0:2], dproto[g].at[2:4]
        t = order[g // 2]
        if t == 2:
            relays = [links.send(low, a_relay.at[0], a_peer(1)), links.send(high, a_relay.at[1], a_peer(3))]
        if t == 1:
            plains[0] = links.send(high, a_plain.at[0], a_peer(1))
        if t == 3:
            plains[1] = links.send(low, a_plain.at[1], a_peer(3))
    d_right, d_left, d_own = dproto[3], dproto[5], dproto[7]

    dunit = expo.at[:, 0:width]
    seg_part = both // nz
    z_half = seg_part // 2
    z_right, z_left, z_far = lax.rem(z + 1, 4), lax.rem(z + 3, 4), lax.rem(z + 2, 4)

    def views(k):
        at = pl.ds(pl.multiple_of(k * seg_part, seg_part), seg_part)
        total = None
        for g in range(8):
            rows_g = low_proto[pl.ds(pl.multiple_of(chunks[g] * 128, 512), 512), :]
            term = dot(dscore[g][at, :], rows_g, NN)
            total = term if total is None else total + term
        dunit[at, :] = total

    def part(ref, k, lower):
        start = k * seg_part + (0 if lower else z_half)
        return ref.at[pl.ds(pl.multiple_of(start, z_half), z_half)]

    views(z_far)
    z_relays = [
        links.send(part(dunit, z_far, True), z_relay.at[0], z_peer(1)),
        links.send(part(dunit, z_far, False), z_relay.at[1], z_peer(3)),
    ]
    views(z_right)
    z_plains = [links.send(part(dunit, z_right, False), z_plain.at[0], z_peer(1))]
    relays[0].wait_recv()
    low_joints, high_joints = [None] * 2, [None] * 2
    for q in (0, 1):
        d_right[q] = d_right[q] + a_relay[0, q]
        low_joints[q] = links.send(d_right.at[q], a_joint.at[0, q], a_peer(1))
    relays[1].wait_recv()
    for q in (1, 0):
        d_left[2 + q] = d_left[2 + q] + a_relay[1, q]
        high_joints[q] = links.send(d_left.at[2 + q], a_joint.at[1, q], a_peer(3))

    views(z_left)
    z_plains.append(links.send(part(dunit, z_left, True), z_plain.at[1], z_peer(3)))
    views(z)

    far, left, right = 0, 1, 3
    width_half = width // 2
    for copy in plains:
        copy.wait_recv()
    low_joints[0].wait_recv()
    d_own[far] = d_own[far] + (a_joint[0, 0] + a_plain[1, 0])
    b_relays = [
        links.send(d_own.at[far, 0:width_half], b_relay.at[0], b_peer(1)),
        links.send(d_own.at[far, width_half:width], b_relay.at[1], b_peer(3)),
    ]
    high_joints[1].wait_recv()
    d_own[right] = d_own[right] + (a_plain[0, 1] + a_joint[1, 1])
    b_plains = [links.send(d_own.at[right, width_half:width], b_plain.at[0], b_peer(1))]
    low_joints[1].wait_recv()
    d_own[left] = d_own[left] + (a_joint[0, 1] + a_plain[1, 1])
    b_plains.append(links.send(d_own.at[left, 0:width_half], b_plain.at[1], b_peer(3)))
    high_joints[0].wait_recv()
    d_own[2] = d_own[2] + (a_plain[0, 0] + a_joint[1, 0])

    z_joints = []
    for way, k, skip, peer in ((0, z_right, 0, z_peer(1)), (1, z_left, z_half, z_peer(3))):
        z_relays[way].wait_recv()
        at = pl.ds(pl.multiple_of(k * seg_part + skip, z_half), z_half)
        dunit[at, :] = dunit[at, :] + z_relay[way]
        z_joints.append(links.send(dunit.at[at], z_joint.at[way], peer))

    b_joints = []
    for way, k, skip, peer in ((0, right, 0, b_peer(1)), (1, left, width_half, b_peer(3))):
        b_relays[way].wait_recv()
        at = slice(skip, skip + width_half)
        d_own[k, at, :] = d_own[k, at, :] + b_relay[way]
        b_joints.append(links.send(d_own.at[k, at], b_joint.at[way], peer))
    for copy in b_plains + b_joints:
        copy.wait_recv()
    me = 2
    d_own[me, 0:width_half, :] = d_own[me, 0:width_half, :] + (b_joint[0] + b_plain[1])
    d_own[me, width_half:width, :] = d_own[me, width_half:width, :] + (b_plain[0] + b_joint[1])
    fetch[2].wait()
    gproto[...] = back(jnp.transpose(d_own[me]), own_proto[...])

    def rows_of(chunk, part=None):
        if part is None:
            return gproto_hbm.at[pl.ds(pl.multiple_of(chunk * 128, 128), 128)]
        return gproto_hbm.at[pl.ds(pl.multiple_of(chunk * 128 + part * 64, 64), 64)]

    def chunk_of(a, b):
        return core * 16 + a * 4 + b

    across = []

    def to_sibling(place, src=None):
        across.append(links.send(place if src is None else src, place, sibling))

    b_right, b_left, b_far = lax.rem(at_b + 1, 4), lax.rem(at_b + 3, 4), lax.rem(at_b + 2, 4)
    a_right, a_left, a_far = lax.rem(at_a + 1, 4), lax.rem(at_a + 3, 4), lax.rem(at_a + 2, 4)
    b_in, a_in, a_halves = {}, {}, {}

    def along_a(key, b, part, src=None):
        place = rows_of(chunk_of(at_a, b), part)
        src = place if src is None else src
        a_in[key, 0, part] = links.send(src, place, a_peer(1))
        a_in[key, 1, part] = links.send(src, place, a_peer(3))

    mine_half = [gproto.at[0:64], gproto.at[64:128]]
    b_in[0, 0] = links.send(mine_half[0], rows_of(mine, 0), b_peer(1))
    b_in[1, 1] = links.send(mine_half[1], rows_of(mine, 1), b_peer(3))
    along_a(0, at_b, 0, mine_half[0])
    b_in[0, 1] = links.send(mine_half[1], rows_of(mine, 1), b_peer(1))
    b_in[1, 0] = links.send(mine_half[0], rows_of(mine, 0), b_peer(3))
    along_a(0, at_b, 1, mine_half[1])
    to_sibling(rows_of(mine), gproto)
    keep = pltpu.make_async_copy(gproto, rows_of(mine), local_sem.at[11])
    keep.start()

    for copy in z_plains + z_joints:
        copy.wait_recv()
    at = pl.ds(pl.multiple_of(z * seg_part, z_half), z_half)
    dunit[at, :] = dunit[at, :] + (z_joint[0] + z_plain[1])
    at = pl.ds(pl.multiple_of(z * seg_part + z_half, z_half), z_half)
    dunit[at, :] = dunit[at, :] + (z_plain[0] + z_joint[1])
    at = pl.ds(pl.multiple_of(z * seg_part, seg_part), seg_part)
    dunit[at, :] = back(dunit[at, :], raw[at, :])
    gview, place = dunit.at[at], gview_hbm.at[at]
    z_whole = [links.send(gview, place, z_peer(1)), links.send(gview, place, z_peer(3))]
    keep_view = pltpu.make_async_copy(gview, place, local_sem.at[12])
    keep_view.start()

    b_in[0, 0].wait_recv()
    from_left, from_right = chunk_of(at_a, b_left), chunk_of(at_a, b_right)
    b_halves = [links.send(rows_of(from_left, 0), rows_of(from_left, 0), b_peer(1))]
    along_a(3, b_left, 0)
    b_in[1, 1].wait_recv()
    b_halves.append(links.send(rows_of(from_right, 1), rows_of(from_right, 1), b_peer(3)))
    along_a(1, b_right, 1)
    b_in[0, 1].wait_recv()
    along_a(3, b_left, 1)
    b_in[1, 0].wait_recv()
    along_a(1, b_right, 0)
    to_sibling(rows_of(from_left))
    to_sibling(rows_of(from_right))

    def pass_on(key, b):
        left, right = chunk_of(a_left, b), chunk_of(a_right, b)
        a_in[key, 0, 0].wait_recv()
        a_halves[key] = [links.send(rows_of(left, 0), rows_of(left, 0), a_peer(1))]
        a_in[key, 1, 1].wait_recv()
        a_halves[key].append(links.send(rows_of(right, 1), rows_of(right, 1), a_peer(3)))

    def settle(key, b):
        a_in[key, 0, 1].wait_recv()
        to_sibling(rows_of(chunk_of(a_left, b)))
        a_in[key, 1, 0].wait_recv()
        to_sibling(rows_of(chunk_of(a_right, b)))

    pass_on(0, at_b)
    b_halves[0].wait_recv()
    along_a(2, b_far, 0)
    b_halves[1].wait_recv()
    along_a(2, b_far, 1)
    to_sibling(rows_of(chunk_of(at_a, b_far)))
    settle(0, at_b)

    z_left_place = gview_hbm.at[pl.ds(pl.multiple_of(z_left * seg_part, seg_part), z_half)]
    z_right_place = gview_hbm.at[pl.ds(pl.multiple_of(z_right * seg_part + z_half, z_half), z_half)]
    z_whole[0].wait_recv()
    z_halves = [links.send(z_left_place, z_left_place, z_peer(1))]
    z_whole[1].wait_recv()
    z_halves.append(links.send(z_right_place, z_right_place, z_peer(3)))

    pass_on(3, b_left)
    pass_on(1, b_right)
    settle(3, b_left)
    settle(1, b_right)

    def far_halves(key, b):
        chunk = chunk_of(a_far, b)
        for way in range(2):
            a_halves[key][way].wait_recv()
            to_sibling(rows_of(chunk, way))

    far_halves(0, at_b)
    pass_on(2, b_far)
    far_halves(3, b_left)
    far_halves(1, b_right)
    settle(2, b_far)
    far_halves(2, b_far)
    for copy in z_halves + across:
        copy.wait_recv()
    keep.wait()
    keep_view.wait()
    links.drain()


def balance(mesh, one, two, protos, pair):
    nx, ny, nz = mesh.shape["replica"], mesh.shape["batch"] // 2, mesh.shape["proto"]
    segs, width = one.shape
    count = protos.shape[0]
    both = 2 * segs
    z_half = both // nz // 2
    copies = ITERS * (nx * ny + nz + 1) + 100
    vmem, hbm = pl.BlockSpec(memory_space=pltpu.VMEM), pl.BlockSpec(memory_space=pl.ANY)
    return pl.pallas_call(
        functools.partial(balance_kernel, nx, ny, nz),
        out_shape=(
            pltpu.VMEM((both, width), F32),
            pltpu.VMEM((count, width), F32),
            pltpu.VMEM(pair.shape, jnp.int32),
        ),
        in_specs=[hbm, hbm, hbm, vmem],
        out_specs=(hbm, hbm, vmem),
        scratch_shapes=[
            pltpu.VMEM((both, width), BF16),
            pltpu.VMEM((both, count), F32),
            [pltpu.VMEM((both, count // 8), BF16)] * 8,
            pltpu.VMEM((both, width), BF16),
            pltpu.VMEM((width, both), BF16),
            pltpu.VMEM((count, width), BF16),
            pltpu.VMEM((both, 128), F32),
            pltpu.VMEM((both, 128), F32),
            pltpu.VMEM((ITERS, 8, 8, 128), F32),
            pltpu.VMEM((ITERS, 4, 8, 128), F32),
            pltpu.VMEM((ITERS, nx * ny, 4, 8, 128), F32),
            pltpu.VMEM((ITERS, 8, 8, 128), F32),
            pltpu.VMEM((ITERS, 16, 128), F32),
            pltpu.VMEM((ITERS, nz, 16, 128), F32),
            pltpu.VMEM((16, 128), F32),
            [pltpu.VMEM((4, width, 128), F32)] * 8,
            pltpu.VMEM((4, 4, width, 128), F32),
            pltpu.VMEM((128, width), BF16),
            pltpu.VMEM((128, width), F32),
        ]
        + [pltpu.VMEM((2, 2, width, 128), F32)] * 3
        + [pltpu.VMEM((2, width // 2, 128), F32)] * 3
        + [pltpu.VMEM((2, z_half, width), F32)] * 3
        + [
            pltpu.SemaphoreType.DMA((copies,)),
            pltpu.SemaphoreType.DMA((copies,)),
            pltpu.SemaphoreType.DMA((13,)),
        ],
        compiler_params=pltpu.CompilerParams(
            collective_id=0, has_side_effects=True, vmem_limit_bytes=53 << 20
        ),
        name="balance",
    )(one, two, protos, pair)


def hand_over_kernel(gview, gproto, pair_ref, one_out, two_out, proto_out, two, sems):
    segs = one_out.shape[0]
    parts = 8
    size = proto_out.shape[0] // parts
    copies = [pltpu.make_async_copy(gview.at[0:segs], one_out, sems.at[parts])]
    for i in range(parts):
        at = slice(i * size, (i + 1) * size)
        copies.append(pltpu.make_async_copy(gproto.at[at], proto_out.at[at], sems.at[i]))
    for copy in copies:
        copy.start()
    pair = jnp.broadcast_to(pair_ref[...], (segs, segs))
    number = lax.broadcasted_iota(jnp.int32, (segs, segs), 0)
    onehot = jnp.where(pair == number, 1.0, 0.0).astype(BF16)
    d = gview[segs:2 * segs, :]
    top = d.astype(BF16)
    rest = d - top.astype(F32)
    middle = rest.astype(BF16)
    end = (rest - middle.astype(F32)).astype(BF16)
    two[...] = dot(onehot, top, NN) + (dot(onehot, middle, NN) + dot(onehot, end, NN))
    copies.append(pltpu.make_async_copy(two, two_out, sems.at[parts + 1]))
    copies[-1].start()
    for copy in copies:
        copy.wait()


def hand_over(gview, gproto, pairing):
    segs, width = gview.shape[0] // 2, gview.shape[1]
    half = jax.ShapeDtypeStruct((segs, width), F32)
    vmem, hbm = pl.BlockSpec(memory_space=pltpu.VMEM), pl.BlockSpec(memory_space=pl.ANY)
    return pl.pallas_call(
        hand_over_kernel,
        out_shape=(half, half, jax.ShapeDtypeStruct(gproto.shape, F32)),
        in_specs=[vmem, hbm, vmem],
        out_specs=(hbm,) * 3,
        scratch_shapes=[
            pltpu.VMEM((segs, width), F32),
            pltpu.SemaphoreType.DMA((10,)),
        ],
        compiler_params=pltpu.CompilerParams(vmem_limit_bytes=10 << 20),
        name="hand_over",
    )(gview, gproto, pairing)


def per_device(mesh, view_one, view_two, prototypes, pairing):
    return hand_over(*balance(mesh, view_one, view_two, prototypes, pairing))


def solution(mesh):
    rows = P(("batch", "replica"), None)
    protos = P("proto", None)
    return jax.shard_map(
        functools.partial(per_device, mesh),
        mesh=mesh,
        in_specs=(rows, rows, protos, rows),
        out_specs=(rows, rows, protos),
        check_vma=False,
    )
```

```python
import functools

import jax
import jax.numpy as jnp
from jax import lax
from jax.experimental import pallas as pl
from jax.experimental.pallas import tpu as pltpu
from jax.sharding import PartitionSpec as P

ITERS = 3
EPS = 1e-06
F32 = jnp.float32
BF16 = jnp.bfloat16
MESH = pl.DeviceIdType.MESH
NN = (((1,), (0,)), ((), ()))
NT = (((1,), (1,)), ((), ()))
TN = (((0,), (0,)), ((), ()))
LOG2E = 1.4426950408889634


def dot(a, b, dims):
    return lax.dot_general(a, b, dims, preferred_element_type=F32)


def here():
    batch = lax.axis_index("batch")
    return lax.div(batch, 2), lax.rem(batch, 2), lax.axis_index("replica"), lax.axis_index("proto")


class Links:
    def __init__(self, send_sem, recv_sem):
        self.send_sem, self.recv_sem, self.used, self.sent = send_sem, recv_sem, 0, []

    def send(self, src, dst, peer):
        copy = pltpu.make_async_remote_copy(
            src_ref=src, dst_ref=dst,
            send_sem=self.send_sem.at[self.used], recv_sem=self.recv_sem.at[self.used],
            device_id=peer, device_id_type=MESH,
        )
        copy.start()
        self.used += 1
        self.sent.append(copy)
        return copy

    def drain(self, count):
        for copy in self.sent[:count]:
            copy.wait_send()
        self.sent = self.sent[count:]


def back(d, raw):
    xf = raw.astype(F32)
    inv = lax.rsqrt(jnp.sum(xf * xf, -1, keepdims=True) + EPS)
    u = xf * inv
    return inv * (d - u * jnp.sum(u * d, -1, keepdims=True))


def balance_kernel(
    nx, ny, nz,
    one_hbm, two_hbm, proto_hbm, pair_ref,
    gview_hbm, gproto_hbm, pair_out,
    raw, expo, dscore, low_seg, low_seg_t, low_proto, row_scale, prob_scale,
    cols, cols_in, plane_in, weight, rows, rows_in, tile_u,
    dproto, from_core, own_proto, gproto,
    a_relay, a_plain, a_joint, b_relay, b_plain, b_joint, z_relay, z_plain, z_joint,
    send_sem, recv_sem, local_sem,
):
    y, core, x, z = here()
    spot = y * nx + x
    links = Links(send_sem, recv_sem)
    at_a = core * y + (1 - core) * x
    at_b = core * x + (1 - core) * y
    mine = core * 16 + at_a * 4 + at_b

    def plane_peer(dx, dy):
        return (lax.rem(y + dy, ny) * 2 + core, lax.rem(x + dx, nx), z)

    def z_peer(step):
        return (y * 2 + core, x, lax.rem(z + step, nz))

    def a_peer(step):
        return (lax.rem(y + core * step, ny) * 2 + core, lax.rem(x + (1 - core) * step, nx), z)

    def b_peer(step):
        return (lax.rem(y + (1 - core) * step, ny) * 2 + core, lax.rem(x + core * step, nx), z)

    sibling = (y * 2 + 1 - core, x, z)

    segs = one_hbm.shape[0]
    protos, width = low_proto.shape
    both = 2 * segs
    pieces = 8
    piece = protos // pieces
    fetch = [
        pltpu.make_async_copy(one_hbm, raw.at[0:segs], local_sem.at[0]),
        pltpu.make_async_copy(two_hbm, low_seg.at[0:segs], local_sem.at[1]),
        pltpu.make_async_copy(proto_hbm.at[pl.ds(mine * 128, 128)], own_proto, local_sem.at[2]),
    ]
    fetch_protos = [
        pltpu.make_async_copy(
            proto_hbm.at[i * piece:(i + 1) * piece], low_proto.at[i * piece:(i + 1) * piece], local_sem.at[3 + i]
        )
        for i in range(pieces)
    ]
    for copy in fetch + fetch_protos:
        copy.start()
    def hops(step):
        return min(step[0], nx - step[0]) + min(step[1], ny - step[1])

    steps = sorted([(dx, dy) for dx in range(nx) for dy in range(ny)][1:], key=hops, reverse=True)
    peers = [plane_peer(*p) for p in steps] + [z_peer(s) for s in range(1, nz)] + [sibling]
    barrier = pltpu.get_barrier_semaphore()
    for peer in peers:
        pl.semaphore_signal(barrier, inc=1, device_id=peer, device_id_type=MESH)

    def unit(block):
        xf = block.astype(F32)
        inv = lax.rsqrt(jnp.sum(xf * xf, -1, keepdims=True) + EPS)
        return (xf * inv).astype(BF16)

    def norm_views(i, carry):
        at = pl.ds(pl.multiple_of(i * 128, 128), 128)
        low_seg[at, :] = unit(raw[at, :])
        return carry

    fetch[0].wait()
    fetch[1].wait()
    pair_out[...] = pair_ref[...]
    pair = jnp.broadcast_to(pair_ref[...], (segs, segs))
    number = lax.broadcasted_iota(jnp.int32, (segs, segs), 0)
    onehot = dscore[0].at[0:segs]
    onehot[...] = jnp.where(pair == number, 1.0, 0.0).astype(BF16)
    raw[segs:both, :] = dot(onehot[...], low_seg[0:segs, :], TN).astype(BF16)
    lax.fori_loop(0, both // 128, norm_views, 0, unroll=2)

    def norm_protos(i, carry):
        at = pl.ds(pl.multiple_of(i * 128, 128), 128)
        low_proto[at, :] = unit(low_proto[at, :])
        return carry

    for i, copy in enumerate(fetch_protos):
        copy.wait()
        lax.fori_loop(i * piece // 128, (i + 1) * piece // 128, norm_protos, 0, unroll=4)

    wide = protos // 4

    def scores(view):
        ours = pl.ds(pl.multiple_of(view * segs, segs), segs)

        def block(j, carry):
            for q in range(wide // 256):
                at = pl.ds(pl.multiple_of(j * wide + q * 256, 256), 256)
                s = dot(low_seg[ours, :], low_proto[at, :], NT)
                e = jnp.exp2(s * (10.0 * LOG2E))
                expo[ours, at] = e
                total = jnp.sum(e * e, axis=0, keepdims=True)
                for h in range(2):
                    cols[0, view * 4 + j, q * 2 + h:q * 2 + h + 1, :] = total[:, h * 128:(h + 1) * 128]
            return carry

        lax.fori_loop(0, 4, block, 0)

    scores(1 - core)

    def col_sums(it, view):
        def block(j, carry):
            k = view * 4 + j
            first = pl.multiple_of(lax.div(k, 4) * segs, segs)
            left = lax.rem(k, 4) * wide

            def some(r, acc):
                acc = list(acc)
                at = pl.ds(pl.multiple_of(first + r * 128, 128), 128)
                scale = row_scale.at[at]
                tiles = expo.at[at, pl.ds(pl.multiple_of(left, 128), wide)]
                for t in range(16):
                    u = scale[t * 8:(t + 1) * 8, :]
                    for l in range(wide // 128):
                        e = tiles[t * 8:(t + 1) * 8, l * 128:(l + 1) * 128]
                        n = (t % 2) * (wide // 128) + l
                        acc[n] = acc[n] + (e * e) * u
                return tuple(acc)

            zero = jnp.zeros((8, 128), F32)
            acc = lax.fori_loop(0, segs // 128, some, (zero,) * (wide // 64))
            acc = [acc[l] + acc[wide // 128 + l] for l in range(wide // 128)]
            for l in range(wide // 128):
                cols[it, k, l:l + 1, :] = jnp.sum(acc[l], axis=0, keepdims=True)
            return carry

        lax.fori_loop(0, 4, block, 0)

    def turn_segs():
        for i in range(both // 128):
            block = low_seg[i * 128:(i + 1) * 128, :].astype(F32)
            low_seg_t[:, i * 128:(i + 1) * 128] = jnp.transpose(block).astype(BF16)

    def tiles_of(k):
        return pl.ds(pl.multiple_of(k * 4, 4), 4)

    def swap_cols(it):
        return links.send(cols.at[it, tiles_of(1 - core)], cols_in.at[it], sibling)

    def all_cols(it, swap):
        swap.wait_recv()
        plane_in[it, spot] = cols[it, tiles_of(core)] + cols_in[it]
        copies = [
            links.send(plane_in.at[it, spot], plane_in.at[it, spot], plane_peer(*p)) for p in steps
        ]
        if it == 0:
            turn_segs()
        for copy in copies:
            copy.wait_recv()
        total = plane_in[it, 0]
        for k in range(1, nx * ny):
            total = total + plane_in[it, k]
        weight[it, tiles_of(core)] = 1.0 / total
        return links.send(weight.at[it, tiles_of(core)], weight.at[it, tiles_of(core)], sibling)

    spare = dproto[7]

    def row_sums(it, with_total, view):
        def block(b, carry):
            at = pl.ds(pl.multiple_of(view * segs + b * 64, 64), 64)
            acc = jnp.zeros((64, 128), F32)
            tot = jnp.zeros((64, 128), F32)
            tiles = expo.at[at]
            scale = weight.at[it, pl.ds(view * 4, 4)]
            for l in range(protos // 128):
                e = tiles[:, l * 128:(l + 1) * 128]
                v = scale[l // 8, l % 8:l % 8 + 1, :]
                acc = acc + (e * e) * v
                if with_total:
                    tot = tot + e
            spare[view, pl.ds(pl.multiple_of(b * 64, 64), 64), :] = acc
            if with_total:
                spare[2 + view, pl.ds(pl.multiple_of(b * 64, 64), 64), :] = tot
            return carry

        lax.fori_loop(0, segs // 64, block, 0)

    def turn_sums(it, with_total):
        for b in range(both // 128):
            view, at = b // 4, slice(b % 4 * 128, (b % 4 + 1) * 128)
            rows[it, b:b + 1, :] = jnp.sum(jnp.transpose(spare[view, at, :]), axis=0, keepdims=True)
            if with_total:
                tot = jnp.sum(jnp.transpose(spare[2 + view, at, :]), axis=0, keepdims=True)
                rows[it, 8 + b:9 + b, :] = tot

    def spread(out, row):
        for b in range(both // 128):
            wide_row = jnp.broadcast_to(tile_u[row + b:row + b + 1, :], (128, 128))
            out[b * 128:(b + 1) * 128, :] = jnp.transpose(wide_row)

    def all_rows(it, with_total, scale):
        size = 16 if with_total else 8
        rows_in[it, z] = rows[it]
        copies = []
        for s in (2, 1, 3):
            copies.append(links.send(rows.at[it, 0:size], rows_in.at[it, z, 0:size], z_peer(s)))
        for copy in copies:
            copy.wait_recv()
        total = rows_in[it, 0, 0:size]
        for k in range(1, nz):
            total = total + rows_in[it, k, 0:size]
        tile_u[0:8, :] = scale / total[0:8]
        spread(row_scale, 0)
        if with_total:
            tile_u[8:16, :] = 5.0 / total[8:16]
            spread(prob_scale, 8)

    pl.semaphore_wait(barrier, len(peers))
    for it in range(ITERS):
        if it:
            col_sums(it, 1 - core)
            swap = swap_cols(it)
            col_sums(it, core)
        else:
            swap = swap_cols(it)
            scores(core)
        back_copy = all_cols(it, swap)
        row_sums(it, it == 0, core)
        back_copy.wait_recv()
        row_sums(it, it == 0, 1 - core)
        turn_sums(it, it == 0)
        all_rows(it, it == 0, 5.0 if it == ITERS - 1 else 1.0)

    last = ITERS - 1

    half_b = 256

    def elements(ds, chunk, j):
        tiles = expo.at[:, pl.ds(pl.multiple_of(chunk * 128 + j * half_b, half_b), half_b)]
        to = ds.at[:, pl.ds(pl.multiple_of(j * half_b, half_b), half_b)]
        tile = lax.div(chunk, 8)
        row = lax.rem(chunk, 8) + j * 2
        v_one = [weight[last, tile, pl.ds(row + h, 1), :] for h in range(2)]
        v_two = [weight[last, 4 + tile, pl.ds(row + h, 1), :] for h in range(2)]
        for b in range(segs // 32):
            first = slice(b * 32, (b + 1) * 32)
            second = slice(segs + b * 32, segs + (b + 1) * 32)
            u_one, u_two = row_scale[first, :], row_scale[second, :]
            p_one, p_two = prob_scale[first, :], prob_scale[second, :]
            for h in range(2):
                at = slice(h * 128, (h + 1) * 128)
                e_one = tiles[first, at]
                e_two = tiles[second, at]
                t_one = (e_two * e_two) * u_two * v_two[h]
                t_two = (e_one * e_one) * u_one * v_one[h]
                to[first, at] = (e_one * p_one - t_one).astype(BF16)
                to[second, at] = (e_two * p_two - t_two).astype(BF16)

    def step(new, old):
        def both_parts(j, carry):
            if old is not None:
                at = pl.ds(pl.multiple_of(j * half_b, half_b), half_b)
                part = dot(low_seg_t[...], dscore[old][:, at], NN)
                middle = at_a if old % 2 == 0 else at_b
                dproto[old][lax.rem(2 * j + 6 - middle, 4)] = part[:, 0:128]
                dproto[old][lax.rem(2 * j + 7 - middle, 4)] = part[:, 128:256]
            if new is not None:
                elements(dscore[new], chunks[new], j)
            return carry

        lax.fori_loop(0, 2, both_parts, 0)

    order = (2, 1, 3, 0)
    chunks, spots = [], []
    small_sends = len(links.sent)
    for t in order:
        for half, place in ((1 - core, at_b), (core, at_a)):
            spots.append(lax.rem(place + t, 4))
            chunks.append(half * 16 + spots[-1] * 4)
    relays, plains = [None] * 2, [None] * 2
    crossing = [None] * 8
    step(0, None)
    for g in range(8):
        step(g + 1 if g < 7 else None, g)
        if g % 2 == 0:
            crossing[g] = links.send(dproto[g], from_core.at[g // 2], sibling)
            continue
        crossing[g - 1].wait_recv()
        for q in range(4):
            dproto[g][q] = dproto[g][q] + from_core[g // 2, q]
        low, high = dproto[g].at[0:2], dproto[g].at[2:4]
        t = order[g // 2]
        if t == 2:
            relays = [links.send(low, a_relay.at[0], a_peer(1)), links.send(high, a_relay.at[1], a_peer(3))]
        if t == 1:
            plains[0] = links.send(high, a_plain.at[0], a_peer(1))
        if t == 3:
            plains[1] = links.send(low, a_plain.at[1], a_peer(3))
    d_right, d_left, d_own = dproto[3], dproto[5], dproto[7]

    dunit = expo.at[:, 0:width]
    seg_part = both // nz
    z_half = seg_part // 2
    z_right, z_left, z_far = lax.rem(z + 1, 4), lax.rem(z + 3, 4), lax.rem(z + 2, 4)

    def views(k):
        at = pl.ds(pl.multiple_of(k * seg_part, seg_part), seg_part)
        total = None
        for g in range(8):
            rows_g = low_proto[pl.ds(pl.multiple_of(chunks[g] * 128, 512), 512), :]
            term = dot(dscore[g][at, :], rows_g, NN)
            total = term if total is None else total + term
        dunit[at, :] = total

    def part(ref, k, lower):
        start = k * seg_part + (0 if lower else z_half)
        return ref.at[pl.ds(pl.multiple_of(start, z_half), z_half)]

    views(z_far)
    z_relays = [
        links.send(part(dunit, z_far, True), z_relay.at[0], z_peer(1)),
        links.send(part(dunit, z_far, False), z_relay.at[1], z_peer(3)),
    ]
    views(z_right)
    z_plains = [links.send(part(dunit, z_right, False), z_plain.at[0], z_peer(1))]
    links.drain(small_sends)
    relays[0].wait_recv()
    low_joints, high_joints = [None] * 2, [None] * 2
    for q in (0, 1):
        d_right[q] = d_right[q] + a_relay[0, q]
        low_joints[q] = links.send(d_right.at[q], a_joint.at[0, q], a_peer(1))
    relays[1].wait_recv()
    for q in (1, 0):
        d_left[2 + q] = d_left[2 + q] + a_relay[1, q]
        high_joints[q] = links.send(d_left.at[2 + q], a_joint.at[1, q], a_peer(3))

    views(z_left)
    z_plains.append(links.send(part(dunit, z_left, True), z_plain.at[1], z_peer(3)))
    views(z)

    far, left, right = 0, 1, 3
    width_half = width // 2
    for copy in plains:
        copy.wait_recv()
    low_joints[0].wait_recv()
    d_own[far] = d_own[far] + (a_joint[0, 0] + a_plain[1, 0])
    b_relays = [
        links.send(d_own.at[far, 0:width_half], b_relay.at[0], b_peer(1)),
        links.send(d_own.at[far, width_half:width], b_relay.at[1], b_peer(3)),
    ]
    high_joints[1].wait_recv()
    d_own[right] = d_own[right] + (a_plain[0, 1] + a_joint[1, 1])
    b_plains = [links.send(d_own.at[right, width_half:width], b_plain.at[0], b_peer(1))]
    low_joints[1].wait_recv()
    d_own[left] = d_own[left] + (a_joint[0, 1] + a_plain[1, 1])
    b_plains.append(links.send(d_own.at[left, 0:width_half], b_plain.at[1], b_peer(3)))
    high_joints[0].wait_recv()
    d_own[2] = d_own[2] + (a_plain[0, 0] + a_joint[1, 0])

    z_joints = []
    for way, k, skip, peer in ((0, z_right, 0, z_peer(1)), (1, z_left, z_half, z_peer(3))):
        z_relays[way].wait_recv()
        at = pl.ds(pl.multiple_of(k * seg_part + skip, z_half), z_half)
        dunit[at, :] = dunit[at, :] + z_relay[way]
        z_joints.append(links.send(dunit.at[at], z_joint.at[way], peer))

    b_joints = []
    for way, k, skip, peer in ((0, right, 0, b_peer(1)), (1, left, width_half, b_peer(3))):
        b_relays[way].wait_recv()
        at = slice(skip, skip + width_half)
        d_own[k, at, :] = d_own[k, at, :] + b_relay[way]
        b_joints.append(links.send(d_own.at[k, at], b_joint.at[way], peer))
    for copy in b_plains + b_joints:
        copy.wait_recv()
    me = 2
    d_own[me, 0:width_half, :] = d_own[me, 0:width_half, :] + (b_joint[0] + b_plain[1])
    d_own[me, width_half:width, :] = d_own[me, width_half:width, :] + (b_plain[0] + b_joint[1])
    fetch[2].wait()
    gproto[...] = back(jnp.transpose(d_own[me]), own_proto[...])

    def rows_of(chunk, part=None):
        if part is None:
            return gproto_hbm.at[pl.ds(pl.multiple_of(chunk * 128, 128), 128)]
        return gproto_hbm.at[pl.ds(pl.multiple_of(chunk * 128 + part * 64, 64), 64)]

    def chunk_of(a, b):
        return core * 16 + a * 4 + b

    across = []

    def to_sibling(place, src=None):
        across.append(links.send(place if src is None else src, place, sibling))

    b_right, b_left, b_far = lax.rem(at_b + 1, 4), lax.rem(at_b + 3, 4), lax.rem(at_b + 2, 4)
    a_right, a_left, a_far = lax.rem(at_a + 1, 4), lax.rem(at_a + 3, 4), lax.rem(at_a + 2, 4)
    b_in, a_in, a_halves = {}, {}, {}
    sum_sends = len(links.sent)

    def along_a(key, b, part, src=None):
        place = rows_of(chunk_of(at_a, b), part)
        src = place if src is None else src
        a_in[key, 0, part] = links.send(src, place, a_peer(1))
        a_in[key, 1, part] = links.send(src, place, a_peer(3))

    mine_half = [gproto.at[0:64], gproto.at[64:128]]
    b_in[0, 0] = links.send(mine_half[0], rows_of(mine, 0), b_peer(1))
    b_in[1, 1] = links.send(mine_half[1], rows_of(mine, 1), b_peer(3))
    along_a(0, at_b, 0, mine_half[0])
    b_in[0, 1] = links.send(mine_half[1], rows_of(mine, 1), b_peer(1))
    b_in[1, 0] = links.send(mine_half[0], rows_of(mine, 0), b_peer(3))
    along_a(0, at_b, 1, mine_half[1])
    to_sibling(rows_of(mine), gproto)
    keep = pltpu.make_async_copy(gproto, rows_of(mine), local_sem.at[11])
    keep.start()

    for copy in z_plains + z_joints:
        copy.wait_recv()
    at = pl.ds(pl.multiple_of(z * seg_part, z_half), z_half)
    dunit[at, :] = dunit[at, :] + (z_joint[0] + z_plain[1])
    at = pl.ds(pl.multiple_of(z * seg_part + z_half, z_half), z_half)
    dunit[at, :] = dunit[at, :] + (z_plain[0] + z_joint[1])
    at = pl.ds(pl.multiple_of(z * seg_part, seg_part), seg_part)
    dunit[at, :] = back(dunit[at, :], raw[at, :])
    gview, place = dunit.at[at], gview_hbm.at[at]
    z_whole = [links.send(gview, place, z_peer(1)), links.send(gview, place, z_peer(3))]
    keep_view = pltpu.make_async_copy(gview, place, local_sem.at[12])
    keep_view.start()

    links.drain(sum_sends)
    b_in[0, 0].wait_recv()
    from_left, from_right = chunk_of(at_a, b_left), chunk_of(at_a, b_right)
    b_halves = [links.send(rows_of(from_left, 0), rows_of(from_left, 0), b_peer(1))]
    along_a(3, b_left, 0)
    b_in[1, 1].wait_recv()
    b_halves.append(links.send(rows_of(from_right, 1), rows_of(from_right, 1), b_peer(3)))
    along_a(1, b_right, 1)
    b_in[0, 1].wait_recv()
    along_a(3, b_left, 1)
    b_in[1, 0].wait_recv()
    along_a(1, b_right, 0)
    to_sibling(rows_of(from_left))
    to_sibling(rows_of(from_right))

    def pass_on(key, b):
        left, right = chunk_of(a_left, b), chunk_of(a_right, b)
        a_in[key, 0, 0].wait_recv()
        a_halves[key] = [links.send(rows_of(left, 0), rows_of(left, 0), a_peer(1))]
        a_in[key, 1, 1].wait_recv()
        a_halves[key].append(links.send(rows_of(right, 1), rows_of(right, 1), a_peer(3)))

    def settle(key, b):
        a_in[key, 0, 1].wait_recv()
        to_sibling(rows_of(chunk_of(a_left, b)))
        a_in[key, 1, 0].wait_recv()
        to_sibling(rows_of(chunk_of(a_right, b)))

    pass_on(0, at_b)
    b_halves[0].wait_recv()
    along_a(2, b_far, 0)
    b_halves[1].wait_recv()
    along_a(2, b_far, 1)
    to_sibling(rows_of(chunk_of(at_a, b_far)))
    settle(0, at_b)

    z_left_place = gview_hbm.at[pl.ds(pl.multiple_of(z_left * seg_part, seg_part), z_half)]
    z_right_place = gview_hbm.at[pl.ds(pl.multiple_of(z_right * seg_part + z_half, z_half), z_half)]
    z_whole[0].wait_recv()
    z_halves = [links.send(z_left_place, z_left_place, z_peer(1))]
    z_whole[1].wait_recv()
    z_halves.append(links.send(z_right_place, z_right_place, z_peer(3)))

    pass_on(3, b_left)
    pass_on(1, b_right)
    settle(3, b_left)
    settle(1, b_right)

    def far_halves(key, b):
        chunk = chunk_of(a_far, b)
        for way in range(2):
            a_halves[key][way].wait_recv()
            to_sibling(rows_of(chunk, way))

    far_halves(0, at_b)
    pass_on(2, b_far)
    far_halves(3, b_left)
    far_halves(1, b_right)
    settle(2, b_far)
    far_halves(2, b_far)
    for copy in z_halves + across:
        copy.wait_recv()
    keep.wait()
    keep_view.wait()
    links.drain(len(links.sent))


def balance(mesh, one, two, protos, pair):
    nx, ny, nz = mesh.shape["replica"], mesh.shape["batch"] // 2, mesh.shape["proto"]
    segs, width = one.shape
    count = protos.shape[0]
    both = 2 * segs
    z_half = both // nz // 2
    copies = ITERS * (nx * ny + nz + 1) + 100
    vmem, hbm = pl.BlockSpec(memory_space=pltpu.VMEM), pl.BlockSpec(memory_space=pl.ANY)
    return pl.pallas_call(
        functools.partial(balance_kernel, nx, ny, nz),
        out_shape=(
            pltpu.VMEM((both, width), F32),
            pltpu.VMEM((count, width), F32),
            pltpu.VMEM(pair.shape, jnp.int32),
        ),
        in_specs=[hbm, hbm, hbm, vmem],
        out_specs=(hbm, hbm, vmem),
        scratch_shapes=[
            pltpu.VMEM((both, width), BF16),
            pltpu.VMEM((both, count), F32),
            [pltpu.VMEM((both, count // 8), BF16)] * 8,
            pltpu.VMEM((both, width), BF16),
            pltpu.VMEM((width, both), BF16),
            pltpu.VMEM((count, width), BF16),
            pltpu.VMEM((both, 128), F32),
            pltpu.VMEM((both, 128), F32),
            pltpu.VMEM((ITERS, 8, 8, 128), F32),
            pltpu.VMEM((ITERS, 4, 8, 128), F32),
            pltpu.VMEM((ITERS, nx * ny, 4, 8, 128), F32),
            pltpu.VMEM((ITERS, 8, 8, 128), F32),
            pltpu.VMEM((ITERS, 16, 128), F32),
            pltpu.VMEM((ITERS, nz, 16, 128), F32),
            pltpu.VMEM((16, 128), F32),
            [pltpu.VMEM((4, width, 128), F32)] * 8,
            pltpu.VMEM((4, 4, width, 128), F32),
            pltpu.VMEM((128, width), BF16),
            pltpu.VMEM((128, width), F32),
        ]
        + [pltpu.VMEM((2, 2, width, 128), F32)] * 3
        + [pltpu.VMEM((2, width // 2, 128), F32)] * 3
        + [pltpu.VMEM((2, z_half, width), F32)] * 3
        + [
            pltpu.SemaphoreType.DMA((copies,)),
            pltpu.SemaphoreType.DMA((copies,)),
            pltpu.SemaphoreType.DMA((13,)),
        ],
        compiler_params=pltpu.CompilerParams(
            collective_id=0, has_side_effects=True, vmem_limit_bytes=53 << 20
        ),
        name="balance",
    )(one, two, protos, pair)


def hand_over_kernel(gview, gproto, pair_ref, one_out, two_out, proto_out, two, sems):
    segs = one_out.shape[0]
    parts = 8
    size = proto_out.shape[0] // parts
    copies = [pltpu.make_async_copy(gview.at[0:segs], one_out, sems.at[parts])]
    for i in range(parts):
        at = slice(i * size, (i + 1) * size)
        copies.append(pltpu.make_async_copy(gproto.at[at], proto_out.at[at], sems.at[i]))
    for copy in copies:
        copy.start()
    pair = jnp.broadcast_to(pair_ref[...], (segs, segs))
    number = lax.broadcasted_iota(jnp.int32, (segs, segs), 0)
    onehot = jnp.where(pair == number, 1.0, 0.0).astype(BF16)
    d = gview[segs:2 * segs, :]
    top = d.astype(BF16)
    rest = d - top.astype(F32)
    middle = rest.astype(BF16)
    end = (rest - middle.astype(F32)).astype(BF16)
    two[...] = dot(onehot, top, NN) + (dot(onehot, middle, NN) + dot(onehot, end, NN))
    copies.append(pltpu.make_async_copy(two, two_out, sems.at[parts + 1]))
    copies[-1].start()
    for copy in copies:
        copy.wait()


def hand_over(gview, gproto, pairing):
    segs, width = gview.shape[0] // 2, gview.shape[1]
    half = jax.ShapeDtypeStruct((segs, width), F32)
    vmem, hbm = pl.BlockSpec(memory_space=pltpu.VMEM), pl.BlockSpec(memory_space=pl.ANY)
    return pl.pallas_call(
        hand_over_kernel,
        out_shape=(half, half, jax.ShapeDtypeStruct(gproto.shape, F32)),
        in_specs=[vmem, hbm, vmem],
        out_specs=(hbm,) * 3,
        scratch_shapes=[
            pltpu.VMEM((segs, width), F32),
            pltpu.SemaphoreType.DMA((10,)),
        ],
        compiler_params=pltpu.CompilerParams(vmem_limit_bytes=10 << 20),
        name="hand_over",
    )(gview, gproto, pairing)


def per_device(mesh, view_one, view_two, prototypes, pairing):
    return hand_over(*balance(mesh, view_one, view_two, prototypes, pairing))


def solution(mesh):
    rows = P(("batch", "replica"), None)
    protos = P("proto", None)
    return jax.shard_map(
        functools.partial(per_device, mesh),
        mesh=mesh,
        in_specs=(rows, rows, protos, rows),
        out_specs=(rows, rows, protos),
        check_vma=False,
    )
```
